32 devices in a mesh: row: 8 (over z, core), col: 4 (over y, x).
Axes of the slice: x: 2, y: 2, z: 4, core: 2. Of those that a mesh axis runs over, the one named last changes fastest.
Arguments:
- adjoint_out: float32 [8, 4, 2, 3, 8, 1024], P('row', 'col'), may hold values from -6 to 6
- lateral: float32 [8, 4, 2, 8, 1024], P('row', 'col'), may hold values from 0.04 to 0.12
- diagonal: float32 [8, 4, 2, 8, 1024], P('row', 'col'), may hold values from 0.02 to 0.06
- vertical: float32 [8, 4, 2, 8, 1024], P('row', 'col'), may hold values from 0.1 to 10
- depth: int32 [8, 4, 2, 1024], P('row', 'col'), may hold values from 0 to 8
- tile_home: int32 [48], replicated, may hold values from 0 to 63, as said below
- edge_link: int32 [48, 4], replicated, may hold values from 0 to 383, as said below
- corner_link: int32 [48, 4], replicated, may hold values from -1 to 191, as said below
Outputs:
- adjoint_in: float32 [8, 4, 2, 3, 8, 1024], P('row', 'col')
The draws below stay inside these ranges and needn't reach their ends.
Inputs may be any that keep to these rules, and one draw needn't show every extreme that they name: tile_home[t] = 2 * d + s for the flat device index d and place s; all values are distinct, every device holds a tile at place 0, and some devices hold a second one at place 1. `edge_link`: the pairing of tile edges is symmetric: if edge e of tile t names edge f of tile u with reversal r, then edge f of tile u names edge e of tile t with the same r. The partner tile lies on a device whose row index i' has i' // 2 equal to i // 2 for the row index i of tile t's device. `corner_link`: the pairing of tile corners is symmetric; exactly 24 corners, those at cube corners, are -1; a partner tile lies on a device whose row index i' has i' // 2 equal to i // 2 for the row index i of the corner's own device.
All inputs are finite; a program needn't handle non-finite values.
Results may differ from the reference program's by a relative error of at most 0.0003.
Values sent between devices are 32-bit elements; how exact they have to be, the bound alone decides.
No kernel may reach another device: no remote copies, remote signals or barrier semaphores. Data moves between devices by JAX's collectives and lax.ppermute only.
A program may use at most 64 MiB of HBM per device.

```python
import math
import jax
import jax.numpy as jnp

TS = 32
LEV = 8
TRACERS = 3
SLOTS = 2
STEPS = 2
TILES = 48
CELLS = 1024
N_ROW = 8
N_COL = 4


def home_places(key):
    device_count = N_ROW * N_COL
    chosen = jax.random.permutation(jax.random.fold_in(key, 11), device_count).astype(jnp.int32)
    second = chosen[:TILES - device_count] * SLOTS + 1
    places = jnp.concatenate([jnp.arange(device_count, dtype=jnp.int32) * SLOTS, second])
    shuffle = jax.random.permutation(jax.random.fold_in(key, 12), TILES).astype(jnp.int32)
    return places[shuffle].astype(jnp.int32)


def band_pairing(key, salt, lone_counts):
    homes = home_places(key)
    item_count = 4 * TILES
    tile_band = homes // SLOTS // N_COL // 2
    item_band = jnp.repeat(tile_band, 4).astype(jnp.int32)
    noise = jax.random.permutation(jax.random.fold_in(key, salt), item_count).astype(jnp.int32)
    score = item_band * item_count + noise
    order = jnp.argsort(score, stable=True).astype(jnp.int32)
    sorted_band = item_band[order]
    positions = jnp.arange(item_count, dtype=jnp.int32)
    starts = jnp.searchsorted(sorted_band, sorted_band, side='left').astype(jnp.int32)
    rank = positions - starts
    lone_here = lone_counts[sorted_band]
    lonely = rank < lone_here
    relative = rank - lone_here
    leading = relative % 2 == 0
    partner_pos = jnp.where(leading, positions + 1, positions - 1)
    partner_pos = jnp.clip(jnp.where(lonely, positions, partner_pos), 0, item_count - 1)
    pair_start = jnp.where(leading, positions, positions - 1)
    pair_start = jnp.clip(jnp.where(lonely, positions, pair_start), 0, item_count - 1)
    return (order, partner_pos, lonely, pair_start)


def draw_tile_home(key, part):
    return home_places(key)


def draw_edge_link(key, part):
    item_count = 4 * TILES
    band_count = N_ROW // 2
    lone_counts = jnp.zeros((band_count,), jnp.int32)
    order, partner_pos, lonely, pair_start = band_pairing(key, 21, lone_counts)
    flip_bits = jax.random.randint(jax.random.fold_in(key, 22), (item_count,), 0, 2, dtype=jnp.int32)
    partner = jnp.zeros((item_count,), jnp.int32).at[order].set(order[partner_pos])
    reverse = jnp.zeros((item_count,), jnp.int32).at[order].set(flip_bits[pair_start])
    return (partner * 2 + reverse).reshape(TILES, 4).astype(jnp.int32)


def draw_corner_link(key, part):
    item_count = 4 * TILES
    band_count = N_ROW // 2
    band_ids = jnp.arange(band_count, dtype=jnp.int32)
    lone_counts = 2 * (12 // band_count) + 2 * (band_ids < 12 % band_count).astype(jnp.int32)
    order, partner_pos, lonely, pair_start = band_pairing(key, 31, lone_counts)
    linked = jnp.where(lonely, -1, order[partner_pos]).astype(jnp.int32)
    partner = jnp.full((item_count,), -1, jnp.int32).at[order].set(linked)
    return partner.reshape(TILES, 4).astype(jnp.int32)


def plant(array, rng, smallest, high):
    longest = array.shape.index(max(array.shape))
    spots = []
    for shift in (0, 1):
        where = [jax.random.randint(jax.random.fold_in(rng, axis), (), 0, length) for axis, length in enumerate(array.shape)]
        where[longest] = (where[longest] + shift) % array.shape[longest]
        spots.append(tuple(where))
    return array.at[spots[0]].set(smallest).at[spots[1]].set(high)


def shard_levels(rng, dims, cuts, smallest, top_value):
    loudness = 1.0
    for axis_at, shards_of in cuts:
        steps = jax.random.uniform(jax.random.fold_in(jax.random.fold_in(rng, 6), axis_at), (shards_of,), jnp.float32, smallest / len(cuts), top_value / len(cuts))
        loudness = loudness * jnp.repeat(jnp.exp(steps), dims[axis_at] // shards_of).reshape((-1,) + (1,) * (len(dims) - 1 - axis_at))
    return loudness


def gaussian(own_key, dims, deviation, bound, pieces=(), kind=jnp.bfloat16):
    loudness = shard_levels(own_key, dims, pieces, -0.22, 0.18) if pieces else 1.0
    array = jax.random.normal(own_key, dims, jnp.float32) * deviation * loudness
    return jnp.minimum(jnp.maximum(array, -bound), bound).astype(kind)


def setup_inputs(seed: int = 0) -> dict:
    keys = jax.random.split(jax.random.key(seed), 9)
    adjoint_out = gaussian(keys[0], (N_ROW, N_COL, SLOTS, TRACERS, LEV, CELLS), 1.0, 6.0, ((0, 8), (1, 4)), jnp.float32)
    lateral = jnp.clip(0.04 + 0.08 * jax.random.uniform(keys[1], (N_ROW, N_COL, SLOTS, LEV, CELLS), jnp.float32) ** shard_levels(keys[1], (N_ROW, N_COL, SLOTS, LEV, CELLS), ((0, 8), (1, 4)), -0.2, 0.2), 0.04, 0.12)
    diagonal = jnp.clip(0.02 + 0.04 * jax.random.uniform(keys[2], (N_ROW, N_COL, SLOTS, LEV, CELLS), jnp.float32) ** shard_levels(keys[2], (N_ROW, N_COL, SLOTS, LEV, CELLS), ((0, 8), (1, 4)), -0.2, 0.2), 0.02, 0.06)
    vertical = jnp.clip(jnp.exp(math.log(10.0) - 4.6051702 * jax.random.uniform(keys[3], (N_ROW, N_COL, SLOTS, LEV, CELLS), jnp.float32) ** shard_levels(keys[3], (N_ROW, N_COL, SLOTS, LEV, CELLS), ((0, 8), (1, 4)), -0.2, 0.2)), 0.1, 10.0)
    depth = plant(jax.random.randint(keys[4], (N_ROW, N_COL, SLOTS, CELLS), 0, LEV + 1), jax.random.fold_in(keys[4], 1), 0, LEV).astype(jnp.int32)
    tile_home = draw_tile_home(jax.random.fold_in(keys[8], 71), 0)
    edge_link = draw_edge_link(jax.random.fold_in(keys[8], 71), 0)
    corner_link = draw_corner_link(jax.random.fold_in(keys[8], 71), 0)
    return dict(adjoint_out=adjoint_out, lateral=lateral, diagonal=diagonal, vertical=vertical, depth=depth, tile_home=tile_home, edge_link=edge_link, corner_link=corner_link)


def vertical_solve(rhs_field, coupling):
    level_count = rhs_field.shape[2]
    couple = coupling[:, None]
    ratios = []
    partial_rhs = []
    for layer_index in range(level_count):
        below_link = couple[:, :, layer_index]
        pivot_value = 1.0 + below_link
        current = rhs_field[:, :, layer_index]
        if layer_index > 0:
            above_link = couple[:, :, layer_index - 1]
            pivot_value = pivot_value + above_link - above_link * ratios[-1]
            current = current + above_link * partial_rhs[-1]
        ratios.append(below_link / pivot_value)
        partial_rhs.append(current / pivot_value)
    solution = [partial_rhs[-1]]
    for layer_index in range(level_count - 2, -1, -1):
        solution.insert(0, partial_rhs[layer_index] + ratios[layer_index] * solution[0])
    return jnp.stack(solution, axis=2)

def edge_lines(tile_data):
    return jnp.stack([tile_data[..., 0, :], tile_data[..., :, -1], tile_data[..., -1, :], tile_data[..., :, 0]], axis=1)

def corner_cells(tile_data):
    return jnp.stack([tile_data[..., 0, 0], tile_data[..., 0, -1], tile_data[..., -1, -1], tile_data[..., -1, 0]], axis=1)

def extend(tile_data, edge_link, corner_link):
    tile_count = tile_data.shape[0]
    edge_rows = edge_lines(tile_data)
    edge_rows = edge_rows.reshape((tile_count * 4,) + edge_rows.shape[2:])
    ghosts = edge_rows[edge_link // 2]
    flipped = (edge_link % 2 == 1)[:, :, None, None, None]
    ghosts = jnp.where(flipped, ghosts[..., ::-1], ghosts)
    points = corner_cells(tile_data)
    points = points.reshape((tile_count * 4,) + points.shape[2:])
    present = (corner_link >= 0)[:, :, None, None]
    corner_ghost = jnp.where(present, points[jnp.maximum(corner_link, 0)], 0.0)
    padded = jnp.pad(tile_data, ((0, 0), (0, 0), (0, 0), (1, 1), (1, 1)))
    padded = padded.at[..., 0, 1:-1].set(ghosts[:, 0])
    padded = padded.at[..., 1:-1, -1].set(ghosts[:, 1])
    padded = padded.at[..., -1, 1:-1].set(ghosts[:, 2])
    padded = padded.at[..., 1:-1, 0].set(ghosts[:, 3])
    padded = padded.at[..., 0, 0].set(corner_ghost[:, 0])
    padded = padded.at[..., 0, -1].set(corner_ghost[:, 1])
    padded = padded.at[..., -1, -1].set(corner_ghost[:, 2])
    padded = padded.at[..., -1, 0].set(corner_ghost[:, 3])
    return padded

def forward_step(tile_data, along_coef, across_coef, coupling, wet_mask, edge_link, corner_link):
    padded = extend(tile_data, edge_link, corner_link)
    middle = padded[..., 1:-1, 1:-1]
    sides = padded[..., 2:, 1:-1] + padded[..., :-2, 1:-1] + padded[..., 1:-1, 2:] + padded[..., 1:-1, :-2]
    diagonals = padded[..., 2:, 2:] + padded[..., 2:, :-2] + padded[..., :-2, 2:] + padded[..., :-2, :-2]
    mixed = middle + along_coef * (sides - 4.0 * middle) + across_coef * (diagonals - 4.0 * middle)
    return vertical_solve(mixed, coupling) * wet_mask

def reference(adjoint_out, lateral, diagonal, vertical, depth, tile_home, edge_link, corner_link):
    places = N_ROW * N_COL * SLOTS
    seed_tiles = adjoint_out.reshape(places, TRACERS, LEV, TS, TS)[tile_home]
    along_coef = lateral.reshape(places, LEV, TS, TS)[tile_home][:, None]
    across_coef = diagonal.reshape(places, LEV, TS, TS)[tile_home][:, None]
    vertical_tiles = vertical.reshape(places, LEV, TS, TS)[tile_home]
    depth_tiles = depth.reshape(places, TS, TS)[tile_home]
    wet = (jnp.arange(LEV, dtype=jnp.int32)[None, :, None, None] < depth_tiles[:, None]).astype(jnp.float32)
    wet_next = jnp.concatenate([wet[:, 1:], jnp.zeros_like(wet[:, :1])], axis=1)
    coupling = vertical_tiles * wet * wet_next
    wet_mask = wet[:, None]

    def run_model(tracer_tiles):
        for step_index in range(STEPS):
            tracer_tiles = forward_step(tracer_tiles, along_coef, across_coef, coupling, wet_mask, edge_link, corner_link)
        return tracer_tiles
    outputs, pullback = jax.vjp(run_model, jnp.zeros_like(seed_tiles))
    gradient, = pullback(seed_tiles)
    placed = jnp.zeros((places, TRACERS, LEV, TS * TS), jnp.float32)
    placed = placed.at[tile_home].set(gradient.reshape(TILES, TRACERS, LEV, TS * TS))
    return placed.reshape(N_ROW, N_COL, SLOTS, TRACERS, LEV, TS * TS)
```

```python
import jax
import jax.numpy as jnp
from jax import lax
from jax.experimental import pallas as pl
from jax.experimental.pallas import tpu as pltpu
from jax.sharding import PartitionSpec as P

LEVELS = 8
PLACES = 2
TRACERS = 3
FIELDS = PLACES * TRACERS
BLOCKS = 8
LANES = 128
BLOCK_COUNT = 20
CORNER_BLOCK = 18
END_BLOCK = 19
VMEM_LIMIT = 4 * 2**20

CORNER_OF = (0, 1, 1, 2, 3, 2, 0, 3)
OTHER_EDGE = (3, 1, 0, 2, 3, 1, 0, 2)
OTHER_END = (0, 0, 1, 1, 1, 1, 0, 0)
CORNER_A = (0, 1, 3, 4)
CORNER_B = (6, 2, 5, 7)

LINE_AT = 0
END_AT = 12
POINT_AT = 44
OCCUPIED_AT = 68
TABLE = 72


def f32(shape):
    return jax.ShapeDtypeStruct(shape, jnp.float32)


def lane_iota():
    return lax.broadcasted_iota(jnp.int32, (LEVELS, LANES), 1)


def take(block, index):
    return jnp.take_along_axis(block, index, axis=1, mode="promise_in_bounds")


def level_rows(k):
    return pl.ds(k, BLOCKS, stride=LEVELS)


def tile_rows(j):
    return pl.ds(j * LEVELS, LEVELS)


def column_solve(rhs, inverse, ratio, couple):
    partial = []
    for k in range(LEVELS):
        current = rhs[k]
        if k > 0:
            current = current + couple[k - 1] * partial[-1]
        partial.append(current * inverse[k])
    found = [partial[-1]]
    for k in range(LEVELS - 2, -1, -1):
        found.insert(0, partial[k] + ratio[k] * found[0])
    return found


def column_factors(couple, depth=None):
    inverse, ratio = [], []
    for k in range(LEVELS):
        pivot = 1.0 + couple[k]
        if k > 0:
            pivot = pivot + couple[k - 1] - couple[k - 1] * ratio[-1]
        inv = 1.0 / pivot
        if depth is not None:
            inv = jnp.where(depth > k, inv, 0.0)
        inverse.append(inv)
        ratio.append(couple[k] * inv)
    return inverse, ratio


def beside(block, lane):
    b = lane % 32
    return jnp.where(b > 0, pltpu.roll(block, 1, 1), 0.0) + jnp.where(b < 31, pltpu.roll(block, LANES - 1, 1), 0.0)


def above_below(blocks, lane):
    up = [pltpu.roll(block, 32, 1) for block in blocks]
    down = [pltpu.roll(block, LANES - 32, 1) for block in blocks]
    zero = jnp.zeros_like(blocks[0])
    sums = []
    for j in range(BLOCKS):
        before = jnp.where(lane >= 32, up[j], up[j - 1] if j > 0 else zero)
        after = jnp.where(lane < 96, down[j], down[j + 1] if j < BLOCKS - 1 else zero)
        sums.append(before + after)
    return sums


def stencil(z, along_coef, across_coef, lane):
    along = [c * v for c, v in zip(along_coef, z)]
    across = [c * v for c, v in zip(across_coef, z)]
    along_sum = above_below(along, lane)
    across_sum = above_below(across, lane)
    sideways = [a + b for a, b in zip(along, across_sum)]
    inner = [
        z[j] - 4.0 * (along[j] + across[j]) + along_sum[j] + beside(sideways[j], lane) for j in range(BLOCKS)
    ]
    return inner, along, across, sideways


def pack_lines(columns, low, high, lane):
    residue = lane % 32
    mixed = pltpu.roll(columns[0], 1, 1)
    for j in range(1, BLOCKS):
        mixed = jnp.where(residue // 2 == j, pltpu.roll(columns[j], 2 * j + 1, 1), mixed)
    q, j = residue % 4, residue // 4
    index = jnp.where(lane < 64, 32 * ((q + 1) % 4) + 2 * j, 32 * q + 2 * j + 1)
    sides = take(mixed, index)
    segment = lane // 32
    return jnp.where(segment == 0, low, jnp.where(segment == 2, pltpu.roll(high, LANES - 32, 1), sides))


def unpack_lines(line, lane):
    residue = lane % 32
    q, j = lane // 32, residue // 2
    index = jnp.where(residue % 2 == 0, 32 + 4 * j + (q + 3) % 4, 96 + 4 * j + q) % LANES
    mixed = take(line, index)
    edge = (residue == 0) | (residue == 31)
    adds = [jnp.where(edge, pltpu.roll(mixed, LANES - 2 * j - 1, 1), 0.0) for j in range(BLOCKS)]
    adds[0] = adds[0] + jnp.where(lane < 32, line, 0.0)
    adds[-1] = adds[-1] + jnp.where(lane >= 96, pltpu.roll(line, 32, 1), 0.0)
    return adds


def pack_corners(low, high, lane):
    c = lane % 4
    return jnp.where(
        c < 2, take(low, jnp.where(c == 1, 31, 0)), take(high, jnp.where(c == 3, 96, 127))
    )


def first_kernel(x_ref, lat_ref, dia_ref, ver_ref, dep_ref, pay_ref, y_ref, fac_ref, z_ref):
    lane = lane_iota()
    level = lax.broadcasted_iota(jnp.int32, (LEVELS, LANES), 0)
    corners = jnp.zeros((LEVELS, LANES), jnp.float32)
    ends = jnp.zeros((LEVELS, LANES), jnp.float32)
    end_lane = 32 * (lane % 8 // 2) + 31 * (lane % 2)
    for p in range(PLACES):
        depth = dep_ref[pl.ds(p, BLOCKS, stride=PLACES), :]
        couple = [
            jnp.where(depth > k + 1, ver_ref[p, level_rows(k), :], 0.0) if k < LEVELS - 1 else jnp.zeros((BLOCKS, LANES), jnp.float32)
            for k in range(LEVELS)
        ]
        inverse, ratio = column_factors(couple, depth)
        for k in range(LEVELS):
            fac_ref[p, 0, k] = inverse[k]
            fac_ref[p, 1, k] = ratio[k]
            fac_ref[p, 2, k] = couple[k]
        for t in range(TRACERS):
            f = p * TRACERS + t
            found = column_solve([x_ref[f, level_rows(k), :] for k in range(LEVELS)], inverse, ratio, couple)
            for k in range(LEVELS):
                z_ref[f, level_rows(k), :] = found[k]
        lat = [lat_ref[p, tile_rows(j), :] for j in range(BLOCKS)]
        dia = [dia_ref[p, tile_rows(j), :] for j in range(BLOCKS)]
        wet_lat, wet_dia, link = [], [], []
        for j in range(BLOCKS):
            row = dep_ref[j * PLACES + p : j * PLACES + p + 1, :]
            wet_lat.append(jnp.where(row > level, lat[j], 0.0))
            wet_dia.append(jnp.where(row > level, dia[j], 0.0))
            link.append(jnp.where((row > level + 1) & (level < LEVELS - 1), ver_ref[p, tile_rows(j), :], 0.0))
        for i, blocks in enumerate((link, wet_lat, wet_dia)):
            pay_ref[12 + p * 3 + i] = pack_lines(blocks, blocks[0], blocks[-1], lane)
        link_corners = pack_corners(link[0], link[-1], lane)
        dia_corners = pack_corners(wet_dia[0], wet_dia[-1], lane)
        for t in range(TRACERS):
            f = p * TRACERS + t
            z = [z_ref[f, tile_rows(j), :] for j in range(BLOCKS)]
            inner, along, across, sideways = stencil(z, lat, dia, lane)
            for j in range(BLOCKS):
                y_ref[f, tile_rows(j), :] = inner[j]
            strips = pack_lines(
                sideways, along[0] + beside(across[0], lane), along[-1] + beside(across[-1], lane), lane
            )
            pay_ref[f] = strips
            pay_ref[FIELDS + f] = pack_lines(inner, inner[0], inner[-1], lane)
            group = lane // 32
            cells = jnp.where(
                group == 0,
                pack_corners(across[0], across[-1], lane),
                jnp.where(
                    group == 1,
                    pack_corners(inner[0], inner[-1], lane),
                    jnp.where(group == 2, link_corners, dia_corners),
                ),
            )
            corners = jnp.where(lane % 32 // 4 == p * 4 + t, cells, corners)
            ends = jnp.where(lane // 8 == p * 4 + t, take(strips, end_lane), ends)
    pay_ref[CORNER_BLOCK] = corners
    pay_ref[END_BLOCK] = ends


def pick(values, index, bits):
    packed = 0
    for i, value in enumerate(values):
        packed |= value << (bits * i)
    return lax.shift_right_logical(jnp.int32(packed), index * bits) & (2**bits - 1)


def table_kernel(home_ref, edge_ref, corner_ref, out_ref):
    row = lax.axis_index("row")
    col = lax.axis_index("col")
    col_count = lax.axis_size("col")
    device = row * col_count + col

    def scan(t, found):
        here = home_ref[t]
        return tuple(jnp.where(here == device * PLACES + p, t, found[p]) for p in range(PLACES))

    tile_count = home_ref.shape[0]
    unroll = 8 if tile_count % 8 == 0 else 1

    def scan_some(i, found):
        for s in range(unroll):
            found = scan(i * unroll + s, found)
        return found

    tiles = lax.fori_loop(0, tile_count // unroll, scan_some, tuple(jnp.int32(-1) for _ in range(PLACES)))

    def block_of(tile):
        place = home_ref[tile]
        other = lax.shift_right_logical(place, 1)
        other_row = other // col_count
        slot = jnp.where(other_row != row, col_count, 0) + ((other % col_count) ^ col)
        return slot * BLOCK_COUNT, place & 1

    def edge_of(tile, edge):
        code = edge_ref[edge, tile]
        return lax.shift_right_logical(code, 3), lax.shift_right_logical(code, 1) & 3, code & 1

    def strip_end(tile, edge_end):
        other, f, r = edge_of(tile, lax.shift_right_logical(edge_end, 1))
        base, place = block_of(other)
        return base + END_BLOCK, place * 32 + f * 2 + ((edge_end & 1) ^ r)

    def point(tile, corner):
        code = corner_ref[corner, tile]
        safe = jnp.maximum(code, 0)
        other, g = lax.shift_right_logical(safe, 2), safe & 3
        base, place = block_of(other)
        return base + CORNER_BLOCK, jnp.where(code >= 0, place * 16 + g, -1), other, g

    for p in range(PLACES):
        at = p * TABLE
        tile = jnp.maximum(tiles[p], 0)
        out_ref[at + OCCUPIED_AT] = jnp.where(tiles[p] >= 0, 1, 0)
        for e in range(4):
            other, f, r = edge_of(tile, e)
            base, place = block_of(other)
            out_ref[at + LINE_AT + 3 * e] = base + place * 3
            out_ref[at + LINE_AT + 3 * e + 1] = 32 * f + 31 * r
            out_ref[at + LINE_AT + 3 * e + 2] = 1 - 2 * r
            for end in range(2):
                index = f * 2 + (end ^ r)
                strip_row, strip_lane = strip_end(other, pick(OTHER_EDGE, index, 2) * 2 + pick(OTHER_END, index, 1))
                point_row, point_lane, _, _ = point(other, pick(CORNER_OF, index, 2))
                slot = at + END_AT + 4 * (2 * e + end)
                out_ref[slot] = strip_row
                out_ref[slot + 1] = strip_lane
                out_ref[slot + 2] = point_row
                out_ref[slot + 3] = point_lane
        for c in range(4):
            point_row, point_lane, other, g = point(tile, c)
            slot = at + POINT_AT + 6 * c
            out_ref[slot] = point_row
            out_ref[slot + 1] = point_lane
            row_a, lane_a = strip_end(other, pick(CORNER_A, g, 3))
            row_b, lane_b = strip_end(other, pick(CORNER_B, g, 3))
            out_ref[slot + 2] = row_a
            out_ref[slot + 3] = lane_a
            out_ref[slot + 4] = row_b
            out_ref[slot + 5] = lane_b


def second_kernel(tab_ref, y_ref, fac_ref, lat_ref, dia_ref, *refs):
    pay_refs = refs[:-5]
    out_ref, all_ref, z_ref, line_ref, link_ref = refs[-5:]
    lane = lane_iota()
    zero = jnp.zeros((LEVELS, LANES), jnp.float32)
    for slot, ref in enumerate(pay_refs):
        for i in range(BLOCK_COUNT):
            all_ref[slot * BLOCK_COUNT + i] = ref[i]
    segment, position = lane // 32, lane % 32
    line_end = (position == 0) | (position == 31)

    strips, lines, line_lat, line_dia = [], [], [], []
    for p in range(PLACES):
        at = p * TABLE + LINE_AT
        rows = [tab_ref[at + 3 * e] for e in range(4)]
        index = zero.astype(jnp.int32)
        for e in range(4):
            index = jnp.where(segment == e, tab_ref[at + 3 * e + 1] + tab_ref[at + 3 * e + 2] * position, index)

        def fetch(block):
            found = take(all_ref[rows[0] + block], index)
            for e in range(1, 4):
                found = jnp.where(segment == e, take(all_ref[rows[e] + block], index), found)
            return found

        for t in range(TRACERS):
            strips.append(fetch(t))
            lines.append(fetch(FIELDS + t))
        link = fetch(12)
        for t in range(TRACERS):
            link_ref[tile_rows(p * TRACERS + t), :] = link
        line_lat.append(fetch(13))
        line_dia.append(fetch(14))

    ends = zero
    tracer = lane % 32 // 8
    for p in range(PLACES):
        for i in range(8):
            at = p * TABLE + END_AT + 4 * i
            here = (segment == p) & (lane % 8 == i)
            strip = take(all_ref[tab_ref[at]], tab_ref[at + 1] + tracer * 8)
            point_lane = tab_ref[at + 3]
            point = take(all_ref[tab_ref[at + 2]], jnp.maximum(point_lane, 0) + tracer * 4)
            ends = jnp.where(here, strip + jnp.where(point_lane >= 0, point, 0.0), ends)

    cells = zero
    cell_adds = zero
    cell_tracer = lane % 16 // 4
    for p in range(PLACES):
        for c in range(4):
            at = p * TABLE + POINT_AT + 6 * c
            here = (position // 16 == p) & (lane % 4 == c)
            point_lane = tab_ref[at + 1]
            cell = take(all_ref[tab_ref[at]], jnp.maximum(point_lane, 0) + 32 * segment + 4 * cell_tracer)
            cells = jnp.where(here & (point_lane >= 0), cell, cells)
            strip_a = take(all_ref[tab_ref[at + 2]], tab_ref[at + 3] + cell_tracer * 8)
            strip_b = take(all_ref[tab_ref[at + 4]], tab_ref[at + 5] + cell_tracer * 8)
            cell_adds = jnp.where(here, strip_a + strip_b, cell_adds)
    cell_adds = cell_adds + pltpu.roll(all_ref[CORNER_BLOCK], 32, 1)

    for f in range(FIELDS):
        spread = take(ends, f // TRACERS * 32 + f % TRACERS * 8 + segment * 2 + jnp.where(position == 31, 1, 0))
        line_ref[tile_rows(f), :] = lines[f] + all_ref[f] + jnp.where(line_end, spread, 0.0)
    line_ref[tile_rows(FIELDS), :] = cells + cell_adds
    line_ref[tile_rows(FIELDS + 1), :] = zero
    link_ref[tile_rows(FIELDS), :] = pltpu.roll(cells, LANES - 32, 1)
    link_ref[tile_rows(FIELDS + 1), :] = zero
    couple = [link_ref[level_rows(k), :] for k in range(LEVELS)]
    couple[-1] = zero
    inverse, ratio = column_factors(couple)
    found = column_solve([line_ref[level_rows(k), :] for k in range(LEVELS)], inverse, ratio, couple)
    for k in range(LEVELS):
        line_ref[level_rows(k), :] = found[k]
    points = line_ref[tile_rows(FIELDS), :] * pltpu.roll(cells, LANES - 64, 1)

    corner_of_lane = jnp.where(segment == 0, jnp.where(position == 31, 1, 0), jnp.where(position == 31, 2, 3))
    at_corner = line_end & (segment % 2 == 0)
    for p in range(PLACES):
        occupied = tab_ref[p * TABLE + OCCUPIED_AT] > 0
        inverse = [fac_ref[p, 0, k] for k in range(LEVELS)]
        ratio = [fac_ref[p, 1, k] for k in range(LEVELS)]
        couple = [fac_ref[p, 2, k] for k in range(LEVELS)]
        lat = [lat_ref[p, tile_rows(j), :] for j in range(BLOCKS)]
        dia = [dia_ref[p, tile_rows(j), :] for j in range(BLOCKS)]
        for t in range(TRACERS):
            f = p * TRACERS + t
            corner_index = p * 16 + t * 4 + corner_of_lane
            ghosts = strips[f] + jnp.where(at_corner, take(cells, corner_index), 0.0)
            adds = unpack_lines(ghosts, lane)
            for j in range(BLOCKS):
                z_ref[f, tile_rows(j), :] = y_ref[f, tile_rows(j), :] + adds[j]
            found = column_solve([z_ref[f, level_rows(k), :] for k in range(LEVELS)], inverse, ratio, couple)
            for k in range(LEVELS):
                z_ref[f, level_rows(k), :] = found[k]
            z = [z_ref[f, tile_rows(j), :] for j in range(BLOCKS)]
            inner, _, _, _ = stencil(z, lat, dia, lane)
            line = line_ref[tile_rows(f), :]
            ghosts = line_lat[p] * line + beside(line_dia[p] * line, lane)
            ghosts = ghosts + jnp.where(at_corner, take(points, 32 + corner_index), 0.0)
            adds = unpack_lines(ghosts, lane)
            for j in range(BLOCKS):
                out_ref[f, tile_rows(j), :] = jnp.where(occupied, inner[j] + adds[j], 0.0)


def swap(value, axes, row_count, col_count, row_bit, col_bits):
    pairs = []
    for i in range(row_count):
        for j in range(col_count):
            pairs.append((i * col_count + j, (i ^ row_bit) * col_count + (j ^ col_bits)))
    return lax.ppermute(value, axes, pairs)


def tiled(array, lead):
    blocks = array.reshape(lead + (-1, BLOCKS, LANES))
    rows = blocks.shape[-3]
    order = tuple(range(len(lead))) + (len(lead) + 1, len(lead), len(lead) + 2)
    return blocks.transpose(order).reshape(lead + (BLOCKS * rows, LANES))


def on_device(adjoint_out, lateral, diagonal, vertical, depth, tile_home, edge_link, corner_link):
    row_count, col_count = lax.axis_size("row"), lax.axis_size("col")
    axes = ("row", "col")
    vmem = pl.BlockSpec(memory_space=pltpu.VMEM)
    smem = pl.BlockSpec(memory_space=pltpu.SMEM)
    params = pltpu.CompilerParams(vmem_limit_bytes=VMEM_LIMIT)
    rows = BLOCKS * LEVELS
    x = tiled(adjoint_out, (FIELDS,))
    lat = tiled(lateral, (PLACES,))
    dia = tiled(diagonal, (PLACES,))
    ver = tiled(vertical, (PLACES,))
    dep = tiled(depth, ())
    payload, y, fac = pl.pallas_call(
        first_kernel,
        out_shape=(
            f32((BLOCK_COUNT, LEVELS, LANES)),
            f32((FIELDS, rows, LANES)),
            f32((PLACES, 3, LEVELS, BLOCKS, LANES)),
        ),
        in_specs=[vmem] * 5,
        out_specs=(vmem, vmem, vmem),
        scratch_shapes=[pltpu.VMEM((FIELDS, rows, LANES), jnp.float32)],
        compiler_params=params,
        name="first",
    )(x, lat, dia, ver, dep)
    table = pl.pallas_call(
        table_kernel,
        out_shape=jax.ShapeDtypeStruct((PLACES * TABLE,), jnp.int32),
        in_specs=[smem] * 3,
        out_specs=smem,
        compiler_params=params,
        name="table",
    )(tile_home, edge_link.T, corner_link.T)
    near = [swap(payload, axes, row_count, col_count, 0, m) for m in range(1, col_count)]
    twin = swap(payload, axes, row_count, col_count, 1, 0)
    far = [swap(value, axes, row_count, col_count, 1, 0) for value in near]
    payloads = [payload] + near + [twin] + far
    out = pl.pallas_call(
        second_kernel,
        out_shape=f32((FIELDS, rows, LANES)),
        in_specs=[smem] + [vmem] * (4 + len(payloads)),
        out_specs=vmem,
        scratch_shapes=[
            pltpu.VMEM((len(payloads) * BLOCK_COUNT, LEVELS, LANES), jnp.float32),
            pltpu.VMEM((FIELDS, rows, LANES), jnp.float32),
            pltpu.VMEM((rows, LANES), jnp.float32),
            pltpu.VMEM((rows, LANES), jnp.float32),
        ],
        compiler_params=pltpu.CompilerParams(vmem_limit_bytes=VMEM_LIMIT + 2 * len(payloads) * BLOCK_COUNT * 4096),
        name="second",
    )(table, y, fac, lat, dia, *payloads)
    out = out.reshape(FIELDS, BLOCKS, LEVELS, LANES).transpose(0, 2, 1, 3)
    return out.reshape(adjoint_out.shape)


def solution(mesh):
    return jax.shard_map(
        on_device,
        mesh=mesh,
        in_specs=(
            P("row", "col", None, None, None, None),
            P("row", "col", None, None, None),
            P("row", "col", None, None, None),
            P("row", "col", None, None, None),
            P("row", "col", None, None),
            P(),
            P(),
            P(),
        ),
        out_specs=P("row", "col", None, None, None, None),
        check_vma=False,
    )
```

```python
import jax
import jax.numpy as jnp
from jax import lax
from jax.experimental import pallas as pl
from jax.experimental.pallas import tpu as pltpu
from jax.sharding import PartitionSpec as P

LEVELS = 8
PLACES = 2
TRACERS = 3
FIELDS = PLACES * TRACERS
BLOCKS = 8
LANES = 128
BLOCK_COUNT = 20
CORNER_BLOCK = 18
END_BLOCK = 19
VMEM_LIMIT = 4 * 2**20

CORNER_OF = (0, 1, 1, 2, 3, 2, 0, 3)
OTHER_EDGE = (3, 1, 0, 2, 3, 1, 0, 2)
OTHER_END = (0, 0, 1, 1, 1, 1, 0, 0)
CORNER_A = (0, 1, 3, 4)
CORNER_B = (6, 2, 5, 7)

LINE_AT = 0
END_AT = 12
POINT_AT = 44
OCCUPIED_AT = 68
TABLE = 72


def f32(shape):
    return jax.ShapeDtypeStruct(shape, jnp.float32)


def lane_iota():
    return lax.broadcasted_iota(jnp.int32, (LEVELS, LANES), 1)


def take(block, index):
    return jnp.take_along_axis(block, index, axis=1, mode="promise_in_bounds")


def level_rows(k):
    return pl.ds(k, BLOCKS, stride=LEVELS)


def tile_rows(j):
    return pl.ds(j * LEVELS, LEVELS)


def column_solve(rhs, inverse, ratio, couple):
    partial = [[] for _ in rhs]
    for k in range(LEVELS):
        for values, done in zip(rhs, partial):
            current = values[k]
            if k > 0:
                current = current + couple[k - 1] * done[-1]
            done.append(current * inverse[k])
    found = [[done[-1]] for done in partial]
    for k in range(LEVELS - 2, -1, -1):
        for done, values in zip(partial, found):
            values.insert(0, done[k] + ratio[k] * values[0])
    return found


def column_factors(couples, depths):
    factors = [([], []) for _ in couples]
    for k in range(LEVELS):
        for couple, depth, (inverse, ratio) in zip(couples, depths, factors):
            pivot = 1.0 + couple[k]
            if k > 0:
                pivot = pivot + couple[k - 1] - couple[k - 1] * ratio[-1]
            inv = 1.0 / pivot
            if depth is not None:
                inv = jnp.where(depth > k, inv, 0.0)
            inverse.append(inv)
            ratio.append(couple[k] * inv)
    return factors


def beside(block, lane):
    b = lane % 32
    return jnp.where(b > 0, pltpu.roll(block, 1, 1), 0.0) + jnp.where(b < 31, pltpu.roll(block, LANES - 1, 1), 0.0)


def above_below(blocks, lane):
    up = [pltpu.roll(block, 32, 1) for block in blocks]
    down = [pltpu.roll(block, LANES - 32, 1) for block in blocks]
    zero = jnp.zeros_like(blocks[0])
    sums = []
    for j in range(BLOCKS):
        before = jnp.where(lane >= 32, up[j], up[j - 1] if j > 0 else zero)
        after = jnp.where(lane < 96, down[j], down[j + 1] if j < BLOCKS - 1 else zero)
        sums.append(before + after)
    return sums


def stencil(z, along_coef, across_coef, lane):
    along = [c * v for c, v in zip(along_coef, z)]
    across = [c * v for c, v in zip(across_coef, z)]
    along_sum = above_below(along, lane)
    across_sum = above_below(across, lane)
    sideways = [a + b for a, b in zip(along, across_sum)]
    inner = [
        z[j] - 4.0 * (along[j] + across[j]) + along_sum[j] + beside(sideways[j], lane) for j in range(BLOCKS)
    ]
    return inner, along, across, sideways


def pack_lines(columns, low, high, lane):
    residue = lane % 32
    mixed = pltpu.roll(columns[0], 1, 1)
    for j in range(1, BLOCKS):
        mixed = jnp.where(residue // 2 == j, pltpu.roll(columns[j], 2 * j + 1, 1), mixed)
    q, j = residue % 4, residue // 4
    index = jnp.where(lane < 64, 32 * ((q + 1) % 4) + 2 * j, 32 * q + 2 * j + 1)
    sides = take(mixed, index)
    segment = lane // 32
    return jnp.where(segment == 0, low, jnp.where(segment == 2, pltpu.roll(high, LANES - 32, 1), sides))


def unpack_lines(outer, inner, lane):
    residue = lane % 32
    j, part, q = residue // 4, residue % 4, lane // 32
    index = jnp.where(part < 2, 32 + 4 * j + (q + 3) % 4, 96 + 4 * j + q)
    mixed = jnp.where((part == 0) | (part == 3), take(inner, index), take(outer, index))
    near = (residue < 2) | (residue >= 30)
    adds = [jnp.where(near, pltpu.roll(mixed, (LANES - 4 * j - 2) % LANES, 1), 0.0) for j in range(BLOCKS)]
    segment = lane // 32
    low = jnp.where(segment == 0, outer, jnp.where(segment == 1, pltpu.roll(inner, 32, 1), 0.0))
    high = jnp.where(segment == 3, pltpu.roll(outer, 32, 1), jnp.where(segment == 2, inner, 0.0))
    adds[0] = adds[0] + low
    adds[-1] = adds[-1] + high
    return adds


def pack_corners(low, high, lane):
    c = lane % 4
    return jnp.where(
        c < 2, take(low, jnp.where(c == 1, 31, 0)), take(high, jnp.where(c == 3, 96, 127))
    )


def first_kernel(
    *refs,
):
    sources, refs = refs[:8], refs[8:]
    pay_ref, y_ref, fac_ref, dep_ref, lat_ref, dia_ref, home_ref, edge_ref, corner_ref, ver_ref, x_ref, z_ref, sems = refs
    targets = (dep_ref, ver_ref, x_ref, lat_ref, dia_ref, home_ref, edge_ref, corner_ref)
    moves = [pltpu.make_async_copy(source, target, sems.at[i]) for i, (source, target) in enumerate(zip(sources, targets))]
    for move in moves:
        move.start()
    lane = lane_iota()
    level = lax.broadcasted_iota(jnp.int32, (LEVELS, LANES), 0)
    group = lane // 32
    corners = jnp.zeros((LEVELS, LANES), jnp.float32)
    ends = jnp.zeros((LEVELS, LANES), jnp.float32)
    end_lane = 32 * (lane % 8 // 2) + 31 * (lane % 2)
    moves[0].wait()
    moves[1].wait()
    depth = [dep_ref[pl.ds(p, BLOCKS, stride=PLACES), :] for p in range(PLACES)]
    couple = [
        [jnp.where(depth[p] > k + 1, ver_ref[p, level_rows(k), :], 0.0) for k in range(LEVELS - 1)]
        + [jnp.zeros((BLOCKS, LANES), jnp.float32)]
        for p in range(PLACES)
    ]
    factors = column_factors(couple, depth)
    for p in range(PLACES):
        for k in range(LEVELS):
            fac_ref[p, 0, k] = factors[p][0][k]
            fac_ref[p, 1, k] = factors[p][1][k]
            fac_ref[p, 2, k] = couple[p][k]
    moves[2].wait()
    for p in range(PLACES):
        fields = [p * TRACERS + t for t in range(TRACERS)]
        found = column_solve(
            [[x_ref[f, level_rows(k), :] for k in range(LEVELS)] for f in fields], *factors[p], couple[p]
        )
        for k in range(LEVELS):
            for f, values in zip(fields, found):
                z_ref[f, level_rows(k), :] = values[k]
    moves[3].wait()
    moves[4].wait()
    for p in range(PLACES):
        lat = [lat_ref[p, tile_rows(j), :] for j in range(BLOCKS)]
        dia = [dia_ref[p, tile_rows(j), :] for j in range(BLOCKS)]
        wet_lat, wet_dia, link = [], [], []
        for j in range(BLOCKS):
            row = dep_ref[j * PLACES + p : j * PLACES + p + 1, :]
            wet_lat.append(jnp.where(row > level, lat[j], 0.0))
            wet_dia.append(jnp.where(row > level, dia[j], 0.0))
            link.append(jnp.where((row > level + 1) & (level < LEVELS - 1), ver_ref[p, tile_rows(j), :], 0.0))
        for i, blocks in enumerate((link, wet_lat, wet_dia)):
            pay_ref[12 + p * 3 + i] = pack_lines(blocks, blocks[0], blocks[-1], lane)
        link_corners = pack_corners(link[0], link[-1], lane)
        dia_corners = pack_corners(wet_dia[0], wet_dia[-1], lane)
        for t in range(TRACERS):
            f = p * TRACERS + t
            z = [z_ref[f, tile_rows(j), :] for j in range(BLOCKS)]
            inner, along, across, sideways = stencil(z, lat, dia, lane)
            for j in range(BLOCKS):
                y_ref[f, tile_rows(j), :] = inner[j]
            strips = pack_lines(
                sideways, along[0] + beside(across[0], lane), along[-1] + beside(across[-1], lane), lane
            )
            pay_ref[f] = strips
            pay_ref[FIELDS + f] = pack_lines(inner, inner[0], inner[-1], lane)
            cells = jnp.where(
                group == 0,
                pack_corners(across[0], across[-1], lane),
                jnp.where(
                    group == 1,
                    pack_corners(inner[0], inner[-1], lane),
                    jnp.where(group == 2, link_corners, dia_corners),
                ),
            )
            corners = jnp.where(lane % 32 // 4 == p * 4 + t, cells, corners)
            ends = jnp.where(lane // 8 == p * 4 + t, take(strips, end_lane), ends)
    pay_ref[CORNER_BLOCK] = corners
    pay_ref[END_BLOCK] = ends
    for move in moves[5:]:
        move.wait()


def pick(values, index, bits):
    packed = 0
    for i, value in enumerate(values):
        packed |= value << (bits * i)
    return lax.shift_right_logical(jnp.int32(packed), index * bits) & (2**bits - 1)


def window_kernel(
    home_ref, edge_ref, corner_ref, y_ref, fac_ref, lat_ref, dia_ref, dep_ref, pay_ref, out_ref, part_ref, own_ref, z_ref, link_ref
):
    row = lax.axis_index("row")
    col = lax.axis_index("col")
    col_count = lax.axis_size("col")
    device = row * col_count + col

    def scan(t, found):
        here = home_ref[0, t]
        return tuple(jnp.where(here == device * PLACES + p, t, found[p]) for p in range(PLACES))

    tile_count = home_ref.shape[1]
    unroll = 8 if tile_count % 8 == 0 else 1

    def scan_some(i, found):
        for s in range(unroll):
            found = scan(i * unroll + s, found)
        return found

    tiles = lax.fori_loop(0, tile_count // unroll, scan_some, tuple(jnp.int32(-1) for _ in range(PLACES)))

    def block_of(tile):
        place = home_ref[0, tile]
        other = lax.shift_right_logical(place, 1)
        slot = (other ^ device) & (2 * col_count - 1)
        return slot * BLOCK_COUNT, place & 1

    def edge_of(tile, edge):
        code = edge_ref[edge, tile]
        return lax.shift_right_logical(code, 3), lax.shift_right_logical(code, 1) & 3, code & 1

    def strip_end(tile, edge_end):
        other, f, r = edge_of(tile, lax.shift_right_logical(edge_end, 1))
        base, place = block_of(other)
        return base + END_BLOCK, place * 32 + f * 2 + ((edge_end & 1) ^ r)

    def point(tile, corner):
        code = corner_ref[corner, tile]
        safe = jnp.maximum(code, 0)
        other, g = lax.shift_right_logical(safe, 2), safe & 3
        base, place = block_of(other)
        return base + CORNER_BLOCK, jnp.where(code >= 0, place * 16 + g, -1), other, g

    for p in range(PLACES):
        at = p * TABLE
        tile = jnp.maximum(tiles[p], 0)
        out_ref[at + OCCUPIED_AT] = jnp.where(tiles[p] >= 0, 1, 0)
        for e in range(4):
            other, f, r = edge_of(tile, e)
            base, place = block_of(other)
            out_ref[at + LINE_AT + 3 * e] = base + place * 3
            out_ref[at + LINE_AT + 3 * e + 1] = 32 * f + 31 * r
            out_ref[at + LINE_AT + 3 * e + 2] = 1 - 2 * r
            for end in range(2):
                index = f * 2 + (end ^ r)
                strip_row, strip_lane = strip_end(other, pick(OTHER_EDGE, index, 2) * 2 + pick(OTHER_END, index, 1))
                point_row, point_lane, _, _ = point(other, pick(CORNER_OF, index, 2))
                slot = at + END_AT + 4 * (2 * e + end)
                out_ref[slot] = strip_row
                out_ref[slot + 1] = strip_lane
                out_ref[slot + 2] = point_row
                out_ref[slot + 3] = point_lane
        for c in range(4):
            point_row, point_lane, other, g = point(tile, c)
            slot = at + POINT_AT + 6 * c
            out_ref[slot] = point_row
            out_ref[slot + 1] = point_lane
            row_a, lane_a = strip_end(other, pick(CORNER_A, g, 3))
            row_b, lane_b = strip_end(other, pick(CORNER_B, g, 3))
            out_ref[slot + 2] = row_a
            out_ref[slot + 3] = lane_a
            out_ref[slot + 4] = row_b
            out_ref[slot + 5] = lane_b

    lane = lane_iota()
    level = lax.broadcasted_iota(jnp.int32, (LEVELS, LANES), 0)
    for p in range(PLACES):
        fields = [p * TRACERS + t for t in range(TRACERS)]
        inverse = [fac_ref[p, 0, k] for k in range(LEVELS)]
        ratio = [fac_ref[p, 1, k] for k in range(LEVELS)]
        couple = [fac_ref[p, 2, k] for k in range(LEVELS)]
        found = column_solve(
            [[y_ref[f, level_rows(k), :] for k in range(LEVELS)] for f in fields], inverse, ratio, couple
        )
        for k in range(LEVELS):
            for f, values in zip(fields, found):
                z_ref[f, level_rows(k), :] = values[k]
    for p in range(PLACES):
        lat = [lat_ref[p, tile_rows(j), :] for j in range(BLOCKS)]
        dia = [dia_ref[p, tile_rows(j), :] for j in range(BLOCKS)]
        for t in range(TRACERS):
            f = p * TRACERS + t
            inner, _, _, _ = stencil([z_ref[f, tile_rows(j), :] for j in range(BLOCKS)], lat, dia, lane)
            for j in range(BLOCKS):
                part_ref[f, tile_rows(j), :] = jnp.where(tiles[p] >= 0, inner[j], 0.0)

    wet = []
    for p in range(PLACES):
        rows = [dep_ref[j * PLACES + p : j * PLACES + p + 1, :] for j in range(BLOCKS)]
        masks = [jnp.where(row > level, 1.0, 0.0) for row in rows]
        wet.append(pack_lines(masks, masks[0], masks[-1], lane))
    for f in range(LEVELS):
        link_ref[0, tile_rows(f), :] = pay_ref[12 + f // TRACERS % PLACES * 3]
        link_ref[1, tile_rows(f), :] = wet[f // TRACERS % PLACES]
    couple = [link_ref[0, level_rows(k), :] for k in range(LEVELS)]
    ((inverse, ratio),) = column_factors([couple], [None])
    for k in range(LEVELS):
        mask = link_ref[1, level_rows(k), :]
        own_ref[0, k] = inverse[k] * mask
        own_ref[1, k] = ratio[k]
        own_ref[2, k] = couple[k]


def second_kernel(tab_ref, part_ref, own_ref, *refs):
    pay_refs = refs[:-5]
    out_ref, all_ref, own_line_ref, line_ref, link_ref = refs[-5:]
    lane = lane_iota()
    zero = jnp.zeros((LEVELS, LANES), jnp.float32)
    for slot, ref in enumerate(pay_refs):
        for i in range(BLOCK_COUNT):
            all_ref[slot * BLOCK_COUNT + i] = ref[i]
    segment, position = lane // 32, lane % 32
    line_end = (position == 0) | (position == 31)

    strips, lines, line_lat, line_dia = [], [], [], []
    for p in range(PLACES):
        at = p * TABLE + LINE_AT
        rows = [tab_ref[at + 3 * e] for e in range(4)]
        places = [tab_ref[at + 3 * e + 1] for e in range(4)]
        signs = [tab_ref[at + 3 * e + 2] for e in range(4)]
        index = zero.astype(jnp.int32)
        for e in range(4):
            index = jnp.where(segment == e, places[e] + signs[e] * position, index)

        def fetch(block):
            found = take(all_ref[rows[0] + block], index)
            for e in range(1, 4):
                found = jnp.where(segment == e, take(all_ref[rows[e] + block], index), found)
            return found

        for t in range(TRACERS):
            strips.append(fetch(t))
            lines.append(fetch(FIELDS + t))
        link = fetch(12)
        for t in range(TRACERS):
            link_ref[tile_rows(p * TRACERS + t), :] = link
        line_lat.append(fetch(13))
        line_dia.append(fetch(14))

    ends = zero
    tracer = lane % 32 // 8
    for p in range(PLACES):
        for i in range(8):
            at = p * TABLE + END_AT + 4 * i
            here = (segment == p) & (lane % 8 == i)
            strip = take(all_ref[tab_ref[at]], tab_ref[at + 1] + tracer * 8)
            point_lane = tab_ref[at + 3]
            point = take(all_ref[tab_ref[at + 2]], jnp.maximum(point_lane, 0) + tracer * 4)
            ends = jnp.where(here, strip + jnp.where(point_lane >= 0, point, 0.0), ends)

    cells = zero
    cell_adds = zero
    cell_tracer = lane % 16 // 4
    for p in range(PLACES):
        for c in range(4):
            at = p * TABLE + POINT_AT + 6 * c
            here = (position // 16 == p) & (lane % 4 == c)
            point_lane = tab_ref[at + 1]
            cell = take(all_ref[tab_ref[at]], jnp.maximum(point_lane, 0) + 32 * segment + 4 * cell_tracer)
            cells = jnp.where(here & (point_lane >= 0), cell, cells)
            strip_a = take(all_ref[tab_ref[at + 2]], tab_ref[at + 3] + cell_tracer * 8)
            strip_b = take(all_ref[tab_ref[at + 4]], tab_ref[at + 5] + cell_tracer * 8)
            cell_adds = jnp.where(here, strip_a + strip_b, cell_adds)
    cell_adds = cell_adds + pltpu.roll(all_ref[CORNER_BLOCK], 32, 1)

    corner_of_lane = jnp.where(segment == 0, jnp.where(position == 31, 1, 0), jnp.where(position == 31, 2, 3))
    at_corner = line_end & (segment % 2 == 0)
    for f in range(FIELDS):
        p, t = f // TRACERS, f % TRACERS
        spread = take(ends, p * 32 + t * 8 + segment * 2 + jnp.where(position == 31, 1, 0))
        line_ref[tile_rows(f), :] = lines[f] + all_ref[f] + jnp.where(line_end, spread, 0.0)
        points = take(cells, p * 16 + t * 4 + corner_of_lane)
        own_line_ref[tile_rows(f), :] = strips[f] + jnp.where(at_corner, points, 0.0)
    line_ref[tile_rows(FIELDS), :] = cells + cell_adds
    line_ref[tile_rows(FIELDS + 1), :] = zero
    own_line_ref[tile_rows(FIELDS), :] = zero
    own_line_ref[tile_rows(FIELDS + 1), :] = zero
    link_ref[tile_rows(FIELDS), :] = pltpu.roll(cells, LANES - 32, 1)
    link_ref[tile_rows(FIELDS + 1), :] = zero
    couple = [link_ref[level_rows(k), :] for k in range(LEVELS - 1)] + [zero]
    ((inverse, ratio),) = column_factors([couple], [None])
    (own_found,) = column_solve(
        [[own_line_ref[level_rows(k), :] for k in range(LEVELS)]],
        [own_ref[0, k] for k in range(LEVELS)],
        [own_ref[1, k] for k in range(LEVELS)],
        [own_ref[2, k] for k in range(LEVELS)],
    )
    (found,) = column_solve([[line_ref[level_rows(k), :] for k in range(LEVELS)]], inverse, ratio, couple)
    for k in range(LEVELS):
        own_line_ref[level_rows(k), :] = own_found[k]
        line_ref[level_rows(k), :] = found[k]
    points = line_ref[tile_rows(FIELDS), :] * pltpu.roll(cells, LANES - 64, 1)

    for p in range(PLACES):
        occupied = tab_ref[p * TABLE + OCCUPIED_AT] > 0
        own_lat, own_dia = all_ref[13 + 3 * p], all_ref[14 + 3 * p]
        for t in range(TRACERS):
            f = p * TRACERS + t
            line = line_ref[tile_rows(f), :]
            outer = line_lat[p] * line + beside(line_dia[p] * line, lane)
            outer = outer + jnp.where(at_corner, take(points, 32 + p * 16 + t * 4 + corner_of_lane), 0.0)
            line = own_line_ref[tile_rows(f), :]
            along, across = own_lat * line, own_dia * line
            outer = outer + line - 4.0 * (along + across) + beside(along, lane)
            inner = along + beside(across, lane)
            adds = unpack_lines(jnp.where(occupied, outer, 0.0), jnp.where(occupied, inner, 0.0), lane)
            for j in range(BLOCKS):
                out_ref[f, tile_rows(j), :] = part_ref[f, tile_rows(j), :] + adds[j]


def swap(value, axes, row_count, col_count, row_bit, col_bits):
    pairs = []
    for i in range(row_count):
        for j in range(col_count):
            pairs.append((i * col_count + j, (i ^ row_bit) * col_count + (j ^ col_bits)))
    return lax.ppermute(value, axes, pairs)


def tiled(array, lead):
    blocks = array.reshape(lead + (-1, BLOCKS, LANES))
    rows = blocks.shape[-3]
    order = tuple(range(len(lead))) + (len(lead) + 1, len(lead), len(lead) + 2)
    return blocks.transpose(order).reshape(lead + (BLOCKS * rows, LANES))


def on_device(adjoint_out, lateral, diagonal, vertical, depth, tile_home, edge_link, corner_link):
    row_count, col_count = lax.axis_size("row"), lax.axis_size("col")
    axes = ("row", "col")
    vmem = pl.BlockSpec(memory_space=pltpu.VMEM)
    smem = pl.BlockSpec(memory_space=pltpu.SMEM)
    params = pltpu.CompilerParams(vmem_limit_bytes=VMEM_LIMIT)
    rows = BLOCKS * LEVELS
    x = tiled(adjoint_out, (FIELDS,))
    lat = tiled(lateral, (PLACES,))
    dia = tiled(diagonal, (PLACES,))
    ver = tiled(vertical, (PLACES,))
    dep = tiled(depth, ())
    hbm = pl.BlockSpec(memory_space=pltpu.HBM)
    home, edges, corners = tile_home.reshape(1, -1), edge_link.T, corner_link.T
    sources = (dep, ver, x, lat, dia, home, edges, corners)
    payload, y, fac, dep, lat, dia, home, edges, corners = pl.pallas_call(
        first_kernel,
        out_shape=(
            f32((BLOCK_COUNT, LEVELS, LANES)),
            f32((FIELDS, rows, LANES)),
            f32((PLACES, 3, LEVELS, BLOCKS, LANES)),
        )
        + tuple(jax.ShapeDtypeStruct(value.shape, value.dtype) for value in (dep, lat, dia, home, edges, corners)),
        in_specs=[hbm] * len(sources),
        out_specs=(vmem,) * 9,
        scratch_shapes=[
            pltpu.VMEM((PLACES, rows, LANES), jnp.float32),
            pltpu.VMEM((FIELDS, rows, LANES), jnp.float32),
            pltpu.VMEM((FIELDS, rows, LANES), jnp.float32),
            pltpu.SemaphoreType.DMA((len(sources),)),
        ],
        compiler_params=params,
        name="first",
    )(*(pltpu.with_memory_space_constraint(value, pltpu.HBM) for value in sources))
    near = [swap(payload, axes, row_count, col_count, 0, m) for m in range(1, col_count)]
    table, part, own = pl.pallas_call(
        window_kernel,
        out_shape=(
            jax.ShapeDtypeStruct((PLACES * TABLE,), jnp.int32),
            f32((FIELDS, rows, LANES)),
            f32((3, LEVELS, LEVELS, LANES)),
        ),
        in_specs=[smem] * 3 + [vmem] * 6,
        out_specs=(smem, vmem, vmem),
        scratch_shapes=[
            pltpu.VMEM((FIELDS, rows, LANES), jnp.float32),
            pltpu.VMEM((2, rows, LANES), jnp.float32),
        ],
        compiler_params=params,
        name="window",
    )(home, edges, corners, y, fac, lat, dia, dep, payload)
    *near, table = lax.optimization_barrier((*near, table))
    twin = swap(payload, axes, row_count, col_count, 1, 0)
    far = [swap(value, axes, row_count, col_count, 1, 0) for value in near]
    payloads = [payload] + near + [twin] + far
    out = pl.pallas_call(
        second_kernel,
        out_shape=f32((FIELDS, rows, LANES)),
        in_specs=[smem] + [vmem] * (2 + len(payloads)),
        out_specs=vmem,
        scratch_shapes=[
            pltpu.VMEM((len(payloads) * BLOCK_COUNT, LEVELS, LANES), jnp.float32),
            pltpu.VMEM((rows, LANES), jnp.float32),
            pltpu.VMEM((rows, LANES), jnp.float32),
            pltpu.VMEM((rows, LANES), jnp.float32),
        ],
        compiler_params=pltpu.CompilerParams(vmem_limit_bytes=VMEM_LIMIT + 2 * len(payloads) * BLOCK_COUNT * 4096),
        name="second",
    )(table, part, own, *payloads)
    out = out.reshape(FIELDS, BLOCKS, LEVELS, LANES).transpose(0, 2, 1, 3)
    return out.reshape(adjoint_out.shape)


def solution(mesh):
    return jax.shard_map(
        on_device,
        mesh=mesh,
        in_specs=(
            P("row", "col", None, None, None, None),
            P("row", "col", None, None, None),
            P("row", "col", None, None, None),
            P("row", "col", None, None, None),
            P("row", "col", None, None),
            P(),
            P(),
            P(),
        ),
        out_specs=P("row", "col", None, None, None, None),
        check_vma=False,
    )
```

```python
import jax
import jax.numpy as jnp
import numpy as np
from jax import lax
from jax.experimental import pallas as pl
from jax.experimental.pallas import tpu as pltpu
from jax.sharding import PartitionSpec as P

LEVELS = 8
PLACES = 2
TRACERS = 3
FIELDS = PLACES * TRACERS
BLOCKS = 8
LANES = 128
BLOCK_COUNT = 20
CORNER_BLOCK = 18
END_BLOCK = 19
VMEM_LIMIT = 8 * 2**20

CORNER_OF = (0, 1, 1, 2, 3, 2, 0, 3)
OTHER_EDGE = (3, 1, 0, 2, 3, 1, 0, 2)
OTHER_END = (0, 0, 1, 1, 1, 1, 0, 0)
CORNER_A = (0, 1, 3, 4)
CORNER_B = (6, 2, 5, 7)

LINE_AT = 0
END_AT = 12
POINT_AT = 44
OCCUPIED_AT = 68
TABLE = 72


def f32(shape):
    return jax.ShapeDtypeStruct(shape, jnp.float32)


def lane_iota():
    return lax.broadcasted_iota(jnp.int32, (LEVELS, LANES), 1)


def take(block, index):
    return jnp.take_along_axis(block, index, axis=1, mode="promise_in_bounds")


def level_rows(k):
    return pl.ds(k, BLOCKS, stride=LEVELS)


def tile_rows(j):
    return pl.ds(j * LEVELS, LEVELS)


def column_solve(rhs, inverse, ratio, couple):
    partial = [[] for _ in rhs]
    for k in range(LEVELS):
        for values, done in zip(rhs, partial):
            current = values[k]
            if k > 0:
                current = current + couple[k - 1] * done[-1]
            done.append(current * inverse[k])
    found = [[done[-1]] for done in partial]
    for k in range(LEVELS - 2, -1, -1):
        for done, values in zip(partial, found):
            values.insert(0, done[k] + ratio[k] * values[0])
    return found


def column_factors(couples, depths):
    factors = [([], []) for _ in couples]
    for k in range(LEVELS):
        for couple, depth, (inverse, ratio) in zip(couples, depths, factors):
            pivot = 1.0 + couple[k]
            if k > 0:
                pivot = pivot + couple[k - 1] - couple[k - 1] * ratio[-1]
            inv = 1.0 / pivot
            if depth is not None:
                inv = jnp.where(depth > k, inv, 0.0)
            inverse.append(inv)
            ratio.append(couple[k] * inv)
    return factors


def beside(block, lane):
    b = lane % 32
    return jnp.where(b > 0, pltpu.roll(block, 1, 1), 0.0) + jnp.where(b < 31, pltpu.roll(block, LANES - 1, 1), 0.0)


def spread_matrix():
    matrix = np.zeros((3, LANES, 3, LANES), np.float32)
    own, beyond, edge = range(3)
    sides = ((1, 0), (-1, 0), (0, 1), (0, -1))
    diagonals = ((1, 1), (1, -1), (-1, 1), (-1, -1))
    moves = [[(0, 0, 1.0)]]
    for offsets in (sides, diagonals):
        moves.append([(0, 0, -4.0)] + [(da, db, 1.0) for da, db in offsets])
    for source in range(3):
        for q in range(4):
            for b in range(32):
                for da, db, weight in moves[source]:
                    row, column = q + da, b + db
                    inside = 0 <= row < 4
                    into = matrix[source, 32 * q + b]
                    if 0 <= column < 32:
                        if inside:
                            into[own, 32 * row + column] += weight
                        else:
                            into[beyond, (0 if row > 0 else 96) + column] += weight
                            into[edge, (0 if row < 0 else 96) + column] += weight
                    if column in (-1, 0, 31, 32):
                        kind = 8 if column in (0, 31) else 0
                        side = 0 if column > 0 else 4
                        into[edge if inside else beyond, 32 + kind + side + row % 4] += weight
    return matrix.reshape(3 * LANES, 3 * LANES)


def split(values):
    high = values.astype(jnp.bfloat16)
    return high, (values - high.astype(jnp.float32)).astype(jnp.bfloat16)


def spread_products(z_ref, lat_ref, dia_ref, mat_ref, left_ref, product_ref):
    rows = BLOCKS * LEVELS
    for f in range(FIELDS):
        z = z_ref[f]
        p = f // TRACERS
        for i, values in enumerate((z, lat_ref[p] * z, dia_ref[p] * z)):
            high, low = split(values)
            left_ref[f * rows : (f + 1) * rows, i * LANES : (i + 1) * LANES] = high
            left_ref[f * rows : (f + 1) * rows, (3 + i) * LANES : (4 + i) * LANES] = low
    width = product_ref.shape[1]
    right = mat_ref[:, :width]
    product_ref[...] = jnp.dot(
        left_ref[...], jnp.concatenate([right, right], axis=0), preferred_element_type=jnp.float32
    )


def product_blocks(product_ref, f, i):
    rows = BLOCKS * LEVELS
    return [
        product_ref[f * rows + j * LEVELS : f * rows + (j + 1) * LEVELS, i * LANES : (i + 1) * LANES] for j in range(BLOCKS)
    ]


def from_neighbours(blocks, beyond, first_row, last_row):
    sums = []
    for j in range(BLOCKS):
        total = blocks[j]
        if j > 0:
            total = total + jnp.where(first_row, beyond[j - 1], 0.0)
        if j < BLOCKS - 1:
            total = total + jnp.where(last_row, beyond[j + 1], 0.0)
        sums.append(total)
    return sums


def pack_lines(columns, lane):
    residue = lane % 32
    mixed = pltpu.roll(columns[0], 1, 1)
    for j in range(1, BLOCKS):
        mixed = jnp.where(residue // 2 == j, pltpu.roll(columns[j], 2 * j + 1, 1), mixed)
    q, j = residue % 4, residue // 4
    index = jnp.where(lane < 64, 32 * ((q + 1) % 4) + 2 * j, 32 * q + 2 * j + 1)
    return jnp.where(lane < 32, columns[0], jnp.where(lane >= 96, columns[-1], take(mixed, index)))


def pack_products(own, beyond, edge, lane):
    q = lane % 4
    sides = from_neighbours(edge, beyond, q == 0, q == 3)
    mixed = pltpu.roll(sides[0], LANES - 32, 1)
    for j in range(1, BLOCKS):
        moved = pltpu.roll(sides[j], (16 * j - 32) % LANES, 1) if j != 2 else sides[j]
        mixed = jnp.where(lane // 16 == j, moved, mixed)
    index = 16 * (lane % 32 // 4) + q + jnp.where(lane >= 64, 4, 0)
    low, high = lane < 32, lane >= 96
    strips = jnp.where(low, edge[0], jnp.where(high, edge[-1], take(mixed, index)))
    lines = jnp.where(low, own[0], jnp.where(high, own[-1], take(mixed, index + 8)))
    return strips, lines


def unpack_lines(outer, inner, lane):
    residue = lane % 32
    j, part, q = residue // 4, residue % 4, lane // 32
    index = jnp.where(part < 2, 32 + 4 * j + (q + 3) % 4, 64 + 4 * j + q)
    mixed = jnp.where((part == 0) | (part == 3), take(inner, index), take(outer, index))
    near = (residue < 2) | (residue >= 30)
    adds = [jnp.where(near, pltpu.roll(mixed, (LANES - 4 * j - 2) % LANES, 1), 0.0) for j in range(BLOCKS)]
    segment = lane // 32
    low = jnp.where(segment == 0, outer, jnp.where(segment == 1, pltpu.roll(inner, 32, 1), 0.0))
    high = jnp.where(segment == 3, outer, jnp.where(segment == 2, pltpu.roll(inner, LANES - 32, 1), 0.0))
    adds[0] = adds[0] + low
    adds[-1] = adds[-1] + high
    return adds


def pack_corners(line, lane):
    c = lane % 4
    return take(line, jnp.where(c == 0, 0, jnp.where(c == 1, 31, jnp.where(c == 2, 127, 96))))


def first_kernel(
    *refs,
):
    sources, refs = refs[:9], refs[9:]
    pay_ref, y_ref, fac_ref, dep_ref, lat_ref, dia_ref, mat_ref, home_ref, edge_ref, corner_ref = refs[:10]
    ver_ref, x_ref, z_ref, left_ref, product_ref, sems = refs[10:]
    targets = (dep_ref, ver_ref, x_ref, lat_ref, dia_ref, mat_ref, home_ref, edge_ref, corner_ref)
    moves = [pltpu.make_async_copy(source, target, sems.at[i]) for i, (source, target) in enumerate(zip(sources, targets))]
    for move in moves:
        move.start()
    lane = lane_iota()
    level = lax.broadcasted_iota(jnp.int32, (LEVELS, LANES), 0)
    group = lane // 32
    corners = jnp.zeros((LEVELS, LANES), jnp.float32)
    ends = jnp.zeros((LEVELS, LANES), jnp.float32)
    end_edge = lane % 8 // 2
    end_lane = 32 * (end_edge ^ (end_edge // 2)) + 31 * (lane % 2)
    moves[0].wait()
    moves[1].wait()
    depth = [dep_ref[pl.ds(p, BLOCKS, stride=PLACES), :] for p in range(PLACES)]
    couple = [
        [jnp.where(depth[p] > k + 1, ver_ref[p, level_rows(k), :], 0.0) for k in range(LEVELS - 1)]
        + [jnp.zeros((BLOCKS, LANES), jnp.float32)]
        for p in range(PLACES)
    ]
    factors = column_factors(couple, depth)
    for p in range(PLACES):
        for k in range(LEVELS):
            fac_ref[p, 0, k] = factors[p][0][k]
            fac_ref[p, 1, k] = factors[p][1][k]
            fac_ref[p, 2, k] = couple[p][k]
    moves[2].wait()
    for p in range(PLACES):
        fields = [p * TRACERS + t for t in range(TRACERS)]
        found = column_solve(
            [[x_ref[f, level_rows(k), :] for k in range(LEVELS)] for f in fields], *factors[p], couple[p]
        )
        for k in range(LEVELS):
            for f, values in zip(fields, found):
                z_ref[f, level_rows(k), :] = values[k]
    for move in moves[3:]:
        move.wait()
    spread_products(z_ref, lat_ref, dia_ref, mat_ref, left_ref, product_ref)
    for p in range(PLACES):
        wet_lat, wet_dia, link = [], [], []
        for j in range(BLOCKS):
            row = dep_ref[j * PLACES + p : j * PLACES + p + 1, :]
            wet_lat.append(jnp.where(row > level, lat_ref[p, tile_rows(j), :], 0.0))
            wet_dia.append(jnp.where(row > level, dia_ref[p, tile_rows(j), :], 0.0))
            link.append(jnp.where((row > level + 1) & (level < LEVELS - 1), ver_ref[p, tile_rows(j), :], 0.0))
        coefs = [pack_lines(blocks, lane) for blocks in (link, wet_lat, wet_dia)]
        for i in range(3):
            pay_ref[12 + p * 3 + i] = coefs[i]
        link_corners = pack_corners(coefs[0], lane)
        dia_corners = pack_corners(coefs[2], lane)
        for t in range(TRACERS):
            f = p * TRACERS + t
            own, beyond, edge = (product_blocks(product_ref, f, i) for i in range(3))
            inner = from_neighbours(own, beyond, lane < 32, lane >= 96)
            for j in range(BLOCKS):
                y_ref[f, tile_rows(j), :] = inner[j]
            strips, lines = pack_products(inner, beyond, edge, lane)
            pay_ref[f] = strips
            pay_ref[FIELDS + f] = lines
            across = jnp.where(
                lane < 64,
                dia_ref[p, tile_rows(0), :] * z_ref[f, tile_rows(0), :],
                dia_ref[p, tile_rows(BLOCKS - 1), :] * z_ref[f, tile_rows(BLOCKS - 1), :],
            )
            cells = jnp.where(
                group == 0,
                pack_corners(across, lane),
                jnp.where(group == 1, pack_corners(lines, lane), jnp.where(group == 2, link_corners, dia_corners)),
            )
            corners = jnp.where(lane % 32 // 4 == p * 4 + t, cells, corners)
            ends = jnp.where(lane // 8 == p * 4 + t, take(strips, end_lane), ends)
    pay_ref[CORNER_BLOCK] = corners
    pay_ref[END_BLOCK] = ends


def pick(values, index, bits):
    packed = 0
    for i, value in enumerate(values):
        packed |= value << (bits * i)
    return lax.shift_right_logical(jnp.int32(packed), index * bits) & (2**bits - 1)


def window_kernel(
    home_ref, edge_ref, corner_ref, y_ref, fac_ref, lat_ref, dia_ref, dep_ref, mat_ref, pay_ref,
    out_ref, part_ref, own_ref, z_ref, link_ref, left_ref, product_ref,
):
    row = lax.axis_index("row")
    col = lax.axis_index("col")
    col_count = lax.axis_size("col")
    device = row * col_count + col

    def scan(t, found):
        here = home_ref[0, t]
        return tuple(jnp.where(here == device * PLACES + p, t, found[p]) for p in range(PLACES))

    tile_count = home_ref.shape[1]
    unroll = 8 if tile_count % 8 == 0 else 1

    def scan_some(i, found):
        for s in range(unroll):
            found = scan(i * unroll + s, found)
        return found

    tiles = lax.fori_loop(0, tile_count // unroll, scan_some, tuple(jnp.int32(-1) for _ in range(PLACES)))

    def block_of(tile):
        place = home_ref[0, tile]
        other = lax.shift_right_logical(place, 1)
        slot = (other ^ device) & (2 * col_count - 1)
        return slot * BLOCK_COUNT, place & 1

    def edge_of(tile, edge):
        code = edge_ref[edge, tile]
        return lax.shift_right_logical(code, 3), lax.shift_right_logical(code, 1) & 3, code & 1

    def strip_end(tile, edge_end):
        other, f, r = edge_of(tile, lax.shift_right_logical(edge_end, 1))
        base, place = block_of(other)
        return base + END_BLOCK, place * 32 + f * 2 + ((edge_end & 1) ^ r)

    def point(tile, corner):
        code = corner_ref[corner, tile]
        safe = jnp.maximum(code, 0)
        other, g = lax.shift_right_logical(safe, 2), safe & 3
        base, place = block_of(other)
        return base + CORNER_BLOCK, jnp.where(code >= 0, place * 16 + g, -1), other, g

    for p in range(PLACES):
        at = p * TABLE
        tile = jnp.maximum(tiles[p], 0)
        out_ref[at + OCCUPIED_AT] = jnp.where(tiles[p] >= 0, 1, 0)
        for e in range(4):
            other, f, r = edge_of(tile, e)
            base, place = block_of(other)
            out_ref[at + LINE_AT + 3 * e] = base + place * 3
            out_ref[at + LINE_AT + 3 * e + 1] = 32 * (f ^ lax.shift_right_logical(f, 1)) + 31 * r
            out_ref[at + LINE_AT + 3 * e + 2] = 1 - 2 * r
            for end in range(2):
                index = f * 2 + (end ^ r)
                strip_row, strip_lane = strip_end(other, pick(OTHER_EDGE, index, 2) * 2 + pick(OTHER_END, index, 1))
                point_row, point_lane, _, _ = point(other, pick(CORNER_OF, index, 2))
                slot = at + END_AT + 4 * (2 * e + end)
                out_ref[slot] = strip_row
                out_ref[slot + 1] = strip_lane
                out_ref[slot + 2] = point_row
                out_ref[slot + 3] = point_lane
        for c in range(4):
            point_row, point_lane, other, g = point(tile, c)
            slot = at + POINT_AT + 6 * c
            out_ref[slot] = point_row
            out_ref[slot + 1] = point_lane
            row_a, lane_a = strip_end(other, pick(CORNER_A, g, 3))
            row_b, lane_b = strip_end(other, pick(CORNER_B, g, 3))
            out_ref[slot + 2] = row_a
            out_ref[slot + 3] = lane_a
            out_ref[slot + 4] = row_b
            out_ref[slot + 5] = lane_b

    lane = lane_iota()
    level = lax.broadcasted_iota(jnp.int32, (LEVELS, LANES), 0)
    for p in range(PLACES):
        fields = [p * TRACERS + t for t in range(TRACERS)]
        inverse = [fac_ref[p, 0, k] for k in range(LEVELS)]
        ratio = [fac_ref[p, 1, k] for k in range(LEVELS)]
        couple = [fac_ref[p, 2, k] for k in range(LEVELS)]
        found = column_solve(
            [[y_ref[f, level_rows(k), :] for k in range(LEVELS)] for f in fields], inverse, ratio, couple
        )
        for k in range(LEVELS):
            for f, values in zip(fields, found):
                z_ref[f, level_rows(k), :] = values[k]
    spread_products(z_ref, lat_ref, dia_ref, mat_ref, left_ref, product_ref)
    for f in range(FIELDS):
        own, beyond = (product_blocks(product_ref, f, i) for i in range(2))
        inner = from_neighbours(own, beyond, lane < 32, lane >= 96)
        for j in range(BLOCKS):
            part_ref[f, tile_rows(j), :] = jnp.where(tiles[f // TRACERS] >= 0, inner[j], 0.0)

    wet = []
    for p in range(PLACES):
        rows = [dep_ref[j * PLACES + p : j * PLACES + p + 1, :] for j in range(BLOCKS)]
        masks = [jnp.where(row > level, 1.0, 0.0) for row in rows]
        wet.append(pack_lines(masks, lane))
    for f in range(LEVELS):
        link_ref[0, tile_rows(f), :] = pay_ref[12 + f // TRACERS % PLACES * 3]
        link_ref[1, tile_rows(f), :] = wet[f // TRACERS % PLACES]
    couple = [link_ref[0, level_rows(k), :] for k in range(LEVELS)]
    ((inverse, ratio),) = column_factors([couple], [None])
    for k in range(LEVELS):
        mask = link_ref[1, level_rows(k), :]
        own_ref[0, k] = inverse[k] * mask
        own_ref[1, k] = ratio[k]
        own_ref[2, k] = couple[k]


def second_kernel(tab_ref, part_ref, own_ref, *refs):
    pay_refs = refs[:-5]
    out_ref, all_ref, own_line_ref, line_ref, link_ref = refs[-5:]
    lane = lane_iota()
    zero = jnp.zeros((LEVELS, LANES), jnp.float32)
    for slot, ref in enumerate(pay_refs):
        for i in range(BLOCK_COUNT):
            all_ref[slot * BLOCK_COUNT + i] = ref[i]
    segment, position = lane // 32, lane % 32
    edge = segment ^ (segment // 2)
    line_end = (position == 0) | (position == 31)

    strips, lines, line_lat, line_dia = [], [], [], []
    for p in range(PLACES):
        at = p * TABLE + LINE_AT
        rows = [tab_ref[at + 3 * e] for e in range(4)]
        places = [tab_ref[at + 3 * e + 1] for e in range(4)]
        signs = [tab_ref[at + 3 * e + 2] for e in range(4)]
        index = zero.astype(jnp.int32)
        for e in range(4):
            index = jnp.where(edge == e, places[e] + signs[e] * position, index)

        def fetch(block):
            found = take(all_ref[rows[0] + block], index)
            for e in range(1, 4):
                found = jnp.where(edge == e, take(all_ref[rows[e] + block], index), found)
            return found

        for t in range(TRACERS):
            strips.append(fetch(t))
            lines.append(fetch(FIELDS + t))
        link = fetch(12)
        for t in range(TRACERS):
            link_ref[tile_rows(p * TRACERS + t), :] = link
        line_lat.append(fetch(13))
        line_dia.append(fetch(14))

    ends = zero
    tracer = lane % 32 // 8
    for p in range(PLACES):
        for i in range(8):
            at = p * TABLE + END_AT + 4 * i
            here = (segment == p) & (lane % 8 == i)
            strip = take(all_ref[tab_ref[at]], tab_ref[at + 1] + tracer * 8)
            point_lane = tab_ref[at + 3]
            point = take(all_ref[tab_ref[at + 2]], jnp.maximum(point_lane, 0) + tracer * 4)
            ends = jnp.where(here, strip + jnp.where(point_lane >= 0, point, 0.0), ends)

    cells = zero
    cell_adds = zero
    cell_tracer = lane % 16 // 4
    for p in range(PLACES):
        for c in range(4):
            at = p * TABLE + POINT_AT + 6 * c
            here = (position // 16 == p) & (lane % 4 == c)
            point_lane = tab_ref[at + 1]
            cell = take(all_ref[tab_ref[at]], jnp.maximum(point_lane, 0) + 32 * segment + 4 * cell_tracer)
            cells = jnp.where(here & (point_lane >= 0), cell, cells)
            strip_a = take(all_ref[tab_ref[at + 2]], tab_ref[at + 3] + cell_tracer * 8)
            strip_b = take(all_ref[tab_ref[at + 4]], tab_ref[at + 5] + cell_tracer * 8)
            cell_adds = jnp.where(here, strip_a + strip_b, cell_adds)
    cell_adds = cell_adds + pltpu.roll(all_ref[CORNER_BLOCK], 32, 1)

    corner_of_lane = jnp.where(segment == 0, jnp.where(position == 31, 1, 0), jnp.where(position == 31, 2, 3))
    at_corner = line_end & ((segment == 0) | (segment == 3))
    for f in range(FIELDS):
        p, t = f // TRACERS, f % TRACERS
        spread = take(ends, p * 32 + t * 8 + edge * 2 + jnp.where(position == 31, 1, 0))
        line_ref[tile_rows(f), :] = lines[f] + all_ref[f] + jnp.where(line_end, spread, 0.0)
        points = take(cells, p * 16 + t * 4 + corner_of_lane)
        own_line_ref[tile_rows(f), :] = strips[f] + jnp.where(at_corner, points, 0.0)
    line_ref[tile_rows(FIELDS), :] = cells + cell_adds
    line_ref[tile_rows(FIELDS + 1), :] = zero
    own_line_ref[tile_rows(FIELDS), :] = zero
    own_line_ref[tile_rows(FIELDS + 1), :] = zero
    link_ref[tile_rows(FIELDS), :] = pltpu.roll(cells, LANES - 32, 1)
    link_ref[tile_rows(FIELDS + 1), :] = zero
    couple = [link_ref[level_rows(k), :] for k in range(LEVELS - 1)] + [zero]
    ((inverse, ratio),) = column_factors([couple], [None])
    (own_found,) = column_solve(
        [[own_line_ref[level_rows(k), :] for k in range(LEVELS)]],
        [own_ref[0, k] for k in range(LEVELS)],
        [own_ref[1, k] for k in range(LEVELS)],
        [own_ref[2, k] for k in range(LEVELS)],
    )
    (found,) = column_solve([[line_ref[level_rows(k), :] for k in range(LEVELS)]], inverse, ratio, couple)
    for k in range(LEVELS):
        own_line_ref[level_rows(k), :] = own_found[k]
        line_ref[level_rows(k), :] = found[k]
    points = line_ref[tile_rows(FIELDS), :] * pltpu.roll(cells, LANES - 64, 1)

    for p in range(PLACES):
        occupied = tab_ref[p * TABLE + OCCUPIED_AT] > 0
        own_lat, own_dia = all_ref[13 + 3 * p], all_ref[14 + 3 * p]
        for t in range(TRACERS):
            f = p * TRACERS + t
            line = line_ref[tile_rows(f), :]
            outer = line_lat[p] * line + beside(line_dia[p] * line, lane)
            outer = outer + jnp.where(at_corner, take(points, 32 + p * 16 + t * 4 + corner_of_lane), 0.0)
            line = own_line_ref[tile_rows(f), :]
            along, across = own_lat * line, own_dia * line
            outer = outer + line - 4.0 * (along + across) + beside(along, lane)
            inner = along + beside(across, lane)
            adds = unpack_lines(jnp.where(occupied, outer, 0.0), jnp.where(occupied, inner, 0.0), lane)
            for j in range(BLOCKS):
                out_ref[f, tile_rows(j), :] = part_ref[f, tile_rows(j), :] + adds[j]


def swap(value, axes, row_count, col_count, row_bit, col_bits):
    pairs = []
    for i in range(row_count):
        for j in range(col_count):
            pairs.append((i * col_count + j, (i ^ row_bit) * col_count + (j ^ col_bits)))
    return lax.ppermute(value, axes, pairs)


def tiled(array, lead):
    blocks = array.reshape(lead + (-1, BLOCKS, LANES))
    rows = blocks.shape[-3]
    order = tuple(range(len(lead))) + (len(lead) + 1, len(lead), len(lead) + 2)
    return blocks.transpose(order).reshape(lead + (BLOCKS * rows, LANES))


def on_device(adjoint_out, lateral, diagonal, vertical, depth, tile_home, edge_link, corner_link):
    row_count, col_count = lax.axis_size("row"), lax.axis_size("col")
    axes = ("row", "col")
    vmem = pl.BlockSpec(memory_space=pltpu.VMEM)
    smem = pl.BlockSpec(memory_space=pltpu.SMEM)
    params = pltpu.CompilerParams(vmem_limit_bytes=VMEM_LIMIT)
    rows = BLOCKS * LEVELS
    x = tiled(adjoint_out, (FIELDS,))
    lat = tiled(lateral, (PLACES,))
    dia = tiled(diagonal, (PLACES,))
    ver = tiled(vertical, (PLACES,))
    dep = tiled(depth, ())
    hbm = pl.BlockSpec(memory_space=pltpu.HBM)
    home, edges, corners = tile_home.reshape(1, -1), edge_link.T, corner_link.T
    matrix = jnp.asarray(spread_matrix(), jnp.bfloat16)
    sources = (dep, ver, x, lat, dia, matrix, home, edges, corners)
    payload, y, fac, dep, lat, dia, matrix, home, edges, corners = pl.pallas_call(
        first_kernel,
        out_shape=(
            f32((BLOCK_COUNT, LEVELS, LANES)),
            f32((FIELDS, rows, LANES)),
            f32((PLACES, 3, LEVELS, BLOCKS, LANES)),
        )
        + tuple(jax.ShapeDtypeStruct(value.shape, value.dtype) for value in (dep, lat, dia, matrix, home, edges, corners)),
        in_specs=[hbm] * len(sources),
        out_specs=(vmem,) * 10,
        scratch_shapes=[
            pltpu.VMEM((PLACES, rows, LANES), jnp.float32),
            pltpu.VMEM((FIELDS, rows, LANES), jnp.float32),
            pltpu.VMEM((FIELDS, rows, LANES), jnp.float32),
            pltpu.VMEM((FIELDS * rows, 6 * LANES), jnp.bfloat16),
            pltpu.VMEM((FIELDS * rows, 3 * LANES), jnp.float32),
            pltpu.SemaphoreType.DMA((len(sources),)),
        ],
        compiler_params=params,
        name="first",
    )(*(pltpu.with_memory_space_constraint(value, pltpu.HBM) for value in sources))
    near = [swap(payload, axes, row_count, col_count, 0, m) for m in range(1, col_count)]
    table, part, own = pl.pallas_call(
        window_kernel,
        out_shape=(
            jax.ShapeDtypeStruct((PLACES * TABLE,), jnp.int32),
            f32((FIELDS, rows, LANES)),
            f32((3, LEVELS, LEVELS, LANES)),
        ),
        in_specs=[smem] * 3 + [vmem] * 7,
        out_specs=(smem, vmem, vmem),
        scratch_shapes=[
            pltpu.VMEM((FIELDS, rows, LANES), jnp.float32),
            pltpu.VMEM((2, rows, LANES), jnp.float32),
            pltpu.VMEM((FIELDS * rows, 6 * LANES), jnp.bfloat16),
            pltpu.VMEM((FIELDS * rows, 2 * LANES), jnp.float32),
        ],
        compiler_params=params,
        name="window",
    )(home, edges, corners, y, fac, lat, dia, dep, matrix, payload)
    *near, table = lax.optimization_barrier((*near, table))
    twin = swap(payload, axes, row_count, col_count, 1, 0)
    far = [swap(value, axes, row_count, col_count, 1, 0) for value in near]
    payloads = [payload] + near + [twin] + far
    out = pl.pallas_call(
        second_kernel,
        out_shape=f32((FIELDS, rows, LANES)),
        in_specs=[smem] + [vmem] * (2 + len(payloads)),
        out_specs=vmem,
        scratch_shapes=[
            pltpu.VMEM((len(payloads) * BLOCK_COUNT, LEVELS, LANES), jnp.float32),
            pltpu.VMEM((rows, LANES), jnp.float32),
            pltpu.VMEM((rows, LANES), jnp.float32),
            pltpu.VMEM((rows, LANES), jnp.float32),
        ],
        compiler_params=pltpu.CompilerParams(vmem_limit_bytes=VMEM_LIMIT + 2 * len(payloads) * BLOCK_COUNT * 4096),
        name="second",
    )(table, part, own, *payloads)
    out = out.reshape(FIELDS, BLOCKS, LEVELS, LANES).transpose(0, 2, 1, 3)
    return out.reshape(adjoint_out.shape)


def solution(mesh):
    return jax.shard_map(
        on_device,
        mesh=mesh,
        in_specs=(
            P("row", "col", None, None, None, None),
            P("row", "col", None, None, None),
            P("row", "col", None, None, None),
            P("row", "col", None, None, None),
            P("row", "col", None, None),
            P(),
            P(),
            P(),
        ),
        out_specs=P("row", "col", None, None, None, None),
        check_vma=False,
    )
```

```python
import jax
import jax.numpy as jnp
import numpy as np
from jax import lax
from jax.experimental import pallas as pl
from jax.experimental.pallas import tpu as pltpu
from jax.sharding import PartitionSpec as P

LEVELS = 8
PLACES = 2
TRACERS = 3
FIELDS = PLACES * TRACERS
BLOCKS = 8
LANES = 128
BLOCK_COUNT = 20
CORNER_BLOCK = 18
END_BLOCK = 19
VMEM_LIMIT = 8 * 2**20

CORNER_OF = (0, 1, 1, 2, 3, 2, 0, 3)
OTHER_EDGE = (3, 1, 0, 2, 3, 1, 0, 2)
OTHER_END = (0, 0, 1, 1, 1, 1, 0, 0)
CORNER_A = (0, 1, 3, 4)
CORNER_B = (6, 2, 5, 7)

LINE_AT = 0
END_AT = 12
POINT_AT = 44
OCCUPIED_AT = 68
TABLE = 72


def f32(shape):
    return jax.ShapeDtypeStruct(shape, jnp.float32)


def lane_iota():
    return lax.broadcasted_iota(jnp.int32, (LEVELS, LANES), 1)


def take(block, index):
    return jnp.take_along_axis(block, index, axis=1, mode="promise_in_bounds")


def level_rows(k):
    return pl.ds(k, BLOCKS, stride=LEVELS)


def tile_rows(j):
    return pl.ds(j * LEVELS, LEVELS)


def column_solve(rhs, inverse, ratio, couple):
    partial = [[] for _ in rhs]
    for k in range(LEVELS):
        for values, done in zip(rhs, partial):
            current = values[k]
            if k > 0:
                current = current + couple[k - 1] * done[-1]
            done.append(current * inverse[k])
    found = [[done[-1]] for done in partial]
    for k in range(LEVELS - 2, -1, -1):
        for done, values in zip(partial, found):
            values.insert(0, done[k] + ratio[k] * values[0])
    return found


def column_factors(couples, depths):
    factors = [([], []) for _ in couples]
    for k in range(LEVELS):
        for couple, depth, (inverse, ratio) in zip(couples, depths, factors):
            pivot = 1.0 + couple[k]
            if k > 0:
                pivot = pivot + couple[k - 1] - couple[k - 1] * ratio[-1]
            inv = 1.0 / pivot
            if depth is not None:
                inv = jnp.where(depth > k, inv, 0.0)
            inverse.append(inv)
            ratio.append(couple[k] * inv)
    return factors


def beside(block, lane):
    b = lane % 32
    return jnp.where(b > 0, pltpu.roll(block, 1, 1), 0.0) + jnp.where(b < 31, pltpu.roll(block, LANES - 1, 1), 0.0)


def spread_matrix():
    matrix = np.zeros((3, LANES, 3, LANES), np.float32)
    own, beyond, edge = range(3)
    sides = ((1, 0), (-1, 0), (0, 1), (0, -1))
    diagonals = ((1, 1), (1, -1), (-1, 1), (-1, -1))
    moves = [[(0, 0, 1.0)]]
    for offsets in (sides, diagonals):
        moves.append([(0, 0, -4.0)] + [(da, db, 1.0) for da, db in offsets])
    for source in range(3):
        for q in range(4):
            for b in range(32):
                for da, db, weight in moves[source]:
                    row, column = q + da, b + db
                    inside = 0 <= row < 4
                    into = matrix[source, 32 * q + b]
                    if 0 <= column < 32:
                        if inside:
                            into[own, 32 * row + column] += weight
                        else:
                            into[beyond, (0 if row > 0 else 96) + column] += weight
                            into[edge, (0 if row < 0 else 96) + column] += weight
                    if column in (-1, 0, 31, 32):
                        kind = 8 if column in (0, 31) else 0
                        side = 0 if column > 0 else 4
                        into[edge if inside else beyond, 32 + kind + side + row % 4] += weight
    return matrix.reshape(3 * LANES, 3 * LANES)


def split(values):
    high = values.astype(jnp.bfloat16)
    return high, (values - high.astype(jnp.float32)).astype(jnp.bfloat16)


def spread_products(z_ref, lat_ref, dia_ref, mat_ref, left_ref, product_ref):
    rows = BLOCKS * LEVELS
    for f in range(FIELDS):
        z = z_ref[f]
        p = f // TRACERS
        for i, values in enumerate((z, lat_ref[p] * z, dia_ref[p] * z)):
            high, low = split(values)
            left_ref[f * rows : (f + 1) * rows, i * LANES : (i + 1) * LANES] = high
            left_ref[f * rows : (f + 1) * rows, (3 + i) * LANES : (4 + i) * LANES] = low
    width = product_ref.shape[1]
    right = mat_ref[:, :width]
    product_ref[...] = jnp.dot(
        left_ref[...], jnp.concatenate([right, right], axis=0), preferred_element_type=jnp.float32
    )


def product_blocks(product_ref, f, i):
    rows = BLOCKS * LEVELS
    return [
        product_ref[f * rows + j * LEVELS : f * rows + (j + 1) * LEVELS, i * LANES : (i + 1) * LANES] for j in range(BLOCKS)
    ]


def from_neighbours(blocks, beyond, first_row, last_row):
    sums = []
    for j in range(BLOCKS):
        total = blocks[j]
        if j > 0:
            total = total + jnp.where(first_row, beyond[j - 1], 0.0)
        if j < BLOCKS - 1:
            total = total + jnp.where(last_row, beyond[j + 1], 0.0)
        sums.append(total)
    return sums


def pack_lines(columns, lane):
    residue = lane % 32
    mixed = pltpu.roll(columns[0], 1, 1)
    for j in range(1, BLOCKS):
        mixed = jnp.where(residue // 2 == j, pltpu.roll(columns[j], 2 * j + 1, 1), mixed)
    q, j = residue % 4, residue // 4
    index = jnp.where(lane < 64, 32 * ((q + 1) % 4) + 2 * j, 32 * q + 2 * j + 1)
    return jnp.where(lane < 32, columns[0], jnp.where(lane >= 96, columns[-1], take(mixed, index)))


def pack_products(own, beyond, edge, lane):
    q = lane % 4
    sides = from_neighbours(edge, beyond, q == 0, q == 3)
    mixed = pltpu.roll(sides[0], LANES - 32, 1)
    for j in range(1, BLOCKS):
        moved = pltpu.roll(sides[j], (16 * j - 32) % LANES, 1) if j != 2 else sides[j]
        mixed = jnp.where(lane // 16 == j, moved, mixed)
    index = 16 * (lane % 32 // 4) + q + jnp.where(lane >= 64, 4, 0)
    low, high = lane < 32, lane >= 96
    strips = jnp.where(low, edge[0], jnp.where(high, edge[-1], take(mixed, index)))
    lines = jnp.where(low, own[0], jnp.where(high, own[-1], take(mixed, index + 8)))
    return strips, lines


def unpack_lines(outer, inner, lane):
    residue = lane % 32
    j, part, q = residue // 4, residue % 4, lane // 32
    index = jnp.where(part < 2, 32 + 4 * j + (q + 3) % 4, 64 + 4 * j + q)
    mixed = jnp.where((part == 0) | (part == 3), take(inner, index), take(outer, index))
    near = (residue < 2) | (residue >= 30)
    adds = [jnp.where(near, pltpu.roll(mixed, (LANES - 4 * j - 2) % LANES, 1), 0.0) for j in range(BLOCKS)]
    segment = lane // 32
    low = jnp.where(segment == 0, outer, jnp.where(segment == 1, pltpu.roll(inner, 32, 1), 0.0))
    high = jnp.where(segment == 3, outer, jnp.where(segment == 2, pltpu.roll(inner, LANES - 32, 1), 0.0))
    adds[0] = adds[0] + low
    adds[-1] = adds[-1] + high
    return adds


def pack_corners(line, lane):
    c = lane % 4
    return take(line, jnp.where(c == 0, 0, jnp.where(c == 1, 31, jnp.where(c == 2, 127, 96))))


def first_kernel(
    *refs,
):
    sources, refs = refs[:9], refs[9:]
    pay_ref, y_ref, fac_ref, dep_ref, lat_ref, dia_ref, mat_ref, home_ref, edge_ref, corner_ref = refs[:10]
    ver_ref, x_ref, z_ref, left_ref, product_ref, sems = refs[10:]
    targets = (dep_ref, ver_ref, x_ref, lat_ref, dia_ref, mat_ref, home_ref, edge_ref, corner_ref)
    moves = [pltpu.make_async_copy(source, target, sems.at[i]) for i, (source, target) in enumerate(zip(sources, targets))]
    for move in moves:
        move.start()
    lane = lane_iota()
    level = lax.broadcasted_iota(jnp.int32, (LEVELS, LANES), 0)
    group = lane // 32
    corners = jnp.zeros((LEVELS, LANES), jnp.float32)
    ends = jnp.zeros((LEVELS, LANES), jnp.float32)
    end_edge = lane % 8 // 2
    end_lane = 32 * (end_edge ^ (end_edge // 2)) + 31 * (lane % 2)
    moves[0].wait()
    moves[1].wait()
    depth = [dep_ref[pl.ds(p, BLOCKS, stride=PLACES), :] for p in range(PLACES)]
    couple = [
        [jnp.where(depth[p] > k + 1, ver_ref[p, level_rows(k), :], 0.0) for k in range(LEVELS - 1)]
        + [jnp.zeros((BLOCKS, LANES), jnp.float32)]
        for p in range(PLACES)
    ]
    factors = column_factors(couple, depth)
    for p in range(PLACES):
        for k in range(LEVELS):
            fac_ref[p, 0, k] = factors[p][0][k]
            fac_ref[p, 1, k] = factors[p][1][k]
            fac_ref[p, 2, k] = couple[p][k]
    moves[2].wait()
    for p in range(PLACES):
        fields = [p * TRACERS + t for t in range(TRACERS)]
        found = column_solve(
            [[x_ref[f, level_rows(k), :] for k in range(LEVELS)] for f in fields], *factors[p], couple[p]
        )
        for k in range(LEVELS):
            for f, values in zip(fields, found):
                z_ref[f, level_rows(k), :] = values[k]
    for move in moves[3:]:
        move.wait()
    spread_products(z_ref, lat_ref, dia_ref, mat_ref, left_ref, product_ref)
    for p in range(PLACES):
        wet_lat, wet_dia, link = [], [], []
        for j in range(BLOCKS):
            row = dep_ref[j * PLACES + p : j * PLACES + p + 1, :]
            wet_lat.append(jnp.where(row > level, lat_ref[p, tile_rows(j), :], 0.0))
            wet_dia.append(jnp.where(row > level, dia_ref[p, tile_rows(j), :], 0.0))
            link.append(jnp.where((row > level + 1) & (level < LEVELS - 1), ver_ref[p, tile_rows(j), :], 0.0))
        coefs = [pack_lines(blocks, lane) for blocks in (link, wet_lat, wet_dia)]
        for i in range(3):
            pay_ref[12 + p * 3 + i] = coefs[i]
        link_corners = pack_corners(coefs[0], lane)
        dia_corners = pack_corners(coefs[2], lane)
        for t in range(TRACERS):
            f = p * TRACERS + t
            own, beyond, edge = (product_blocks(product_ref, f, i) for i in range(3))
            inner = from_neighbours(own, beyond, lane < 32, lane >= 96)
            for j in range(BLOCKS):
                y_ref[f, tile_rows(j), :] = inner[j]
            strips, lines = pack_products(inner, beyond, edge, lane)
            pay_ref[f] = strips
            pay_ref[FIELDS + f] = lines
            across = jnp.where(
                lane < 64,
                dia_ref[p, tile_rows(0), :] * z_ref[f, tile_rows(0), :],
                dia_ref[p, tile_rows(BLOCKS - 1), :] * z_ref[f, tile_rows(BLOCKS - 1), :],
            )
            cells = jnp.where(
                group == 0,
                pack_corners(across, lane),
                jnp.where(group == 1, pack_corners(lines, lane), jnp.where(group == 2, link_corners, dia_corners)),
            )
            corners = jnp.where(lane % 32 // 4 == p * 4 + t, cells, corners)
            ends = jnp.where(lane // 8 == p * 4 + t, take(strips, end_lane), ends)
    pay_ref[CORNER_BLOCK] = corners
    pay_ref[END_BLOCK] = ends


def pick(values, index, bits):
    packed = 0
    for i, value in enumerate(values):
        packed |= value << (bits * i)
    return lax.shift_right_logical(jnp.int32(packed), index * bits) & (2**bits - 1)


def window_kernel(
    home_ref, edge_ref, corner_ref, y_ref, fac_ref, lat_ref, dia_ref, dep_ref, mat_ref, pay_ref,
    out_ref, part_ref, own_ref, z_ref, link_ref, left_ref, product_ref,
):
    row = lax.axis_index("row")
    col = lax.axis_index("col")
    col_count = lax.axis_size("col")
    device = row * col_count + col

    def scan(t, found):
        here = home_ref[0, t]
        return tuple(jnp.where(here == device * PLACES + p, t, found[p]) for p in range(PLACES))

    tile_count = home_ref.shape[1]
    unroll = 8 if tile_count % 8 == 0 else 1

    def scan_some(i, found):
        for s in range(unroll):
            found = scan(i * unroll + s, found)
        return found

    tiles = lax.fori_loop(0, tile_count // unroll, scan_some, tuple(jnp.int32(-1) for _ in range(PLACES)))

    def block_of(tile):
        place = home_ref[0, tile]
        other = lax.shift_right_logical(place, 1)
        slot = (other ^ device) & (2 * col_count - 1)
        return slot * BLOCK_COUNT, place & 1

    def edge_of(tile, edge):
        code = edge_ref[edge, tile]
        return lax.shift_right_logical(code, 3), lax.shift_right_logical(code, 1) & 3, code & 1

    def strip_end(tile, edge_end):
        other, f, r = edge_of(tile, lax.shift_right_logical(edge_end, 1))
        base, place = block_of(other)
        return base + END_BLOCK, place * 32 + f * 2 + ((edge_end & 1) ^ r)

    def point(tile, corner):
        code = corner_ref[corner, tile]
        safe = jnp.maximum(code, 0)
        other, g = lax.shift_right_logical(safe, 2), safe & 3
        base, place = block_of(other)
        return base + CORNER_BLOCK, jnp.where(code >= 0, place * 16 + g, -1), other, g

    for p in range(PLACES):
        at = p * TABLE
        tile = jnp.maximum(tiles[p], 0)
        out_ref[at + OCCUPIED_AT] = jnp.where(tiles[p] >= 0, 1, 0)
        for e in range(4):
            other, f, r = edge_of(tile, e)
            base, place = block_of(other)
            out_ref[at + LINE_AT + 3 * e] = base + place * 3
            out_ref[at + LINE_AT + 3 * e + 1] = 32 * (f ^ lax.shift_right_logical(f, 1)) + 31 * r
            out_ref[at + LINE_AT + 3 * e + 2] = 1 - 2 * r
            for end in range(2):
                index = f * 2 + (end ^ r)
                strip_row, strip_lane = strip_end(other, pick(OTHER_EDGE, index, 2) * 2 + pick(OTHER_END, index, 1))
                point_row, point_lane, _, _ = point(other, pick(CORNER_OF, index, 2))
                slot = at + END_AT + 4 * (2 * e + end)
                out_ref[slot] = strip_row
                out_ref[slot + 1] = strip_lane
                out_ref[slot + 2] = point_row
                out_ref[slot + 3] = point_lane
        for c in range(4):
            point_row, point_lane, other, g = point(tile, c)
            slot = at + POINT_AT + 6 * c
            out_ref[slot] = point_row
            out_ref[slot + 1] = point_lane
            row_a, lane_a = strip_end(other, pick(CORNER_A, g, 3))
            row_b, lane_b = strip_end(other, pick(CORNER_B, g, 3))
            out_ref[slot + 2] = row_a
            out_ref[slot + 3] = lane_a
            out_ref[slot + 4] = row_b
            out_ref[slot + 5] = lane_b

    lane = lane_iota()
    level = lax.broadcasted_iota(jnp.int32, (LEVELS, LANES), 0)
    for p in range(PLACES):
        fields = [p * TRACERS + t for t in range(TRACERS)]
        inverse = [fac_ref[p, 0, k] for k in range(LEVELS)]
        ratio = [fac_ref[p, 1, k] for k in range(LEVELS)]
        couple = [fac_ref[p, 2, k] for k in range(LEVELS)]
        found = column_solve(
            [[y_ref[f, level_rows(k), :] for k in range(LEVELS)] for f in fields], inverse, ratio, couple
        )
        for k in range(LEVELS):
            for f, values in zip(fields, found):
                z_ref[f, level_rows(k), :] = values[k]
    spread_products(z_ref, lat_ref, dia_ref, mat_ref, left_ref, product_ref)
    for f in range(FIELDS):
        own, beyond = (product_blocks(product_ref, f, i) for i in range(2))
        inner = from_neighbours(own, beyond, lane < 32, lane >= 96)
        for j in range(BLOCKS):
            part_ref[f, tile_rows(j), :] = jnp.where(tiles[f // TRACERS] >= 0, inner[j], 0.0)

    wet = []
    for p in range(PLACES):
        rows = [dep_ref[j * PLACES + p : j * PLACES + p + 1, :] for j in range(BLOCKS)]
        masks = [jnp.where(row > level, 1.0, 0.0) for row in rows]
        wet.append(pack_lines(masks, lane))
    for f in range(LEVELS):
        link_ref[0, tile_rows(f), :] = pay_ref[12 + f // TRACERS % PLACES * 3]
        link_ref[1, tile_rows(f), :] = wet[f // TRACERS % PLACES]
    couple = [link_ref[0, level_rows(k), :] for k in range(LEVELS)]
    ((inverse, ratio),) = column_factors([couple], [None])
    for k in range(LEVELS):
        mask = link_ref[1, level_rows(k), :]
        own_ref[0, k] = inverse[k] * mask
        own_ref[1, k] = ratio[k]
        own_ref[2, k] = couple[k]


def second_kernel(tab_ref, part_ref, own_ref, *refs):
    pay_refs = refs[:-5]
    out_ref, all_ref, own_line_ref, line_ref, link_ref = refs[-5:]
    lane = lane_iota()
    zero = jnp.zeros((LEVELS, LANES), jnp.float32)
    for slot, ref in enumerate(pay_refs):
        for i in range(BLOCK_COUNT):
            all_ref[slot * BLOCK_COUNT + i] = ref[i]
    segment, position = lane // 32, lane % 32
    edge = segment ^ (segment // 2)
    line_end = (position == 0) | (position == 31)

    strips, lines, line_lat, line_dia = [], [], [], []
    for p in range(PLACES):
        at = p * TABLE + LINE_AT
        rows = [tab_ref[at + 3 * e] for e in range(4)]
        places = [tab_ref[at + 3 * e + 1] for e in range(4)]
        signs = [tab_ref[at + 3 * e + 2] for e in range(4)]
        index = zero.astype(jnp.int32)
        for e in range(4):
            index = jnp.where(edge == e, places[e] + signs[e] * position, index)

        def fetch(block):
            found = take(all_ref[rows[0] + block], index)
            for e in range(1, 4):
                found = jnp.where(edge == e, take(all_ref[rows[e] + block], index), found)
            return found

        for t in range(TRACERS):
            strips.append(fetch(t))
            lines.append(fetch(FIELDS + t))
        link = fetch(12)
        for t in range(TRACERS):
            link_ref[tile_rows(p * TRACERS + t), :] = link
        line_lat.append(fetch(13))
        line_dia.append(fetch(14))

    ends = zero
    tracer = lane % 32 // 8
    for p in range(PLACES):
        for i in range(8):
            at = p * TABLE + END_AT + 4 * i
            here = (segment == p) & (lane % 8 == i)
            strip = take(all_ref[tab_ref[at]], tab_ref[at + 1] + tracer * 8)
            point_lane = tab_ref[at + 3]
            point = take(all_ref[tab_ref[at + 2]], jnp.maximum(point_lane, 0) + tracer * 4)
            ends = jnp.where(here, strip + jnp.where(point_lane >= 0, point, 0.0), ends)

    cells = zero
    cell_adds = zero
    cell_tracer = lane % 16 // 4
    for p in range(PLACES):
        for c in range(4):
            at = p * TABLE + POINT_AT + 6 * c
            here = (position // 16 == p) & (lane % 4 == c)
            point_lane = tab_ref[at + 1]
            cell = take(all_ref[tab_ref[at]], jnp.maximum(point_lane, 0) + 32 * segment + 4 * cell_tracer)
            cells = jnp.where(here & (point_lane >= 0), cell, cells)
            strip_a = take(all_ref[tab_ref[at + 2]], tab_ref[at + 3] + cell_tracer * 8)
            strip_b = take(all_ref[tab_ref[at + 4]], tab_ref[at + 5] + cell_tracer * 8)
            cell_adds = jnp.where(here, strip_a + strip_b, cell_adds)
    cell_adds = cell_adds + pltpu.roll(all_ref[CORNER_BLOCK], 32, 1)

    corner_of_lane = jnp.where(segment == 0, jnp.where(position == 31, 1, 0), jnp.where(position == 31, 2, 3))
    at_corner = line_end & ((segment == 0) | (segment == 3))
    for f in range(FIELDS):
        p, t = f // TRACERS, f % TRACERS
        spread = take(ends, p * 32 + t * 8 + edge * 2 + jnp.where(position == 31, 1, 0))
        line_ref[tile_rows(f), :] = lines[f] + all_ref[f] + jnp.where(line_end, spread, 0.0)
        points = take(cells, p * 16 + t * 4 + corner_of_lane)
        own_line_ref[tile_rows(f), :] = strips[f] + jnp.where(at_corner, points, 0.0)
    line_ref[tile_rows(FIELDS), :] = cells + cell_adds
    line_ref[tile_rows(FIELDS + 1), :] = zero
    own_line_ref[tile_rows(FIELDS), :] = zero
    own_line_ref[tile_rows(FIELDS + 1), :] = zero
    link_ref[tile_rows(FIELDS), :] = pltpu.roll(cells, LANES - 32, 1)
    link_ref[tile_rows(FIELDS + 1), :] = zero
    couple = [link_ref[level_rows(k), :] for k in range(LEVELS - 1)] + [zero]
    ((inverse, ratio),) = column_factors([couple], [None])
    (own_found,) = column_solve(
        [[own_line_ref[level_rows(k), :] for k in range(LEVELS)]],
        [own_ref[0, k] for k in range(LEVELS)],
        [own_ref[1, k] for k in range(LEVELS)],
        [own_ref[2, k] for k in range(LEVELS)],
    )
    (found,) = column_solve([[line_ref[level_rows(k), :] for k in range(LEVELS)]], inverse, ratio, couple)
    for k in range(LEVELS):
        own_line_ref[level_rows(k), :] = own_found[k]
        line_ref[level_rows(k), :] = found[k]
    points = line_ref[tile_rows(FIELDS), :] * pltpu.roll(cells, LANES - 64, 1)

    for p in range(PLACES):
        occupied = tab_ref[p * TABLE + OCCUPIED_AT] > 0
        own_lat, own_dia = all_ref[13 + 3 * p], all_ref[14 + 3 * p]
        for t in range(TRACERS):
            f = p * TRACERS + t
            line = line_ref[tile_rows(f), :]
            outer = line_lat[p] * line + beside(line_dia[p] * line, lane)
            outer = outer + jnp.where(at_corner, take(points, 32 + p * 16 + t * 4 + corner_of_lane), 0.0)
            line = own_line_ref[tile_rows(f), :]
            along, across = own_lat * line, own_dia * line
            outer = outer + line - 4.0 * (along + across) + beside(along, lane)
            inner = along + beside(across, lane)
            adds = unpack_lines(jnp.where(occupied, outer, 0.0), jnp.where(occupied, inner, 0.0), lane)
            for j in range(BLOCKS):
                out_ref[f, tile_rows(j), :] = part_ref[f, tile_rows(j), :] + adds[j]


def swap(value, axes, row_count, col_count, row_bit, col_bits):
    pairs = []
    for i in range(row_count):
        for j in range(col_count):
            pairs.append((i * col_count + j, (i ^ row_bit) * col_count + (j ^ col_bits)))
    return lax.ppermute(value, axes, pairs)


def tiled(array, lead):
    blocks = array.reshape(lead + (-1, BLOCKS, LANES))
    rows = blocks.shape[-3]
    order = tuple(range(len(lead))) + (len(lead) + 1, len(lead), len(lead) + 2)
    return blocks.transpose(order).reshape(lead + (BLOCKS * rows, LANES))


def on_device(adjoint_out, lateral, diagonal, vertical, depth, tile_home, edge_link, corner_link):
    row_count, col_count = lax.axis_size("row"), lax.axis_size("col")
    axes = ("row", "col")
    vmem = pl.BlockSpec(memory_space=pltpu.VMEM)
    smem = pl.BlockSpec(memory_space=pltpu.SMEM)
    params = pltpu.CompilerParams(vmem_limit_bytes=VMEM_LIMIT)
    rows = BLOCKS * LEVELS
    x = tiled(adjoint_out, (FIELDS,))
    lat = tiled(lateral, (PLACES,))
    dia = tiled(diagonal, (PLACES,))
    ver = tiled(vertical, (PLACES,))
    dep = tiled(depth, ())
    hbm = pl.BlockSpec(memory_space=pltpu.HBM)
    home, edges, corners = tile_home.reshape(1, -1), edge_link.T, corner_link.T
    matrix = jnp.asarray(spread_matrix(), jnp.bfloat16)
    sources = (dep, ver, x, lat, dia, matrix, home, edges, corners)
    payload, y, fac, dep, lat, dia, matrix, home, edges, corners = pl.pallas_call(
        first_kernel,
        out_shape=(
            f32((BLOCK_COUNT, LEVELS, LANES)),
            f32((FIELDS, rows, LANES)),
            f32((PLACES, 3, LEVELS, BLOCKS, LANES)),
        )
        + tuple(jax.ShapeDtypeStruct(value.shape, value.dtype) for value in (dep, lat, dia, matrix))
        + tuple(pltpu.SMEM(value.shape, value.dtype) for value in (home, edges, corners)),
        in_specs=[hbm] * len(sources),
        out_specs=(vmem,) * 7 + (smem,) * 3,
        scratch_shapes=[
            pltpu.VMEM((PLACES, rows, LANES), jnp.float32),
            pltpu.VMEM((FIELDS, rows, LANES), jnp.float32),
            pltpu.VMEM((FIELDS, rows, LANES), jnp.float32),
            pltpu.VMEM((FIELDS * rows, 6 * LANES), jnp.bfloat16),
            pltpu.VMEM((FIELDS * rows, 3 * LANES), jnp.float32),
            pltpu.SemaphoreType.DMA((len(sources),)),
        ],
        compiler_params=params,
        name="first",
    )(*(pltpu.with_memory_space_constraint(value, pltpu.HBM) for value in sources))
    near = [swap(payload, axes, row_count, col_count, 0, m) for m in range(1, col_count)]
    table, part, own = pl.pallas_call(
        window_kernel,
        out_shape=(
            pltpu.SMEM((PLACES * TABLE,), jnp.int32),
            f32((FIELDS, rows, LANES)),
            f32((3, LEVELS, LEVELS, LANES)),
        ),
        in_specs=[smem] * 3 + [vmem] * 7,
        out_specs=(smem, vmem, vmem),
        scratch_shapes=[
            pltpu.VMEM((FIELDS, rows, LANES), jnp.float32),
            pltpu.VMEM((2, rows, LANES), jnp.float32),
            pltpu.VMEM((FIELDS * rows, 6 * LANES), jnp.bfloat16),
            pltpu.VMEM((FIELDS * rows, 2 * LANES), jnp.float32),
        ],
        compiler_params=params,
        name="window",
    )(home, edges, corners, y, fac, lat, dia, dep, matrix, payload)
    near = [lax.optimization_barrier((value, table))[0] for value in near]
    twin = swap(lax.optimization_barrier((payload, table))[0], axes, row_count, col_count, 1, 0)
    far = [swap(value, axes, row_count, col_count, 1, 0) for value in near]
    payloads = [payload] + near + [twin] + far
    out = pl.pallas_call(
        second_kernel,
        out_shape=f32((FIELDS, rows, LANES)),
        in_specs=[smem] + [vmem] * (2 + len(payloads)),
        out_specs=vmem,
        scratch_shapes=[
            pltpu.VMEM((len(payloads) * BLOCK_COUNT, LEVELS, LANES), jnp.float32),
            pltpu.VMEM((rows, LANES), jnp.float32),
            pltpu.VMEM((rows, LANES), jnp.float32),
            pltpu.VMEM((rows, LANES), jnp.float32),
        ],
        compiler_params=pltpu.CompilerParams(vmem_limit_bytes=VMEM_LIMIT + 2 * len(payloads) * BLOCK_COUNT * 4096),
        name="second",
    )(table, part, own, *payloads)
    out = out.reshape(FIELDS, BLOCKS, LEVELS, LANES).transpose(0, 2, 1, 3)
    return out.reshape(adjoint_out.shape)


def solution(mesh):
    return jax.shard_map(
        on_device,
        mesh=mesh,
        in_specs=(
            P("row", "col", None, None, None, None),
            P("row", "col", None, None, None),
            P("row", "col", None, None, None),
            P("row", "col", None, None, None),
            P("row", "col", None, None),
            P(),
            P(),
            P(),
        ),
        out_specs=P("row", "col", None, None, None, None),
        check_vma=False,
    )
```

```python
import jax
import jax.numpy as jnp
import numpy as np
from jax import lax
from jax.experimental import pallas as pl
from jax.experimental.pallas import tpu as pltpu
from jax.sharding import PartitionSpec as P

LEVELS = 8
PLACES = 2
TRACERS = 3
FIELDS = PLACES * TRACERS
BLOCKS = 8
LANES = 128
BLOCK_COUNT = 20
CORNER_BLOCK = 18
END_BLOCK = 19
VMEM_LIMIT = 8 * 2**20
GROUP = 3

CORNER_OF = (0, 1, 1, 2, 3, 2, 0, 3)
OTHER_EDGE = (3, 1, 0, 2, 3, 1, 0, 2)
OTHER_END = (0, 0, 1, 1, 1, 1, 0, 0)
CORNER_A = (0, 1, 3, 4)
CORNER_B = (6, 2, 5, 7)

LINE_AT = 0
END_AT = 12
POINT_AT = 44
OCCUPIED_AT = 68
TABLE = 72


def f32(shape):
    return jax.ShapeDtypeStruct(shape, jnp.float32)


def lane_iota():
    return lax.broadcasted_iota(jnp.int32, (LEVELS, LANES), 1)


def take(block, index):
    return jnp.take_along_axis(block, index, axis=1, mode="promise_in_bounds")


def level_rows(k):
    return pl.ds(k, BLOCKS, stride=LEVELS)


def tile_rows(j):
    return pl.ds(j * LEVELS, LEVELS)


def column_solve(rhs, inverse, ratio, couple):
    partial = [[] for _ in rhs]
    for k in range(LEVELS):
        for values, done in zip(rhs, partial):
            current = values[k]
            if k > 0:
                current = current + couple[k - 1] * done[-1]
            done.append(current * inverse[k])
    found = [[done[-1]] for done in partial]
    for k in range(LEVELS - 2, -1, -1):
        for done, values in zip(partial, found):
            values.insert(0, done[k] + ratio[k] * values[0])
    return found


def column_factors(couples, depths):
    factors = [([], []) for _ in couples]
    for k in range(LEVELS):
        for couple, depth, (inverse, ratio) in zip(couples, depths, factors):
            pivot = 1.0 + couple[k]
            if k > 0:
                pivot = pivot + couple[k - 1] - couple[k - 1] * ratio[-1]
            inv = 1.0 / pivot
            if depth is not None:
                inv = jnp.where(depth > k, inv, 0.0)
            inverse.append(inv)
            ratio.append(couple[k] * inv)
    return factors


def beside(block, lane):
    b = lane % 32
    return jnp.where(b > 0, pltpu.roll(block, 1, 1), 0.0) + jnp.where(b < 31, pltpu.roll(block, LANES - 1, 1), 0.0)


def spread_matrix():
    matrix = np.zeros((3, LANES, 2, LANES), np.float32)
    own, beyond = range(2)
    sides = ((1, 0), (-1, 0), (0, 1), (0, -1))
    diagonals = ((1, 1), (1, -1), (-1, 1), (-1, -1))
    moves = [[(0, 0, 1.0)]]
    for offsets in (sides, diagonals):
        moves.append([(0, 0, -4.0)] + [(da, db, 1.0) for da, db in offsets])
    for source in range(3):
        for q in range(4):
            for b in range(32):
                for da, db, weight in moves[source]:
                    row, column = q + da, b + db
                    into = matrix[source, 32 * q + b]
                    if 0 <= column < 32:
                        if 0 <= row < 4:
                            into[own, 32 * row + column] += weight
                        else:
                            into[beyond, (0 if row > 0 else 96) + column] += weight
                    if column in (-1, 0, 31, 32):
                        kind = 8 if column in (0, 31) else 0
                        side = 0 if column > 0 else 4
                        into[beyond, 48 + 16 * (row // 4) + kind + side + row % 4] += weight
    return matrix.reshape(3 * LANES, 2 * LANES)


def split(values):
    high = values.astype(jnp.bfloat16)
    return high, (values - high.astype(jnp.float32)).astype(jnp.bfloat16)


def spread_products(z_ref, lat_ref, dia_ref, mat_ref, left_ref, product_ref):
    rows = BLOCKS * LEVELS
    right = jnp.concatenate([mat_ref[...], mat_ref[...]], axis=0)
    for start in range(0, FIELDS, GROUP):
        for f in range(start, start + GROUP):
            z = z_ref[f]
            p = f // TRACERS
            for i, values in enumerate((z, lat_ref[p] * z, dia_ref[p] * z)):
                high, low = split(values)
                left_ref[f * rows : (f + 1) * rows, i * LANES : (i + 1) * LANES] = high
                left_ref[f * rows : (f + 1) * rows, (3 + i) * LANES : (4 + i) * LANES] = low
        part = slice(start * rows, (start + GROUP) * rows)
        product_ref[part, :] = jnp.dot(left_ref[part, :], right, preferred_element_type=jnp.float32)


def product_blocks(product_ref, f, i):
    rows = BLOCKS * LEVELS
    return [
        product_ref[f * rows + j * LEVELS : f * rows + (j + 1) * LEVELS, i * LANES : (i + 1) * LANES] for j in range(BLOCKS)
    ]


def from_neighbours(blocks, beyond, first_row, last_row):
    sums = []
    for j in range(BLOCKS):
        total = blocks[j]
        if j > 0:
            total = total + jnp.where(first_row, beyond[j - 1], 0.0)
        if j < BLOCKS - 1:
            total = total + jnp.where(last_row, beyond[j + 1], 0.0)
        sums.append(total)
    return sums


def pack_lines(columns, lane):
    residue = lane % 32
    mixed = pltpu.roll(columns[0], 1, 1)
    for j in range(1, BLOCKS):
        mixed = jnp.where(residue // 2 == j, pltpu.roll(columns[j], 2 * j + 1, 1), mixed)
    q, j = residue % 4, residue // 4
    index = jnp.where(lane < 64, 32 * ((q + 1) % 4) + 2 * j, 32 * q + 2 * j + 1)
    return jnp.where(lane < 32, columns[0], jnp.where(lane >= 96, columns[-1], take(mixed, index)))


def pack_products(inner, beyond, lane):
    slot = lane // 16
    mixed = jnp.zeros_like(beyond[0])
    for j in range(BLOCKS):
        moved = pltpu.roll(beyond[j], (16 * j - 48) % LANES, 1) if j != 3 else beyond[j]
        mixed = mixed + jnp.where((slot >= j - 1) & (slot <= j + 1), moved, 0.0)
    index = 16 * (lane % 32 // 4) + lane % 4 + jnp.where(lane >= 64, 4, 0)
    low, high = lane < 32, lane >= 96
    ghosts = take(jnp.where(lane < 64, beyond[-1], beyond[0]), lane ^ 96)
    strips = jnp.where(low | high, ghosts, take(mixed, index))
    lines = jnp.where(low, inner[0], jnp.where(high, inner[-1], take(mixed, index + 8)))
    return strips, lines


def unpack_lines(outer, inner, lane):
    residue = lane % 32
    j, part, q = residue // 4, residue % 4, lane // 32
    index = jnp.where(part < 2, 32 + 4 * j + (q + 3) % 4, 64 + 4 * j + q)
    mixed = jnp.where((part == 0) | (part == 3), take(inner, index), take(outer, index))
    near = (residue < 2) | (residue >= 30)
    adds = [jnp.where(near, pltpu.roll(mixed, (LANES - 4 * j - 2) % LANES, 1), 0.0) for j in range(BLOCKS)]
    segment = lane // 32
    low = jnp.where(segment == 0, outer, jnp.where(segment == 1, pltpu.roll(inner, 32, 1), 0.0))
    high = jnp.where(segment == 3, outer, jnp.where(segment == 2, pltpu.roll(inner, LANES - 32, 1), 0.0))
    adds[0] = adds[0] + low
    adds[-1] = adds[-1] + high
    return adds


def pack_corners(line, lane):
    c = lane % 4
    return take(line, jnp.where(c == 0, 0, jnp.where(c == 1, 31, jnp.where(c == 2, 127, 96))))


def first_kernel(
    *refs,
):
    sources, refs = refs[:9], refs[9:]
    pay_ref, y_ref, fac_ref, dep_ref, lat_ref, dia_ref, mat_ref, home_ref, edge_ref, corner_ref = refs[:10]
    ver_ref, x_ref, z_ref, left_ref, product_ref, sems = refs[10:]
    targets = (dep_ref, ver_ref, x_ref, lat_ref, dia_ref, mat_ref, home_ref, edge_ref, corner_ref)
    moves = [pltpu.make_async_copy(source, target, sems.at[i]) for i, (source, target) in enumerate(zip(sources, targets))]
    for move in moves:
        move.start()
    lane = lane_iota()
    level = lax.broadcasted_iota(jnp.int32, (LEVELS, LANES), 0)
    group = lane // 32
    corners = jnp.zeros((LEVELS, LANES), jnp.float32)
    ends = jnp.zeros((LEVELS, LANES), jnp.float32)
    end_edge = lane % 8 // 2
    end_lane = 32 * (end_edge ^ (end_edge // 2)) + 31 * (lane % 2)
    moves[0].wait()
    moves[1].wait()
    depth = [dep_ref[pl.ds(p, BLOCKS, stride=PLACES), :] for p in range(PLACES)]
    couple = [
        [jnp.where(depth[p] > k + 1, ver_ref[p, level_rows(k), :], 0.0) for k in range(LEVELS - 1)]
        + [jnp.zeros((BLOCKS, LANES), jnp.float32)]
        for p in range(PLACES)
    ]
    factors = column_factors(couple, depth)
    for p in range(PLACES):
        for k in range(LEVELS):
            fac_ref[p, 0, k] = factors[p][0][k]
            fac_ref[p, 1, k] = factors[p][1][k]
            fac_ref[p, 2, k] = couple[p][k]
    moves[2].wait()
    for p in range(PLACES):
        fields = [p * TRACERS + t for t in range(TRACERS)]
        found = column_solve(
            [[x_ref[f, level_rows(k), :] for k in range(LEVELS)] for f in fields], *factors[p], couple[p]
        )
        for k in range(LEVELS):
            for f, values in zip(fields, found):
                z_ref[f, level_rows(k), :] = values[k]
    for move in moves[3:]:
        move.wait()
    spread_products(z_ref, lat_ref, dia_ref, mat_ref, left_ref, product_ref)
    for p in range(PLACES):
        wet_lat, wet_dia, link = [], [], []
        for j in range(BLOCKS):
            row = dep_ref[j * PLACES + p : j * PLACES + p + 1, :]
            wet_lat.append(jnp.where(row > level, lat_ref[p, tile_rows(j), :], 0.0))
            wet_dia.append(jnp.where(row > level, dia_ref[p, tile_rows(j), :], 0.0))
            link.append(jnp.where((row > level + 1) & (level < LEVELS - 1), ver_ref[p, tile_rows(j), :], 0.0))
        coefs = [pack_lines(blocks, lane) for blocks in (link, wet_lat, wet_dia)]
        for i in range(3):
            pay_ref[12 + p * 3 + i] = coefs[i]
        link_corners = pack_corners(coefs[0], lane)
        dia_corners = pack_corners(coefs[2], lane)
        for t in range(TRACERS):
            f = p * TRACERS + t
            own, beyond = (product_blocks(product_ref, f, i) for i in range(2))
            inner = from_neighbours(own, beyond, lane < 32, lane >= 96)
            for j in range(BLOCKS):
                y_ref[f, tile_rows(j), :] = inner[j]
            strips, lines = pack_products(inner, beyond, lane)
            pay_ref[f] = strips
            pay_ref[FIELDS + f] = lines
            across = jnp.where(
                lane < 64,
                dia_ref[p, tile_rows(0), :] * z_ref[f, tile_rows(0), :],
                dia_ref[p, tile_rows(BLOCKS - 1), :] * z_ref[f, tile_rows(BLOCKS - 1), :],
            )
            cells = jnp.where(
                group == 0,
                pack_corners(across, lane),
                jnp.where(group == 1, pack_corners(lines, lane), jnp.where(group == 2, link_corners, dia_corners)),
            )
            corners = jnp.where(lane % 32 // 4 == p * 4 + t, cells, corners)
            ends = jnp.where(lane // 8 == p * 4 + t, take(strips, end_lane), ends)
    pay_ref[CORNER_BLOCK] = corners
    pay_ref[END_BLOCK] = ends


def pick(values, index, bits):
    packed = 0
    for i, value in enumerate(values):
        packed |= value << (bits * i)
    return lax.shift_right_logical(jnp.int32(packed), index * bits) & (2**bits - 1)


def window_kernel(
    home_ref, edge_ref, corner_ref, y_ref, fac_ref, lat_ref, dia_ref, dep_ref, mat_ref, pay_ref,
    out_ref, part_ref, own_ref, z_ref, link_ref, left_ref, product_ref,
):
    row = lax.axis_index("row")
    col = lax.axis_index("col")
    col_count = lax.axis_size("col")
    device = row * col_count + col

    def scan(t, found):
        here = home_ref[0, t]
        return tuple(jnp.where(here == device * PLACES + p, t, found[p]) for p in range(PLACES))

    tile_count = home_ref.shape[1]
    unroll = 8 if tile_count % 8 == 0 else 1

    def scan_some(i, found):
        for s in range(unroll):
            found = scan(i * unroll + s, found)
        return found

    tiles = lax.fori_loop(0, tile_count // unroll, scan_some, tuple(jnp.int32(-1) for _ in range(PLACES)))

    def block_of(tile):
        place = home_ref[0, tile]
        other = lax.shift_right_logical(place, 1)
        slot = (other ^ device) & (2 * col_count - 1)
        return slot * BLOCK_COUNT, place & 1

    def edge_of(tile, edge):
        code = edge_ref[edge, tile]
        return lax.shift_right_logical(code, 3), lax.shift_right_logical(code, 1) & 3, code & 1

    def strip_end(tile, edge_end):
        other, f, r = edge_of(tile, lax.shift_right_logical(edge_end, 1))
        base, place = block_of(other)
        return base + END_BLOCK, place * 32 + f * 2 + ((edge_end & 1) ^ r)

    def point(tile, corner):
        code = corner_ref[corner, tile]
        safe = jnp.maximum(code, 0)
        other, g = lax.shift_right_logical(safe, 2), safe & 3
        base, place = block_of(other)
        return base + CORNER_BLOCK, jnp.where(code >= 0, place * 16 + g, -1), other, g

    for p in range(PLACES):
        at = p * TABLE
        tile = jnp.maximum(tiles[p], 0)
        out_ref[at + OCCUPIED_AT] = jnp.where(tiles[p] >= 0, 1, 0)
        for e in range(4):
            other, f, r = edge_of(tile, e)
            base, place = block_of(other)
            out_ref[at + LINE_AT + 3 * e] = base + place * 3
            out_ref[at + LINE_AT + 3 * e + 1] = 32 * (f ^ lax.shift_right_logical(f, 1)) + 31 * r
            out_ref[at + LINE_AT + 3 * e + 2] = 1 - 2 * r
            for end in range(2):
                index = f * 2 + (end ^ r)
                strip_row, strip_lane = strip_end(other, pick(OTHER_EDGE, index, 2) * 2 + pick(OTHER_END, index, 1))
                point_row, point_lane, _, _ = point(other, pick(CORNER_OF, index, 2))
                slot = at + END_AT + 4 * (2 * e + end)
                out_ref[slot] = strip_row
                out_ref[slot + 1] = strip_lane
                out_ref[slot + 2] = point_row
                out_ref[slot + 3] = point_lane
        for c in range(4):
            point_row, point_lane, other, g = point(tile, c)
            slot = at + POINT_AT + 6 * c
            out_ref[slot] = point_row
            out_ref[slot + 1] = point_lane
            row_a, lane_a = strip_end(other, pick(CORNER_A, g, 3))
            row_b, lane_b = strip_end(other, pick(CORNER_B, g, 3))
            out_ref[slot + 2] = row_a
            out_ref[slot + 3] = lane_a
            out_ref[slot + 4] = row_b
            out_ref[slot + 5] = lane_b

    lane = lane_iota()
    level = lax.broadcasted_iota(jnp.int32, (LEVELS, LANES), 0)
    for p in range(PLACES):
        fields = [p * TRACERS + t for t in range(TRACERS)]
        inverse = [fac_ref[p, 0, k] for k in range(LEVELS)]
        ratio = [fac_ref[p, 1, k] for k in range(LEVELS)]
        couple = [fac_ref[p, 2, k] for k in range(LEVELS)]
        found = column_solve(
            [[y_ref[f, level_rows(k), :] for k in range(LEVELS)] for f in fields], inverse, ratio, couple
        )
        for k in range(LEVELS):
            for f, values in zip(fields, found):
                z_ref[f, level_rows(k), :] = values[k]
    spread_products(z_ref, lat_ref, dia_ref, mat_ref, left_ref, product_ref)
    for f in range(FIELDS):
        own, beyond = (product_blocks(product_ref, f, i) for i in range(2))
        inner = from_neighbours(own, beyond, lane < 32, lane >= 96)
        for j in range(BLOCKS):
            part_ref[f, tile_rows(j), :] = jnp.where(tiles[f // TRACERS] >= 0, inner[j], 0.0)

    wet = []
    for p in range(PLACES):
        rows = [dep_ref[j * PLACES + p : j * PLACES + p + 1, :] for j in range(BLOCKS)]
        masks = [jnp.where(row > level, 1.0, 0.0) for row in rows]
        wet.append(pack_lines(masks, lane))
    for f in range(LEVELS):
        link_ref[0, tile_rows(f), :] = pay_ref[12 + f // TRACERS % PLACES * 3]
        link_ref[1, tile_rows(f), :] = wet[f // TRACERS % PLACES]
    couple = [link_ref[0, level_rows(k), :] for k in range(LEVELS)]
    ((inverse, ratio),) = column_factors([couple], [None])
    for k in range(LEVELS):
        mask = link_ref[1, level_rows(k), :]
        own_ref[0, k] = inverse[k] * mask
        own_ref[1, k] = ratio[k]
        own_ref[2, k] = couple[k]


def second_kernel(tab_ref, part_ref, own_ref, *refs):
    pay_refs = refs[:-5]
    out_ref, all_ref, own_line_ref, line_ref, link_ref = refs[-5:]
    lane = lane_iota()
    zero = jnp.zeros((LEVELS, LANES), jnp.float32)
    for slot, ref in enumerate(pay_refs):
        for i in range(BLOCK_COUNT):
            all_ref[slot * BLOCK_COUNT + i] = ref[i]
    segment, position = lane // 32, lane % 32
    edge = segment ^ (segment // 2)
    line_end = (position == 0) | (position == 31)

    strips, lines, line_lat, line_dia = [], [], [], []
    for p in range(PLACES):
        at = p * TABLE + LINE_AT
        rows = [tab_ref[at + 3 * e] for e in range(4)]
        places = [tab_ref[at + 3 * e + 1] for e in range(4)]
        signs = [tab_ref[at + 3 * e + 2] for e in range(4)]
        index = zero.astype(jnp.int32)
        for e in range(4):
            index = jnp.where(edge == e, places[e] + signs[e] * position, index)

        def fetch(block):
            found = take(all_ref[rows[0] + block], index)
            for e in range(1, 4):
                found = jnp.where(edge == e, take(all_ref[rows[e] + block], index), found)
            return found

        for t in range(TRACERS):
            strips.append(fetch(t))
            lines.append(fetch(FIELDS + t))
        link = fetch(12)
        for t in range(TRACERS):
            link_ref[tile_rows(p * TRACERS + t), :] = link
        line_lat.append(fetch(13))
        line_dia.append(fetch(14))

    ends = zero
    tracer = lane % 32 // 8
    for p in range(PLACES):
        for i in range(8):
            at = p * TABLE + END_AT + 4 * i
            here = (segment == p) & (lane % 8 == i)
            strip = take(all_ref[tab_ref[at]], tab_ref[at + 1] + tracer * 8)
            point_lane = tab_ref[at + 3]
            point = take(all_ref[tab_ref[at + 2]], jnp.maximum(point_lane, 0) + tracer * 4)
            ends = jnp.where(here, strip + jnp.where(point_lane >= 0, point, 0.0), ends)

    cells = zero
    cell_adds = zero
    cell_tracer = lane % 16 // 4
    for p in range(PLACES):
        for c in range(4):
            at = p * TABLE + POINT_AT + 6 * c
            here = (position // 16 == p) & (lane % 4 == c)
            point_lane = tab_ref[at + 1]
            cell = take(all_ref[tab_ref[at]], jnp.maximum(point_lane, 0) + 32 * segment + 4 * cell_tracer)
            cells = jnp.where(here & (point_lane >= 0), cell, cells)
            strip_a = take(all_ref[tab_ref[at + 2]], tab_ref[at + 3] + cell_tracer * 8)
            strip_b = take(all_ref[tab_ref[at + 4]], tab_ref[at + 5] + cell_tracer * 8)
            cell_adds = jnp.where(here, strip_a + strip_b, cell_adds)
    cell_adds = cell_adds + pltpu.roll(all_ref[CORNER_BLOCK], 32, 1)

    corner_of_lane = jnp.where(segment == 0, jnp.where(position == 31, 1, 0), jnp.where(position == 31, 2, 3))
    at_corner = line_end & ((segment == 0) | (segment == 3))
    for f in range(FIELDS):
        p, t = f // TRACERS, f % TRACERS
        spread = take(ends, p * 32 + t * 8 + edge * 2 + jnp.where(position == 31, 1, 0))
        line_ref[tile_rows(f), :] = lines[f] + all_ref[f] + jnp.where(line_end, spread, 0.0)
        points = take(cells, p * 16 + t * 4 + corner_of_lane)
        own_line_ref[tile_rows(f), :] = strips[f] + jnp.where(at_corner, points, 0.0)
    line_ref[tile_rows(FIELDS), :] = cells + cell_adds
    line_ref[tile_rows(FIELDS + 1), :] = zero
    own_line_ref[tile_rows(FIELDS), :] = zero
    own_line_ref[tile_rows(FIELDS + 1), :] = zero
    link_ref[tile_rows(FIELDS), :] = pltpu.roll(cells, LANES - 32, 1)
    link_ref[tile_rows(FIELDS + 1), :] = zero
    couple = [link_ref[level_rows(k), :] for k in range(LEVELS - 1)] + [zero]
    ((inverse, ratio),) = column_factors([couple], [None])
    (own_found,) = column_solve(
        [[own_line_ref[level_rows(k), :] for k in range(LEVELS)]],
        [own_ref[0, k] for k in range(LEVELS)],
        [own_ref[1, k] for k in range(LEVELS)],
        [own_ref[2, k] for k in range(LEVELS)],
    )
    (found,) = column_solve([[line_ref[level_rows(k), :] for k in range(LEVELS)]], inverse, ratio, couple)
    for k in range(LEVELS):
        own_line_ref[level_rows(k), :] = own_found[k]
        line_ref[level_rows(k), :] = found[k]
    points = line_ref[tile_rows(FIELDS), :] * pltpu.roll(cells, LANES - 64, 1)

    for p in range(PLACES):
        occupied = tab_ref[p * TABLE + OCCUPIED_AT] > 0
        own_lat, own_dia = all_ref[13 + 3 * p], all_ref[14 + 3 * p]
        for t in range(TRACERS):
            f = p * TRACERS + t
            line = line_ref[tile_rows(f), :]
            outer = line_lat[p] * line + beside(line_dia[p] * line, lane)
            outer = outer + jnp.where(at_corner, take(points, 32 + p * 16 + t * 4 + corner_of_lane), 0.0)
            line = own_line_ref[tile_rows(f), :]
            along, across = own_lat * line, own_dia * line
            outer = outer + line - 4.0 * (along + across) + beside(along, lane)
            inner = along + beside(across, lane)
            adds = unpack_lines(jnp.where(occupied, outer, 0.0), jnp.where(occupied, inner, 0.0), lane)
            for j in range(BLOCKS):
                out_ref[f, tile_rows(j), :] = part_ref[f, tile_rows(j), :] + adds[j]


def swap(value, axes, row_count, col_count, row_bit, col_bits):
    pairs = []
    for i in range(row_count):
        for j in range(col_count):
            pairs.append((i * col_count + j, (i ^ row_bit) * col_count + (j ^ col_bits)))
    return lax.ppermute(value, axes, pairs)


def tiled(array, lead):
    blocks = array.reshape(lead + (-1, BLOCKS, LANES))
    rows = blocks.shape[-3]
    order = tuple(range(len(lead))) + (len(lead) + 1, len(lead), len(lead) + 2)
    return blocks.transpose(order).reshape(lead + (BLOCKS * rows, LANES))


def on_device(adjoint_out, lateral, diagonal, vertical, depth, tile_home, edge_link, corner_link):
    row_count, col_count = lax.axis_size("row"), lax.axis_size("col")
    axes = ("row", "col")
    vmem = pl.BlockSpec(memory_space=pltpu.VMEM)
    smem = pl.BlockSpec(memory_space=pltpu.SMEM)
    params = pltpu.CompilerParams(vmem_limit_bytes=VMEM_LIMIT)
    rows = BLOCKS * LEVELS
    x = tiled(adjoint_out, (FIELDS,))
    lat = tiled(lateral, (PLACES,))
    dia = tiled(diagonal, (PLACES,))
    ver = tiled(vertical, (PLACES,))
    dep = tiled(depth, ())
    hbm = pl.BlockSpec(memory_space=pltpu.HBM)
    home, edges, corners = tile_home.reshape(1, -1), edge_link.T, corner_link.T
    matrix = jnp.asarray(spread_matrix(), jnp.bfloat16)
    sources = (dep, ver, x, lat, dia, matrix, home, edges, corners)
    payload, y, fac, dep, lat, dia, matrix, home, edges, corners = pl.pallas_call(
        first_kernel,
        out_shape=(
            f32((BLOCK_COUNT, LEVELS, LANES)),
            f32((FIELDS, rows, LANES)),
            f32((PLACES, 3, LEVELS, BLOCKS, LANES)),
        )
        + tuple(jax.ShapeDtypeStruct(value.shape, value.dtype) for value in (dep, lat, dia, matrix))
        + tuple(pltpu.SMEM(value.shape, value.dtype) for value in (home, edges, corners)),
        in_specs=[hbm] * len(sources),
        out_specs=(vmem,) * 7 + (smem,) * 3,
        scratch_shapes=[
            pltpu.VMEM((PLACES, rows, LANES), jnp.float32),
            pltpu.VMEM((FIELDS, rows, LANES), jnp.float32),
            pltpu.VMEM((FIELDS, rows, LANES), jnp.float32),
            pltpu.VMEM((FIELDS * rows, 6 * LANES), jnp.bfloat16),
            pltpu.VMEM((FIELDS * rows, 2 * LANES), jnp.float32),
            pltpu.SemaphoreType.DMA((len(sources),)),
        ],
        compiler_params=params,
        name="first",
    )(*(pltpu.with_memory_space_constraint(value, pltpu.HBM) for value in sources))
    near = [swap(payload, axes, row_count, col_count, 0, m) for m in range(1, col_count)]
    table, part, own = pl.pallas_call(
        window_kernel,
        out_shape=(
            pltpu.SMEM((PLACES * TABLE,), jnp.int32),
            f32((FIELDS, rows, LANES)),
            f32((3, LEVELS, LEVELS, LANES)),
        ),
        in_specs=[smem] * 3 + [vmem] * 7,
        out_specs=(smem, vmem, vmem),
        scratch_shapes=[
            pltpu.VMEM((FIELDS, rows, LANES), jnp.float32),
            pltpu.VMEM((2, rows, LANES), jnp.float32),
            pltpu.VMEM((FIELDS * rows, 6 * LANES), jnp.bfloat16),
            pltpu.VMEM((FIELDS * rows, 2 * LANES), jnp.float32),
        ],
        compiler_params=params,
        name="window",
    )(home, edges, corners, y, fac, lat, dia, dep, matrix, payload)
    near = [lax.optimization_barrier((value, table))[0] for value in near]
    twin = swap(lax.optimization_barrier((payload, table))[0], axes, row_count, col_count, 1, 0)
    far = [swap(value, axes, row_count, col_count, 1, 0) for value in near]
    payloads = [payload] + near + [twin] + far
    out = pl.pallas_call(
        second_kernel,
        out_shape=f32((FIELDS, rows, LANES)),
        in_specs=[smem] + [vmem] * (2 + len(payloads)),
        out_specs=vmem,
        scratch_shapes=[
            pltpu.VMEM((len(payloads) * BLOCK_COUNT, LEVELS, LANES), jnp.float32),
            pltpu.VMEM((rows, LANES), jnp.float32),
            pltpu.VMEM((rows, LANES), jnp.float32),
            pltpu.VMEM((rows, LANES), jnp.float32),
        ],
        compiler_params=pltpu.CompilerParams(vmem_limit_bytes=VMEM_LIMIT + 2 * len(payloads) * BLOCK_COUNT * 4096),
        name="second",
    )(table, part, own, *payloads)
    out = out.reshape(FIELDS, BLOCKS, LEVELS, LANES).transpose(0, 2, 1, 3)
    return out.reshape(adjoint_out.shape)


def solution(mesh):
    return jax.shard_map(
        on_device,
        mesh=mesh,
        in_specs=(
            P("row", "col", None, None, None, None),
            P("row", "col", None, None, None),
            P("row", "col", None, None, None),
            P("row", "col", None, None, None),
            P("row", "col", None, None),
            P(),
            P(),
            P(),
        ),
        out_specs=P("row", "col", None, None, None, None),
        check_vma=False,
    )
```

```python
import functools

import jax
import jax.numpy as jnp
import numpy as np
from jax import lax
from jax.experimental import pallas as pl
from jax.experimental.pallas import tpu as pltpu
from jax.sharding import PartitionSpec as P

LEVELS = 8
PLACES = 2
TRACERS = 3
FIELDS = PLACES * TRACERS
BLOCKS = 8
LANES = 128
BLOCK_COUNT = 20
CORNER_BLOCK = 18
END_BLOCK = 19
VMEM_LIMIT = 8 * 2**20
GROUP = 3

CORNER_OF = (0, 1, 1, 2, 3, 2, 0, 3)
OTHER_EDGE = (3, 1, 0, 2, 3, 1, 0, 2)
OTHER_END = (0, 0, 1, 1, 1, 1, 0, 0)
CORNER_A = (0, 1, 3, 4)
CORNER_B = (6, 2, 5, 7)

PICKED_ENDS = 18
PICKED_CELLS = 19
PICKED_ADDS = 20
PICKED_COUNT = 21

LINE_AT = 0
END_AT = 12
POINT_AT = 44
OCCUPIED_AT = 68
TABLE = 72


def f32(shape):
    return jax.ShapeDtypeStruct(shape, jnp.float32)


def lane_iota():
    return lax.broadcasted_iota(jnp.int32, (LEVELS, LANES), 1)


def take(block, index):
    return jnp.take_along_axis(block, index, axis=1, mode="promise_in_bounds")


def level_rows(k):
    return pl.ds(k, BLOCKS, stride=LEVELS)


def tile_rows(j):
    return pl.ds(j * LEVELS, LEVELS)


def column_solve(rhs, inverse, ratio, couple):
    partial = [[] for _ in rhs]
    for k in range(LEVELS):
        for values, done in zip(rhs, partial):
            current = values[k]
            if k > 0:
                current = current + couple[k - 1] * done[-1]
            done.append(current * inverse[k])
    found = [[done[-1]] for done in partial]
    for k in range(LEVELS - 2, -1, -1):
        for done, values in zip(partial, found):
            values.insert(0, done[k] + ratio[k] * values[0])
    return found


def column_factors(couples, depths):
    factors = [([], []) for _ in couples]
    for k in range(LEVELS):
        for couple, depth, (inverse, ratio) in zip(couples, depths, factors):
            pivot = 1.0 + couple[k]
            if k > 0:
                pivot = pivot + couple[k - 1] - couple[k - 1] * ratio[-1]
            inv = 1.0 / pivot
            if depth is not None:
                inv = jnp.where(depth > k, inv, 0.0)
            inverse.append(inv)
            ratio.append(couple[k] * inv)
    return factors


def beside(block, lane):
    b = lane % 32
    return jnp.where(b > 0, pltpu.roll(block, 1, 1), 0.0) + jnp.where(b < 31, pltpu.roll(block, LANES - 1, 1), 0.0)


def spread_matrix():
    matrix = np.zeros((3, LANES, 2, LANES), np.float32)
    own, beyond = range(2)
    sides = ((1, 0), (-1, 0), (0, 1), (0, -1))
    diagonals = ((1, 1), (1, -1), (-1, 1), (-1, -1))
    moves = [[(0, 0, 1.0)]]
    for offsets in (sides, diagonals):
        moves.append([(0, 0, -4.0)] + [(da, db, 1.0) for da, db in offsets])
    for source in range(3):
        for q in range(4):
            for b in range(32):
                for da, db, weight in moves[source]:
                    row, column = q + da, b + db
                    into = matrix[source, 32 * q + b]
                    if 0 <= column < 32:
                        if 0 <= row < 4:
                            into[own, 32 * row + column] += weight
                        else:
                            into[beyond, (0 if row > 0 else 96) + column] += weight
                    if column in (-1, 0, 31, 32):
                        kind = 8 if column in (0, 31) else 0
                        side = 0 if column > 0 else 4
                        into[beyond, 48 + 16 * (row // 4) + kind + side + row % 4] += weight
    return matrix.reshape(3 * LANES, 2 * LANES)


def split(values):
    high = values.astype(jnp.bfloat16)
    return high, (values - high.astype(jnp.float32)).astype(jnp.bfloat16)


def spread_products(z_ref, lat_ref, dia_ref, mat_ref, left_ref, product_ref):
    rows = BLOCKS * LEVELS
    right = jnp.concatenate([mat_ref[...], mat_ref[...]], axis=0)
    for start in range(0, FIELDS, GROUP):
        for f in range(start, start + GROUP):
            z = z_ref[f]
            p = f // TRACERS
            for i, values in enumerate((z, lat_ref[p] * z, dia_ref[p] * z)):
                high, low = split(values)
                left_ref[f * rows : (f + 1) * rows, i * LANES : (i + 1) * LANES] = high
                left_ref[f * rows : (f + 1) * rows, (3 + i) * LANES : (4 + i) * LANES] = low
        part = slice(start * rows, (start + GROUP) * rows)
        product_ref[part, :] = jnp.dot(left_ref[part, :], right, preferred_element_type=jnp.float32)


def product_blocks(product_ref, f, i):
    rows = BLOCKS * LEVELS
    return [
        product_ref[f * rows + j * LEVELS : f * rows + (j + 1) * LEVELS, i * LANES : (i + 1) * LANES] for j in range(BLOCKS)
    ]


def from_neighbours(blocks, beyond, first_row, last_row):
    sums = []
    for j in range(BLOCKS):
        total = blocks[j]
        if j > 0:
            total = total + jnp.where(first_row, beyond[j - 1], 0.0)
        if j < BLOCKS - 1:
            total = total + jnp.where(last_row, beyond[j + 1], 0.0)
        sums.append(total)
    return sums


def pack_lines(columns, lane):
    residue = lane % 32
    mixed = pltpu.roll(columns[0], 1, 1)
    for j in range(1, BLOCKS):
        mixed = jnp.where(residue // 2 == j, pltpu.roll(columns[j], 2 * j + 1, 1), mixed)
    q, j = residue % 4, residue // 4
    index = jnp.where(lane < 64, 32 * ((q + 1) % 4) + 2 * j, 32 * q + 2 * j + 1)
    return jnp.where(lane < 32, columns[0], jnp.where(lane >= 96, columns[-1], take(mixed, index)))


def pack_products(inner, beyond, lane):
    slot = lane // 16
    mixed = jnp.zeros_like(beyond[0])
    for j in range(BLOCKS):
        moved = pltpu.roll(beyond[j], (16 * j - 48) % LANES, 1) if j != 3 else beyond[j]
        mixed = mixed + jnp.where((slot >= j - 1) & (slot <= j + 1), moved, 0.0)
    index = 16 * (lane % 32 // 4) + lane % 4 + jnp.where(lane >= 64, 4, 0)
    low, high = lane < 32, lane >= 96
    ghosts = take(jnp.where(lane < 64, beyond[-1], beyond[0]), lane ^ 96)
    strips = jnp.where(low | high, ghosts, take(mixed, index))
    lines = jnp.where(low, inner[0], jnp.where(high, inner[-1], take(mixed, index + 8)))
    return strips, lines


def unpack_lines(outer, inner, lane):
    residue = lane % 32
    j, part, q = residue // 4, residue % 4, lane // 32
    index = jnp.where(part < 2, 32 + 4 * j + (q + 3) % 4, 64 + 4 * j + q)
    mixed = jnp.where((part == 0) | (part == 3), take(inner, index), take(outer, index))
    near = (residue < 2) | (residue >= 30)
    adds = [jnp.where(near, pltpu.roll(mixed, (LANES - 4 * j - 2) % LANES, 1), 0.0) for j in range(BLOCKS)]
    segment = lane // 32
    low = jnp.where(segment == 0, outer, jnp.where(segment == 1, pltpu.roll(inner, 32, 1), 0.0))
    high = jnp.where(segment == 3, outer, jnp.where(segment == 2, pltpu.roll(inner, LANES - 32, 1), 0.0))
    adds[0] = adds[0] + low
    adds[-1] = adds[-1] + high
    return adds


def pack_corners(line, lane):
    c = lane % 4
    return take(line, jnp.where(c == 0, 0, jnp.where(c == 1, 31, jnp.where(c == 2, 127, 96))))


def first_kernel(
    *refs,
):
    sources, refs = refs[:9], refs[9:]
    pay_ref, y_ref, fac_ref, dep_ref, lat_ref, dia_ref, mat_ref, home_ref, edge_ref, corner_ref = refs[:10]
    ver_ref, x_ref, z_ref, left_ref, product_ref, sems = refs[10:]
    targets = (dep_ref, ver_ref, x_ref, lat_ref, dia_ref, mat_ref, home_ref, edge_ref, corner_ref)
    moves = [pltpu.make_async_copy(source, target, sems.at[i]) for i, (source, target) in enumerate(zip(sources, targets))]
    for move in moves:
        move.start()
    lane = lane_iota()
    level = lax.broadcasted_iota(jnp.int32, (LEVELS, LANES), 0)
    group = lane // 32
    corners = jnp.zeros((LEVELS, LANES), jnp.float32)
    ends = jnp.zeros((LEVELS, LANES), jnp.float32)
    end_edge = lane % 8 // 2
    end_lane = 32 * (end_edge ^ (end_edge // 2)) + 31 * (lane % 2)
    moves[0].wait()
    moves[1].wait()
    depth = [dep_ref[pl.ds(p, BLOCKS, stride=PLACES), :] for p in range(PLACES)]
    couple = [
        [jnp.where(depth[p] > k + 1, ver_ref[p, level_rows(k), :], 0.0) for k in range(LEVELS - 1)]
        + [jnp.zeros((BLOCKS, LANES), jnp.float32)]
        for p in range(PLACES)
    ]
    factors = column_factors(couple, depth)
    for p in range(PLACES):
        for k in range(LEVELS):
            fac_ref[p, 0, k] = factors[p][0][k]
            fac_ref[p, 1, k] = factors[p][1][k]
            fac_ref[p, 2, k] = couple[p][k]
    moves[2].wait()
    for p in range(PLACES):
        fields = [p * TRACERS + t for t in range(TRACERS)]
        found = column_solve(
            [[x_ref[f, level_rows(k), :] for k in range(LEVELS)] for f in fields], *factors[p], couple[p]
        )
        for k in range(LEVELS):
            for f, values in zip(fields, found):
                z_ref[f, level_rows(k), :] = values[k]
    for move in moves[3:6]:
        move.wait()
    spread_products(z_ref, lat_ref, dia_ref, mat_ref, left_ref, product_ref)
    for p in range(PLACES):
        wet_lat, wet_dia, link = [], [], []
        for j in range(BLOCKS):
            row = dep_ref[j * PLACES + p : j * PLACES + p + 1, :]
            wet_lat.append(jnp.where(row > level, lat_ref[p, tile_rows(j), :], 0.0))
            wet_dia.append(jnp.where(row > level, dia_ref[p, tile_rows(j), :], 0.0))
            link.append(jnp.where((row > level + 1) & (level < LEVELS - 1), ver_ref[p, tile_rows(j), :], 0.0))
        coefs = [pack_lines(blocks, lane) for blocks in (link, wet_lat, wet_dia)]
        for i in range(3):
            pay_ref[12 + p * 3 + i] = coefs[i]
        link_corners = pack_corners(coefs[0], lane)
        dia_corners = pack_corners(coefs[2], lane)
        for t in range(TRACERS):
            f = p * TRACERS + t
            own, beyond = (product_blocks(product_ref, f, i) for i in range(2))
            inner = from_neighbours(own, beyond, lane < 32, lane >= 96)
            for j in range(BLOCKS):
                y_ref[f, tile_rows(j), :] = inner[j]
            strips, lines = pack_products(inner, beyond, lane)
            pay_ref[f] = strips
            pay_ref[FIELDS + f] = lines
            across = jnp.where(
                lane < 64,
                dia_ref[p, tile_rows(0), :] * z_ref[f, tile_rows(0), :],
                dia_ref[p, tile_rows(BLOCKS - 1), :] * z_ref[f, tile_rows(BLOCKS - 1), :],
            )
            cells = jnp.where(
                group == 0,
                pack_corners(across, lane),
                jnp.where(group == 1, pack_corners(lines, lane), jnp.where(group == 2, link_corners, dia_corners)),
            )
            corners = jnp.where(lane % 32 // 4 == p * 4 + t, cells, corners)
            ends = jnp.where(lane // 8 == p * 4 + t, take(strips, end_lane), ends)
    pay_ref[CORNER_BLOCK] = corners
    pay_ref[END_BLOCK] = ends
    for move in moves[6:]:
        move.wait()


def pick(values, index, bits):
    packed = 0
    for i, value in enumerate(values):
        packed |= value << (bits * i)
    return lax.shift_right_logical(jnp.int32(packed), index * bits) & (2**bits - 1)


def window_kernel(
    home_ref, edge_ref, corner_ref, y_ref, fac_ref, lat_ref, dia_ref, dep_ref, mat_ref, pay_ref,
    out_ref, part_ref, own_ref, z_ref, link_ref, left_ref, product_ref,
):
    row = lax.axis_index("row")
    col = lax.axis_index("col")
    col_count = lax.axis_size("col")
    device = row * col_count + col

    first_places = [device * PLACES, (device ^ col_count) * PLACES]

    def scan(t, found):
        here = home_ref[0, t]
        return tuple(
            jnp.where(here == first_places[i // PLACES] + i % PLACES, t, tile) for i, tile in enumerate(found)
        )

    tile_count = home_ref.shape[1]
    unroll = 8 if tile_count % 8 == 0 else 1

    def scan_some(i, found):
        for s in range(unroll):
            found = scan(i * unroll + s, found)
        return found

    tiles = lax.fori_loop(
        0, tile_count // unroll, scan_some, tuple(jnp.int32(-1) for _ in range(2 * PLACES))
    )

    def block_of(tile):
        place = home_ref[0, tile]
        slot = (lax.shift_right_logical(place, 1) ^ device) & (2 * col_count - 1)
        return jnp.where(slot < col_count, slot * BLOCK_COUNT, -BLOCK_COUNT), place & 1

    def edge_of(tile, edge):
        code = edge_ref[edge, tile]
        return lax.shift_right_logical(code, 3), lax.shift_right_logical(code, 1) & 3, code & 1

    def strip_end(tile, edge_end):
        other, f, r = edge_of(tile, lax.shift_right_logical(edge_end, 1))
        base, place = block_of(other)
        return base + END_BLOCK, place * 32 + f * 2 + ((edge_end & 1) ^ r)

    def point(tile, corner):
        code = corner_ref[corner, tile]
        safe = jnp.maximum(code, 0)
        other, g = lax.shift_right_logical(safe, 2), safe & 3
        base, place = block_of(other)
        return jnp.where(code >= 0, base + CORNER_BLOCK, -1), place * 16 + g, other, g

    for i in range(2 * PLACES):
        at = i * TABLE
        tile = jnp.maximum(tiles[i], 0)
        out_ref[at + OCCUPIED_AT] = jnp.where(tiles[i] >= 0, 1, 0)
        for e in range(4):
            other, f, r = edge_of(tile, e)
            base, place = block_of(other)
            out_ref[at + LINE_AT + 3 * e] = base + place * 3
            out_ref[at + LINE_AT + 3 * e + 1] = 32 * (f ^ lax.shift_right_logical(f, 1)) + 31 * r
            out_ref[at + LINE_AT + 3 * e + 2] = 1 - 2 * r
            for end in range(2):
                index = f * 2 + (end ^ r)
                strip_row, strip_lane = strip_end(other, pick(OTHER_EDGE, index, 2) * 2 + pick(OTHER_END, index, 1))
                point_row, point_lane, _, _ = point(other, pick(CORNER_OF, index, 2))
                slot = at + END_AT + 4 * (2 * e + end)
                out_ref[slot] = strip_row
                out_ref[slot + 1] = strip_lane
                out_ref[slot + 2] = point_row
                out_ref[slot + 3] = point_lane
        for c in range(4):
            point_row, point_lane, other, g = point(tile, c)
            slot = at + POINT_AT + 6 * c
            out_ref[slot] = point_row
            out_ref[slot + 1] = point_lane
            row_a, lane_a = strip_end(other, pick(CORNER_A, g, 3))
            row_b, lane_b = strip_end(other, pick(CORNER_B, g, 3))
            out_ref[slot + 2] = row_a
            out_ref[slot + 3] = lane_a
            out_ref[slot + 4] = row_b
            out_ref[slot + 5] = lane_b

    lane = lane_iota()
    level = lax.broadcasted_iota(jnp.int32, (LEVELS, LANES), 0)
    for p in range(PLACES):
        fields = [p * TRACERS + t for t in range(TRACERS)]
        inverse = [fac_ref[p, 0, k] for k in range(LEVELS)]
        ratio = [fac_ref[p, 1, k] for k in range(LEVELS)]
        couple = [fac_ref[p, 2, k] for k in range(LEVELS)]
        found = column_solve(
            [[y_ref[f, level_rows(k), :] for k in range(LEVELS)] for f in fields], inverse, ratio, couple
        )
        for k in range(LEVELS):
            for f, values in zip(fields, found):
                z_ref[f, level_rows(k), :] = values[k]
    spread_products(z_ref, lat_ref, dia_ref, mat_ref, left_ref, product_ref)
    for f in range(FIELDS):
        own, beyond = (product_blocks(product_ref, f, i) for i in range(2))
        inner = from_neighbours(own, beyond, lane < 32, lane >= 96)
        for j in range(BLOCKS):
            part_ref[f, tile_rows(j), :] = jnp.where(tiles[f // TRACERS] >= 0, inner[j], 0.0)

    wet = []
    for p in range(PLACES):
        rows = [dep_ref[j * PLACES + p : j * PLACES + p + 1, :] for j in range(BLOCKS)]
        masks = [jnp.where(row > level, 1.0, 0.0) for row in rows]
        wet.append(pack_lines(masks, lane))
    for f in range(LEVELS):
        link_ref[0, tile_rows(f), :] = pay_ref[12 + f // TRACERS % PLACES * 3]
        link_ref[1, tile_rows(f), :] = wet[f // TRACERS % PLACES]
    couple = [link_ref[0, level_rows(k), :] for k in range(LEVELS)]
    ((inverse, ratio),) = column_factors([couple], [None])
    for k in range(LEVELS):
        mask = link_ref[1, level_rows(k), :]
        own_ref[0, k] = inverse[k] * mask
        own_ref[1, k] = ratio[k]
        own_ref[2, k] = couple[k]


def pick_kernel(half, tab_ref, *refs):
    pay_refs, (out_ref, all_ref) = refs[:-2], refs[-2:]
    lane = lane_iota()
    zero = jnp.zeros((LEVELS, LANES), jnp.float32)
    for slot, ref in enumerate(pay_refs):
        for i in range(BLOCK_COUNT):
            all_ref[slot * BLOCK_COUNT + i] = ref[i]
    segment, position = lane // 32, lane % 32
    edge = segment ^ (segment // 2)

    def held(row, block, index):
        return jnp.where(row >= 0, take(all_ref[jnp.maximum(row, 0) + block], index), 0.0)

    for p in range(PLACES):
        at = (half * PLACES + p) * TABLE + LINE_AT
        rows = [tab_ref[at + 3 * e] for e in range(4)]
        places = [tab_ref[at + 3 * e + 1] for e in range(4)]
        signs = [tab_ref[at + 3 * e + 2] for e in range(4)]
        index = zero.astype(jnp.int32)
        for e in range(4):
            index = jnp.where(edge == e, places[e] + signs[e] * position, index)
        marks = [jnp.where(rows[e] >= 0, e, -1) for e in range(4)]
        rows = [jnp.maximum(row, 0) for row in rows]

        def fetch(block):
            found = zero
            for e in range(4):
                found = jnp.where(edge == marks[e], take(all_ref[rows[e] + block], index), found)
            return found

        for i in range(3):
            out_ref[p * 3 + i] = fetch(i)
            out_ref[FIELDS + p * 3 + i] = fetch(FIELDS + i)
            out_ref[12 + p * 3 + i] = fetch(12 + i)

    ends = zero
    tracer = lane % 32 // 8
    for p in range(PLACES):
        for i in range(8):
            at = (half * PLACES + p) * TABLE + END_AT + 4 * i
            here = (segment == p) & (lane % 8 == i)
            strip = held(tab_ref[at], 0, tab_ref[at + 1] + tracer * 8)
            point = held(tab_ref[at + 2], 0, tab_ref[at + 3] + tracer * 4)
            ends = jnp.where(here, strip + point, ends)
    out_ref[PICKED_ENDS] = ends

    cells = zero
    cell_adds = zero
    cell_tracer = lane % 16 // 4
    for p in range(PLACES):
        for c in range(4):
            at = (half * PLACES + p) * TABLE + POINT_AT + 6 * c
            here = (position // 16 == p) & (lane % 4 == c)
            cell = held(tab_ref[at], 0, tab_ref[at + 1] + 32 * segment + 4 * cell_tracer)
            cells = jnp.where(here, cell, cells)
            strip_a = held(tab_ref[at + 2], 0, tab_ref[at + 3] + cell_tracer * 8)
            strip_b = held(tab_ref[at + 4], 0, tab_ref[at + 5] + cell_tracer * 8)
            cell_adds = jnp.where(here, strip_a + strip_b, cell_adds)
    out_ref[PICKED_CELLS] = cells
    out_ref[PICKED_ADDS] = cell_adds


def second_kernel(
    tab_ref, part_ref, own_ref, pay_ref, mine_ref, other_ref, out_ref, own_line_ref, line_ref, link_ref
):
    lane = lane_iota()
    zero = jnp.zeros((LEVELS, LANES), jnp.float32)
    segment, position = lane // 32, lane % 32
    edge = segment ^ (segment // 2)
    line_end = (position == 0) | (position == 31)

    def picked(i):
        return mine_ref[i] + other_ref[i]

    strips = [picked(f) for f in range(FIELDS)]
    lines = [picked(FIELDS + f) for f in range(FIELDS)]
    line_lat = [picked(13 + 3 * p) for p in range(PLACES)]
    line_dia = [picked(14 + 3 * p) for p in range(PLACES)]
    for p in range(PLACES):
        link = picked(12 + 3 * p)
        for t in range(TRACERS):
            link_ref[tile_rows(p * TRACERS + t), :] = link
    ends = picked(PICKED_ENDS)
    cells = picked(PICKED_CELLS)
    cell_adds = picked(PICKED_ADDS) + pltpu.roll(pay_ref[CORNER_BLOCK], 32, 1)

    corner_of_lane = jnp.where(segment == 0, jnp.where(position == 31, 1, 0), jnp.where(position == 31, 2, 3))
    at_corner = line_end & ((segment == 0) | (segment == 3))
    for f in range(FIELDS):
        p, t = f // TRACERS, f % TRACERS
        spread = take(ends, p * 32 + t * 8 + edge * 2 + jnp.where(position == 31, 1, 0))
        line_ref[tile_rows(f), :] = lines[f] + pay_ref[f] + jnp.where(line_end, spread, 0.0)
        points = take(cells, p * 16 + t * 4 + corner_of_lane)
        own_line_ref[tile_rows(f), :] = strips[f] + jnp.where(at_corner, points, 0.0)
    line_ref[tile_rows(FIELDS), :] = cells + cell_adds
    line_ref[tile_rows(FIELDS + 1), :] = zero
    own_line_ref[tile_rows(FIELDS), :] = zero
    own_line_ref[tile_rows(FIELDS + 1), :] = zero
    link_ref[tile_rows(FIELDS), :] = pltpu.roll(cells, LANES - 32, 1)
    link_ref[tile_rows(FIELDS + 1), :] = zero
    couple = [link_ref[level_rows(k), :] for k in range(LEVELS - 1)] + [zero]
    ((inverse, ratio),) = column_factors([couple], [None])
    (own_found,) = column_solve(
        [[own_line_ref[level_rows(k), :] for k in range(LEVELS)]],
        [own_ref[0, k] for k in range(LEVELS)],
        [own_ref[1, k] for k in range(LEVELS)],
        [own_ref[2, k] for k in range(LEVELS)],
    )
    (found,) = column_solve([[line_ref[level_rows(k), :] for k in range(LEVELS)]], inverse, ratio, couple)
    for k in range(LEVELS):
        own_line_ref[level_rows(k), :] = own_found[k]
        line_ref[level_rows(k), :] = found[k]
    points = line_ref[tile_rows(FIELDS), :] * pltpu.roll(cells, LANES - 64, 1)

    for p in range(PLACES):
        occupied = tab_ref[p * TABLE + OCCUPIED_AT] > 0
        own_lat, own_dia = pay_ref[13 + 3 * p], pay_ref[14 + 3 * p]
        for t in range(TRACERS):
            f = p * TRACERS + t
            line = line_ref[tile_rows(f), :]
            outer = line_lat[p] * line + beside(line_dia[p] * line, lane)
            outer = outer + jnp.where(at_corner, take(points, 32 + p * 16 + t * 4 + corner_of_lane), 0.0)
            line = own_line_ref[tile_rows(f), :]
            along, across = own_lat * line, own_dia * line
            outer = outer + line - 4.0 * (along + across) + beside(along, lane)
            inner = along + beside(across, lane)
            adds = unpack_lines(jnp.where(occupied, outer, 0.0), jnp.where(occupied, inner, 0.0), lane)
            for j in range(BLOCKS):
                out_ref[f, tile_rows(j), :] = part_ref[f, tile_rows(j), :] + adds[j]


def swap(value, axes, row_count, col_count, row_bit, col_bits):
    pairs = []
    for i in range(row_count):
        for j in range(col_count):
            pairs.append((i * col_count + j, (i ^ row_bit) * col_count + (j ^ col_bits)))
    return lax.ppermute(value, axes, pairs)


def tiled(array, lead):
    blocks = array.reshape(lead + (-1, BLOCKS, LANES))
    rows = blocks.shape[-3]
    order = tuple(range(len(lead))) + (len(lead) + 1, len(lead), len(lead) + 2)
    return blocks.transpose(order).reshape(lead + (BLOCKS * rows, LANES))


def on_device(adjoint_out, lateral, diagonal, vertical, depth, tile_home, edge_link, corner_link):
    row_count, col_count = lax.axis_size("row"), lax.axis_size("col")
    axes = ("row", "col")
    vmem = pl.BlockSpec(memory_space=pltpu.VMEM)
    smem = pl.BlockSpec(memory_space=pltpu.SMEM)
    params = pltpu.CompilerParams(vmem_limit_bytes=VMEM_LIMIT)
    rows = BLOCKS * LEVELS
    x = tiled(adjoint_out, (FIELDS,))
    lat = tiled(lateral, (PLACES,))
    dia = tiled(diagonal, (PLACES,))
    ver = tiled(vertical, (PLACES,))
    dep = tiled(depth, ())
    hbm = pl.BlockSpec(memory_space=pltpu.HBM)
    home, edges, corners = tile_home.reshape(1, -1), edge_link.T, corner_link.T
    matrix = jnp.asarray(spread_matrix(), jnp.bfloat16)
    sources = (dep, ver, x, lat, dia, matrix, home, edges, corners)
    payload, y, fac, dep, lat, dia, matrix, home, edges, corners = pl.pallas_call(
        first_kernel,
        out_shape=(
            f32((BLOCK_COUNT, LEVELS, LANES)),
            f32((FIELDS, rows, LANES)),
            f32((PLACES, 3, LEVELS, BLOCKS, LANES)),
        )
        + tuple(jax.ShapeDtypeStruct(value.shape, value.dtype) for value in (dep, lat, dia, matrix))
        + tuple(pltpu.SMEM(value.shape, value.dtype) for value in (home, edges, corners)),
        in_specs=[hbm] * len(sources),
        out_specs=(vmem,) * 7 + (smem,) * 3,
        scratch_shapes=[
            pltpu.VMEM((PLACES, rows, LANES), jnp.float32),
            pltpu.VMEM((FIELDS, rows, LANES), jnp.float32),
            pltpu.VMEM((FIELDS, rows, LANES), jnp.float32),
            pltpu.VMEM((FIELDS * rows, 6 * LANES), jnp.bfloat16),
            pltpu.VMEM((FIELDS * rows, 2 * LANES), jnp.float32),
            pltpu.SemaphoreType.DMA((len(sources),)),
        ],
        compiler_params=params,
        name="first",
    )(*(pltpu.with_memory_space_constraint(value, pltpu.HBM) for value in sources))
    near = [swap(payload, axes, row_count, col_count, 0, m) for m in range(1, col_count)]
    table, part, own = pl.pallas_call(
        window_kernel,
        out_shape=(
            pltpu.SMEM((2 * PLACES * TABLE,), jnp.int32),
            f32((FIELDS, rows, LANES)),
            f32((3, LEVELS, LEVELS, LANES)),
        ),
        in_specs=[smem] * 3 + [vmem] * 7,
        out_specs=(smem, vmem, vmem),
        scratch_shapes=[
            pltpu.VMEM((FIELDS, rows, LANES), jnp.float32),
            pltpu.VMEM((2, rows, LANES), jnp.float32),
            pltpu.VMEM((FIELDS * rows, 6 * LANES), jnp.bfloat16),
            pltpu.VMEM((FIELDS * rows, 2 * LANES), jnp.float32),
        ],
        compiler_params=params,
        name="window",
    )(home, edges, corners, y, fac, lat, dia, dep, matrix, payload)
    near = [lax.optimization_barrier((value, table))[0] for value in near]
    held = [payload] + near

    def pick_for(half, values):
        return pl.pallas_call(
            functools.partial(pick_kernel, half),
            out_shape=f32((PICKED_COUNT, LEVELS, LANES)),
            in_specs=[smem] + [vmem] * len(values),
            out_specs=vmem,
            scratch_shapes=[pltpu.VMEM((len(values) * BLOCK_COUNT, LEVELS, LANES), jnp.float32)],
            compiler_params=params,
            name="pick",
        )(table, *values)

    sent = pick_for(1, held)
    other = swap(sent, axes, row_count, col_count, 1, 0)
    mine = pick_for(0, [payload] + [lax.optimization_barrier((value, sent))[0] for value in near])
    out = pl.pallas_call(
        second_kernel,
        out_shape=f32((FIELDS, rows, LANES)),
        in_specs=[smem] + [vmem] * 5,
        out_specs=vmem,
        scratch_shapes=[pltpu.VMEM((rows, LANES), jnp.float32)] * 3,
        compiler_params=params,
        name="second",
    )(table, part, own, payload, mine, other)
    out = out.reshape(FIELDS, BLOCKS, LEVELS, LANES).transpose(0, 2, 1, 3)
    return out.reshape(adjoint_out.shape)


def solution(mesh):
    return jax.shard_map(
        on_device,
        mesh=mesh,
        in_specs=(
            P("row", "col", None, None, None, None),
            P("row", "col", None, None, None),
            P("row", "col", None, None, None),
            P("row", "col", None, None, None),
            P("row", "col", None, None),
            P(),
            P(),
            P(),
        ),
        out_specs=P("row", "col", None, None, None, None),
        check_vma=False,
    )
```

```python
import jax
import jax.numpy as jnp
from jax import lax
from jax.experimental import pallas as pl
from jax.experimental.pallas import tpu as pltpu
from jax.sharding import PartitionSpec as P

LEVELS = 8
PLACES = 2
TRACERS = 3
FIELDS = PLACES * TRACERS
BLOCKS = 8
LANES = 128
BLOCK_COUNT = 20
CORNER_BLOCK = 18
END_BLOCK = 19
VMEM_LIMIT = 8 * 2**20
GROUP = 3

CORNER_OF = (0, 1, 1, 2, 3, 2, 0, 3)
OTHER_EDGE = (3, 1, 0, 2, 3, 1, 0, 2)
OTHER_END = (0, 0, 1, 1, 1, 1, 0, 0)
CORNER_A = (0, 1, 3, 4)
CORNER_B = (6, 2, 5, 7)

LINE_AT = 0
END_AT = 12
POINT_AT = 44
OCCUPIED_AT = 68
TABLE = 72


def f32(shape):
    return jax.ShapeDtypeStruct(shape, jnp.float32)


def lane_iota():
    return lax.broadcasted_iota(jnp.int32, (LEVELS, LANES), 1)


def take(block, index):
    return jnp.take_along_axis(block, index, axis=1, mode="promise_in_bounds")


def level_rows(k):
    return pl.ds(k, BLOCKS, stride=LEVELS)


def tile_rows(j):
    return pl.ds(j * LEVELS, LEVELS)


def column_solve(rhs, inverse, ratio, couple):
    partial = [[] for _ in rhs]
    for k in range(LEVELS):
        for values, done in zip(rhs, partial):
            current = values[k]
            if k > 0:
                current = current + couple[k - 1] * done[-1]
            done.append(current * inverse[k])
    found = [[done[-1]] for done in partial]
    for k in range(LEVELS - 2, -1, -1):
        for done, values in zip(partial, found):
            values.insert(0, done[k] + ratio[k] * values[0])
    return found


def column_factors(couples, depths):
    factors = [([], []) for _ in couples]
    for k in range(LEVELS):
        for couple, depth, (inverse, ratio) in zip(couples, depths, factors):
            pivot = 1.0 + couple[k]
            if k > 0:
                pivot = pivot + couple[k - 1] - couple[k - 1] * ratio[-1]
            inv = 1.0 / pivot
            if depth is not None:
                inv = jnp.where(depth > k, inv, 0.0)
            inverse.append(inv)
            ratio.append(couple[k] * inv)
    return factors


def beside(block, lane):
    b = lane % 32
    return jnp.where(b > 0, pltpu.roll(block, 1, 1), 0.0) + jnp.where(b < 31, pltpu.roll(block, LANES - 1, 1), 0.0)


def spread_matrix(mat_ref):
    shape = (LANES, LANES)
    source = lax.broadcasted_iota(jnp.int32, shape, 0)
    target = lax.broadcasted_iota(jnp.int32, shape, 1)
    line = (target < 32) | (target >= 96)
    kind, side = target // 8 % 2, target // 4 % 2
    row = jnp.where(target < 32, 4, jnp.where(target >= 96, -1, 4 * (target // 16) - 12 + target % 4))
    column = jnp.where(line, target % 32, jnp.where(side == 0, 32 - kind, kind - 1))
    for half, (to_row, to_column) in enumerate(((target // 32, target % 32), (row, column))):
        rows = jnp.abs(source // 32 - to_row)
        columns = jnp.abs(source % 32 - to_column)
        same = rows + columns == 0
        across = (rows == 1) & (columns == 1)
        weights = (
            jnp.where(same, 1.0, 0.0),
            jnp.where(same, -4.0, jnp.where(rows + columns == 1, 1.0, 0.0)),
            jnp.where(same, -4.0, jnp.where(across, 1.0, 0.0)),
        )
        for i, weight in enumerate(weights):
            mat_ref[i * LANES : (i + 1) * LANES, half * LANES : (half + 1) * LANES] = weight.astype(jnp.bfloat16)


def split(values):
    high = values.astype(jnp.bfloat16)
    return high, (values - high.astype(jnp.float32)).astype(jnp.bfloat16)


def spread_products(z_ref, lat_ref, dia_ref, mat_ref, left_ref, product_ref):
    rows = BLOCKS * LEVELS
    right = jnp.concatenate([mat_ref[...], mat_ref[...]], axis=0)
    for start in range(0, FIELDS, GROUP):
        for f in range(start, start + GROUP):
            z = z_ref[f]
            p = f // TRACERS
            for i, values in enumerate((z, lat_ref[p] * z, dia_ref[p] * z)):
                high, low = split(values)
                left_ref[f * rows : (f + 1) * rows, i * LANES : (i + 1) * LANES] = high
                left_ref[f * rows : (f + 1) * rows, (3 + i) * LANES : (4 + i) * LANES] = low
        part = slice(start * rows, (start + GROUP) * rows)
        product_ref[part, :] = jnp.dot(left_ref[part, :], right, preferred_element_type=jnp.float32)


def product_blocks(product_ref, f, i):
    rows = BLOCKS * LEVELS
    return [
        product_ref[f * rows + j * LEVELS : f * rows + (j + 1) * LEVELS, i * LANES : (i + 1) * LANES] for j in range(BLOCKS)
    ]


def from_neighbours(blocks, beyond, first_row, last_row):
    sums = []
    for j in range(BLOCKS):
        total = blocks[j]
        if j > 0:
            total = total + jnp.where(first_row, beyond[j - 1], 0.0)
        if j < BLOCKS - 1:
            total = total + jnp.where(last_row, beyond[j + 1], 0.0)
        sums.append(total)
    return sums


def pack_lines(columns, lane):
    residue = lane % 32
    mixed = pltpu.roll(columns[0], 1, 1)
    for j in range(1, BLOCKS):
        mixed = jnp.where(residue // 2 == j, pltpu.roll(columns[j], 2 * j + 1, 1), mixed)
    q, j = residue % 4, residue // 4
    index = jnp.where(lane < 64, 32 * ((q + 1) % 4) + 2 * j, 32 * q + 2 * j + 1)
    return jnp.where(lane < 32, columns[0], jnp.where(lane >= 96, columns[-1], take(mixed, index)))


def pack_products(inner, beyond, lane):
    slot = lane // 16
    mixed = jnp.zeros_like(beyond[0])
    for j in range(BLOCKS):
        moved = pltpu.roll(beyond[j], (16 * j - 48) % LANES, 1) if j != 3 else beyond[j]
        mixed = mixed + jnp.where((slot >= j - 1) & (slot <= j + 1), moved, 0.0)
    index = 16 * (lane % 32 // 4) + lane % 4 + jnp.where(lane >= 64, 4, 0)
    low, high = lane < 32, lane >= 96
    ghosts = take(jnp.where(lane < 64, beyond[-1], beyond[0]), lane ^ 96)
    strips = jnp.where(low | high, ghosts, take(mixed, index))
    lines = jnp.where(low, inner[0], jnp.where(high, inner[-1], take(mixed, index + 8)))
    return strips, lines


def unpack_lines(outer, inner, lane):
    residue = lane % 32
    j, part, q = residue // 4, residue % 4, lane // 32
    index = jnp.where(part < 2, 32 + 4 * j + (q + 3) % 4, 64 + 4 * j + q)
    mixed = jnp.where((part == 0) | (part == 3), take(inner, index), take(outer, index))
    near = (residue < 2) | (residue >= 30)
    adds = [jnp.where(near, pltpu.roll(mixed, (LANES - 4 * j - 2) % LANES, 1), 0.0) for j in range(BLOCKS)]
    segment = lane // 32
    low = jnp.where(segment == 0, outer, jnp.where(segment == 1, pltpu.roll(inner, 32, 1), 0.0))
    high = jnp.where(segment == 3, outer, jnp.where(segment == 2, pltpu.roll(inner, LANES - 32, 1), 0.0))
    adds[0] = adds[0] + low
    adds[-1] = adds[-1] + high
    return adds


def pack_corners(line, lane):
    c = lane % 4
    return take(line, jnp.where(c == 0, 0, jnp.where(c == 1, 31, jnp.where(c == 2, 127, 96))))


def first_kernel(
    *refs,
):
    sources, refs = refs[:8], refs[8:]
    pay_ref, y_ref, fac_ref, dep_ref, lat_ref, dia_ref, mat_ref, home_ref, edge_ref, corner_ref = refs[:10]
    ver_ref, x_ref, z_ref, left_ref, product_ref, sems = refs[10:]
    targets = (dep_ref, ver_ref, x_ref, lat_ref, dia_ref, home_ref, edge_ref, corner_ref)
    moves = [pltpu.make_async_copy(source, target, sems.at[i]) for i, (source, target) in enumerate(zip(sources, targets))]
    for move in moves:
        move.start()
    spread_matrix(mat_ref)
    lane = lane_iota()
    level = lax.broadcasted_iota(jnp.int32, (LEVELS, LANES), 0)
    group = lane // 32
    corners = jnp.zeros((LEVELS, LANES), jnp.float32)
    ends = jnp.zeros((LEVELS, LANES), jnp.float32)
    end_edge = lane % 8 // 2
    end_lane = 32 * (end_edge ^ (end_edge // 2)) + 31 * (lane % 2)
    moves[0].wait()
    moves[1].wait()
    depth = [dep_ref[pl.ds(p, BLOCKS, stride=PLACES), :] for p in range(PLACES)]
    couple = [
        [jnp.where(depth[p] > k + 1, ver_ref[p, level_rows(k), :], 0.0) for k in range(LEVELS - 1)]
        + [jnp.zeros((BLOCKS, LANES), jnp.float32)]
        for p in range(PLACES)
    ]
    factors = column_factors(couple, depth)
    for p in range(PLACES):
        for k in range(LEVELS):
            fac_ref[p, 0, k] = factors[p][0][k]
            fac_ref[p, 1, k] = factors[p][1][k]
            fac_ref[p, 2, k] = couple[p][k]
    moves[2].wait()
    for p in range(PLACES):
        fields = [p * TRACERS + t for t in range(TRACERS)]
        found = column_solve(
            [[x_ref[f, level_rows(k), :] for k in range(LEVELS)] for f in fields], *factors[p], couple[p]
        )
        for k in range(LEVELS):
            for f, values in zip(fields, found):
                z_ref[f, level_rows(k), :] = values[k]
    for move in moves[3:5]:
        move.wait()
    spread_products(z_ref, lat_ref, dia_ref, mat_ref, left_ref, product_ref)
    for p in range(PLACES):
        wet_lat, wet_dia, link = [], [], []
        for j in range(BLOCKS):
            row = dep_ref[j * PLACES + p : j * PLACES + p + 1, :]
            wet_lat.append(jnp.where(row > level, lat_ref[p, tile_rows(j), :], 0.0))
            wet_dia.append(jnp.where(row > level, dia_ref[p, tile_rows(j), :], 0.0))
            link.append(jnp.where((row > level + 1) & (level < LEVELS - 1), ver_ref[p, tile_rows(j), :], 0.0))
        coefs = [pack_lines(blocks, lane) for blocks in (link, wet_lat, wet_dia)]
        for i in range(3):
            pay_ref[12 + p * 3 + i] = coefs[i]
        link_corners = pack_corners(coefs[0], lane)
        dia_corners = pack_corners(coefs[2], lane)
        for t in range(TRACERS):
            f = p * TRACERS + t
            own, beyond = (product_blocks(product_ref, f, i) for i in range(2))
            inner = from_neighbours(own, beyond, lane < 32, lane >= 96)
            for j in range(BLOCKS):
                y_ref[f, tile_rows(j), :] = inner[j]
            strips, lines = pack_products(inner, beyond, lane)
            pay_ref[f] = strips
            pay_ref[FIELDS + f] = lines
            across = jnp.where(
                lane < 64,
                dia_ref[p, tile_rows(0), :] * z_ref[f, tile_rows(0), :],
                dia_ref[p, tile_rows(BLOCKS - 1), :] * z_ref[f, tile_rows(BLOCKS - 1), :],
            )
            cells = jnp.where(
                group == 0,
                pack_corners(across, lane),
                jnp.where(group == 1, pack_corners(lines, lane), jnp.where(group == 2, link_corners, dia_corners)),
            )
            corners = jnp.where(lane % 32 // 4 == p * 4 + t, cells, corners)
            ends = jnp.where(lane // 8 == p * 4 + t, take(strips, end_lane), ends)
    pay_ref[CORNER_BLOCK] = corners
    pay_ref[END_BLOCK] = ends
    for move in moves[5:]:
        move.wait()


def pick(values, index, bits):
    packed = 0
    for i, value in enumerate(values):
        packed |= value << (bits * i)
    return lax.shift_right_logical(jnp.int32(packed), index * bits) & (2**bits - 1)


def window_kernel(
    home_ref, edge_ref, corner_ref, y_ref, fac_ref, lat_ref, dia_ref, dep_ref, mat_ref, pay_ref,
    out_ref, part_ref, own_ref, z_ref, link_ref, left_ref, product_ref,
):
    row = lax.axis_index("row")
    col = lax.axis_index("col")
    col_count = lax.axis_size("col")
    device = row * col_count + col

    def scan(t, found):
        here = home_ref[0, t]
        return tuple(jnp.where(here == device * PLACES + p, t, found[p]) for p in range(PLACES))

    tile_count = home_ref.shape[1]
    unroll = 8 if tile_count % 8 == 0 else 1

    def scan_some(i, found):
        for s in range(unroll):
            found = scan(i * unroll + s, found)
        return found

    tiles = lax.fori_loop(0, tile_count // unroll, scan_some, tuple(jnp.int32(-1) for _ in range(PLACES)))

    def block_of(tile):
        place = home_ref[0, tile]
        other = lax.shift_right_logical(place, 1)
        slot = (other ^ device) & (2 * col_count - 1)
        return slot * BLOCK_COUNT, place & 1

    def edge_of(tile, edge):
        code = edge_ref[edge, tile]
        return lax.shift_right_logical(code, 3), lax.shift_right_logical(code, 1) & 3, code & 1

    def strip_end(tile, edge_end):
        other, f, r = edge_of(tile, lax.shift_right_logical(edge_end, 1))
        base, place = block_of(other)
        return base + END_BLOCK, place * 32 + f * 2 + ((edge_end & 1) ^ r)

    def point(tile, corner):
        code = corner_ref[corner, tile]
        safe = jnp.maximum(code, 0)
        other, g = lax.shift_right_logical(safe, 2), safe & 3
        base, place = block_of(other)
        return base + CORNER_BLOCK, jnp.where(code >= 0, place * 16 + g, -1), other, g

    for p in range(PLACES):
        at = p * TABLE
        tile = jnp.maximum(tiles[p], 0)
        out_ref[at + OCCUPIED_AT] = jnp.where(tiles[p] >= 0, 1, 0)
        for e in range(4):
            other, f, r = edge_of(tile, e)
            base, place = block_of(other)
            out_ref[at + LINE_AT + 3 * e] = base + place * 3
            out_ref[at + LINE_AT + 3 * e + 1] = 32 * (f ^ lax.shift_right_logical(f, 1)) + 31 * r
            out_ref[at + LINE_AT + 3 * e + 2] = 1 - 2 * r
            for end in range(2):
                index = f * 2 + (end ^ r)
                strip_row, strip_lane = strip_end(other, pick(OTHER_EDGE, index, 2) * 2 + pick(OTHER_END, index, 1))
                point_row, point_lane, _, _ = point(other, pick(CORNER_OF, index, 2))
                slot = at + END_AT + 4 * (2 * e + end)
                out_ref[slot] = strip_row
                out_ref[slot + 1] = strip_lane
                out_ref[slot + 2] = point_row
                out_ref[slot + 3] = point_lane
        for c in range(4):
            point_row, point_lane, other, g = point(tile, c)
            slot = at + POINT_AT + 6 * c
            out_ref[slot] = point_row
            out_ref[slot + 1] = point_lane
            row_a, lane_a = strip_end(other, pick(CORNER_A, g, 3))
            row_b, lane_b = strip_end(other, pick(CORNER_B, g, 3))
            out_ref[slot + 2] = row_a
            out_ref[slot + 3] = lane_a
            out_ref[slot + 4] = row_b
            out_ref[slot + 5] = lane_b

    lane = lane_iota()
    level = lax.broadcasted_iota(jnp.int32, (LEVELS, LANES), 0)
    for p in range(PLACES):
        fields = [p * TRACERS + t for t in range(TRACERS)]
        inverse = [fac_ref[p, 0, k] for k in range(LEVELS)]
        ratio = [fac_ref[p, 1, k] for k in range(LEVELS)]
        couple = [fac_ref[p, 2, k] for k in range(LEVELS)]
        found = column_solve(
            [[y_ref[f, level_rows(k), :] for k in range(LEVELS)] for f in fields], inverse, ratio, couple
        )
        for k in range(LEVELS):
            for f, values in zip(fields, found):
                z_ref[f, level_rows(k), :] = values[k]
    spread_products(z_ref, lat_ref, dia_ref, mat_ref, left_ref, product_ref)
    for f in range(FIELDS):
        own, beyond = (product_blocks(product_ref, f, i) for i in range(2))
        inner = from_neighbours(own, beyond, lane < 32, lane >= 96)
        for j in range(BLOCKS):
            part_ref[f, tile_rows(j), :] = jnp.where(tiles[f // TRACERS] >= 0, inner[j], 0.0)

    wet = []
    for p in range(PLACES):
        rows = [dep_ref[j * PLACES + p : j * PLACES + p + 1, :] for j in range(BLOCKS)]
        masks = [jnp.where(row > level, 1.0, 0.0) for row in rows]
        wet.append(pack_lines(masks, lane))
    for f in range(LEVELS):
        link_ref[0, tile_rows(f), :] = pay_ref[12 + f // TRACERS % PLACES * 3]
        link_ref[1, tile_rows(f), :] = wet[f // TRACERS % PLACES]
    couple = [link_ref[0, level_rows(k), :] for k in range(LEVELS)]
    ((inverse, ratio),) = column_factors([couple], [None])
    for k in range(LEVELS):
        mask = link_ref[1, level_rows(k), :]
        own_ref[0, k] = inverse[k] * mask
        own_ref[1, k] = ratio[k]
        own_ref[2, k] = couple[k]


def second_kernel(tab_ref, part_ref, own_ref, *refs):
    pay_refs = refs[:-5]
    out_ref, all_ref, own_line_ref, line_ref, link_ref = refs[-5:]
    lane = lane_iota()
    zero = jnp.zeros((LEVELS, LANES), jnp.float32)
    for slot, ref in enumerate(pay_refs):
        for i in range(BLOCK_COUNT):
            all_ref[slot * BLOCK_COUNT + i] = ref[i]
    segment, position = lane // 32, lane % 32
    edge = segment ^ (segment // 2)
    line_end = (position == 0) | (position == 31)

    strips, lines, line_lat, line_dia = [], [], [], []
    for p in range(PLACES):
        at = p * TABLE + LINE_AT
        rows = [tab_ref[at + 3 * e] for e in range(4)]
        places = [tab_ref[at + 3 * e + 1] for e in range(4)]
        signs = [tab_ref[at + 3 * e + 2] for e in range(4)]
        index = zero.astype(jnp.int32)
        for e in range(4):
            index = jnp.where(edge == e, places[e] + signs[e] * position, index)

        def fetch(block):
            found = take(all_ref[rows[0] + block], index)
            for e in range(1, 4):
                found = jnp.where(edge == e, take(all_ref[rows[e] + block], index), found)
            return found

        for t in range(TRACERS):
            strips.append(fetch(t))
            lines.append(fetch(FIELDS + t))
        link = fetch(12)
        for t in range(TRACERS):
            link_ref[tile_rows(p * TRACERS + t), :] = link
        line_lat.append(fetch(13))
        line_dia.append(fetch(14))

    ends = zero
    tracer = lane % 32 // 8
    for p in range(PLACES):
        for i in range(8):
            at = p * TABLE + END_AT + 4 * i
            here = (segment == p) & (lane % 8 == i)
            strip = take(all_ref[tab_ref[at]], tab_ref[at + 1] + tracer * 8)
            point_lane = tab_ref[at + 3]
            point = take(all_ref[tab_ref[at + 2]], jnp.maximum(point_lane, 0) + tracer * 4)
            ends = jnp.where(here, strip + jnp.where(point_lane >= 0, point, 0.0), ends)

    cells = zero
    cell_adds = zero
    cell_tracer = lane % 16 // 4
    for p in range(PLACES):
        for c in range(4):
            at = p * TABLE + POINT_AT + 6 * c
            here = (position // 16 == p) & (lane % 4 == c)
            point_lane = tab_ref[at + 1]
            cell = take(all_ref[tab_ref[at]], jnp.maximum(point_lane, 0) + 32 * segment + 4 * cell_tracer)
            cells = jnp.where(here & (point_lane >= 0), cell, cells)
            strip_a = take(all_ref[tab_ref[at + 2]], tab_ref[at + 3] + cell_tracer * 8)
            strip_b = take(all_ref[tab_ref[at + 4]], tab_ref[at + 5] + cell_tracer * 8)
            cell_adds = jnp.where(here, strip_a + strip_b, cell_adds)
    cell_adds = cell_adds + pltpu.roll(all_ref[CORNER_BLOCK], 32, 1)

    corner_of_lane = jnp.where(segment == 0, jnp.where(position == 31, 1, 0), jnp.where(position == 31, 2, 3))
    at_corner = line_end & ((segment == 0) | (segment == 3))
    for f in range(FIELDS):
        p, t = f // TRACERS, f % TRACERS
        spread = take(ends, p * 32 + t * 8 + edge * 2 + jnp.where(position == 31, 1, 0))
        line_ref[tile_rows(f), :] = lines[f] + all_ref[f] + jnp.where(line_end, spread, 0.0)
        points = take(cells, p * 16 + t * 4 + corner_of_lane)
        own_line_ref[tile_rows(f), :] = strips[f] + jnp.where(at_corner, points, 0.0)
    line_ref[tile_rows(FIELDS), :] = cells + cell_adds
    line_ref[tile_rows(FIELDS + 1), :] = zero
    own_line_ref[tile_rows(FIELDS), :] = zero
    own_line_ref[tile_rows(FIELDS + 1), :] = zero
    link_ref[tile_rows(FIELDS), :] = pltpu.roll(cells, LANES - 32, 1)
    link_ref[tile_rows(FIELDS + 1), :] = zero
    couple = [link_ref[level_rows(k), :] for k in range(LEVELS - 1)] + [zero]
    ((inverse, ratio),) = column_factors([couple], [None])
    (own_found,) = column_solve(
        [[own_line_ref[level_rows(k), :] for k in range(LEVELS)]],
        [own_ref[0, k] for k in range(LEVELS)],
        [own_ref[1, k] for k in range(LEVELS)],
        [own_ref[2, k] for k in range(LEVELS)],
    )
    (found,) = column_solve([[line_ref[level_rows(k), :] for k in range(LEVELS)]], inverse, ratio, couple)
    for k in range(LEVELS):
        own_line_ref[level_rows(k), :] = own_found[k]
        line_ref[level_rows(k), :] = found[k]
    points = line_ref[tile_rows(FIELDS), :] * pltpu.roll(cells, LANES - 64, 1)

    for p in range(PLACES):
        occupied = tab_ref[p * TABLE + OCCUPIED_AT] > 0
        own_lat, own_dia = all_ref[13 + 3 * p], all_ref[14 + 3 * p]
        for t in range(TRACERS):
            f = p * TRACERS + t
            line = line_ref[tile_rows(f), :]
            outer = line_lat[p] * line + beside(line_dia[p] * line, lane)
            outer = outer + jnp.where(at_corner, take(points, 32 + p * 16 + t * 4 + corner_of_lane), 0.0)
            line = own_line_ref[tile_rows(f), :]
            along, across = own_lat * line, own_dia * line
            outer = outer + line - 4.0 * (along + across) + beside(along, lane)
            inner = along + beside(across, lane)
            adds = unpack_lines(jnp.where(occupied, outer, 0.0), jnp.where(occupied, inner, 0.0), lane)
            for j in range(BLOCKS):
                out_ref[f, tile_rows(j), :] = part_ref[f, tile_rows(j), :] + adds[j]


def swap(value, axes, row_count, col_count, row_bit, col_bits):
    pairs = []
    for i in range(row_count):
        for j in range(col_count):
            pairs.append((i * col_count + j, (i ^ row_bit) * col_count + (j ^ col_bits)))
    return lax.ppermute(value, axes, pairs)


def tiled(array, lead):
    blocks = array.reshape(lead + (-1, BLOCKS, LANES))
    rows = blocks.shape[-3]
    order = tuple(range(len(lead))) + (len(lead) + 1, len(lead), len(lead) + 2)
    return blocks.transpose(order).reshape(lead + (BLOCKS * rows, LANES))


def on_device(adjoint_out, lateral, diagonal, vertical, depth, tile_home, edge_link, corner_link):
    row_count, col_count = lax.axis_size("row"), lax.axis_size("col")
    axes = ("row", "col")
    vmem = pl.BlockSpec(memory_space=pltpu.VMEM)
    smem = pl.BlockSpec(memory_space=pltpu.SMEM)
    params = pltpu.CompilerParams(vmem_limit_bytes=VMEM_LIMIT)
    rows = BLOCKS * LEVELS
    x = tiled(adjoint_out, (FIELDS,))
    lat = tiled(lateral, (PLACES,))
    dia = tiled(diagonal, (PLACES,))
    ver = tiled(vertical, (PLACES,))
    dep = tiled(depth, ())
    hbm = pl.BlockSpec(memory_space=pltpu.HBM)
    home, edges, corners = tile_home.reshape(1, -1), edge_link.T, corner_link.T
    sources = (dep, ver, x, lat, dia, home, edges, corners)
    payload, y, fac, dep, lat, dia, matrix, home, edges, corners = pl.pallas_call(
        first_kernel,
        out_shape=(
            f32((BLOCK_COUNT, LEVELS, LANES)),
            f32((FIELDS, rows, LANES)),
            f32((PLACES, 3, LEVELS, BLOCKS, LANES)),
        )
        + tuple(jax.ShapeDtypeStruct(value.shape, value.dtype) for value in (dep, lat, dia))
        + (jax.ShapeDtypeStruct((3 * LANES, 2 * LANES), jnp.bfloat16),)
        + tuple(pltpu.SMEM(value.shape, value.dtype) for value in (home, edges, corners)),
        in_specs=[hbm] * len(sources),
        out_specs=(vmem,) * 7 + (smem,) * 3,
        scratch_shapes=[
            pltpu.VMEM((PLACES, rows, LANES), jnp.float32),
            pltpu.VMEM((FIELDS, rows, LANES), jnp.float32),
            pltpu.VMEM((FIELDS, rows, LANES), jnp.float32),
            pltpu.VMEM((FIELDS * rows, 6 * LANES), jnp.bfloat16),
            pltpu.VMEM((FIELDS * rows, 2 * LANES), jnp.float32),
            pltpu.SemaphoreType.DMA((len(sources),)),
        ],
        compiler_params=params,
        name="first",
    )(*(pltpu.with_memory_space_constraint(value, pltpu.HBM) for value in sources))
    near = [swap(payload, axes, row_count, col_count, 0, m) for m in range(1, col_count)]
    table, part, own = pl.pallas_call(
        window_kernel,
        out_shape=(
            pltpu.SMEM((PLACES * TABLE,), jnp.int32),
            f32((FIELDS, rows, LANES)),
            f32((3, LEVELS, LEVELS, LANES)),
        ),
        in_specs=[smem] * 3 + [vmem] * 7,
        out_specs=(smem, vmem, vmem),
        scratch_shapes=[
            pltpu.VMEM((FIELDS, rows, LANES), jnp.float32),
            pltpu.VMEM((2, rows, LANES), jnp.float32),
            pltpu.VMEM((FIELDS * rows, 6 * LANES), jnp.bfloat16),
            pltpu.VMEM((FIELDS * rows, 2 * LANES), jnp.float32),
        ],
        compiler_params=params,
        name="window",
    )(home, edges, corners, y, fac, lat, dia, dep, matrix, payload)
    near = [lax.optimization_barrier((value, table))[0] for value in near]
    twin = swap(lax.optimization_barrier((payload, table))[0], axes, row_count, col_count, 1, 0)
    far = [swap(value, axes, row_count, col_count, 1, 0) for value in near]
    payloads = [payload] + near + [twin] + far
    out = pl.pallas_call(
        second_kernel,
        out_shape=f32((FIELDS, rows, LANES)),
        in_specs=[smem] + [vmem] * (2 + len(payloads)),
        out_specs=vmem,
        scratch_shapes=[
            pltpu.VMEM((len(payloads) * BLOCK_COUNT, LEVELS, LANES), jnp.float32),
            pltpu.VMEM((rows, LANES), jnp.float32),
            pltpu.VMEM((rows, LANES), jnp.float32),
            pltpu.VMEM((rows, LANES), jnp.float32),
        ],
        compiler_params=pltpu.CompilerParams(vmem_limit_bytes=VMEM_LIMIT + 2 * len(payloads) * BLOCK_COUNT * 4096),
        name="second",
    )(table, part, own, *payloads)
    out = out.reshape(FIELDS, BLOCKS, LEVELS, LANES).transpose(0, 2, 1, 3)
    return out.reshape(adjoint_out.shape)


def solution(mesh):
    return jax.shard_map(
        on_device,
        mesh=mesh,
        in_specs=(
            P("row", "col", None, None, None, None),
            P("row", "col", None, None, None),
            P("row", "col", None, None, None),
            P("row", "col", None, None, None),
            P("row", "col", None, None),
            P(),
            P(),
            P(),
        ),
        out_specs=P("row", "col", None, None, None, None),
        check_vma=False,
    )
```

```python
import jax
import jax.numpy as jnp
from jax import lax
from jax.experimental import pallas as pl
from jax.experimental.pallas import tpu as pltpu
from jax.sharding import PartitionSpec as P

LEVELS = 8
PLACES = 2
TRACERS = 3
FIELDS = PLACES * TRACERS
BLOCKS = 8
LANES = 128
BLOCK_COUNT = 19
CORNER_BLOCK = 18
VMEM_LIMIT = 8 * 2**20
GROUP = 3

CORNER_OF = (0, 1, 1, 2, 3, 2, 0, 3)
OTHER_EDGE = (3, 1, 0, 2, 3, 1, 0, 2)
OTHER_END = (0, 0, 1, 1, 1, 1, 0, 0)
CORNER_A = (0, 1, 3, 4)
CORNER_B = (6, 2, 5, 7)

LINE_AT = 0
END_AT = 12
POINT_AT = 44
OCCUPIED_AT = 68
TABLE = 72


def f32(shape):
    return jax.ShapeDtypeStruct(shape, jnp.float32)


def lane_iota():
    return lax.broadcasted_iota(jnp.int32, (LEVELS, LANES), 1)


def take(block, index):
    return jnp.take_along_axis(block, index, axis=1, mode="promise_in_bounds")


def level_rows(k):
    return pl.ds(k, BLOCKS, stride=LEVELS)


def tile_rows(j):
    return pl.ds(j * LEVELS, LEVELS)


def column_solve(rhs, inverse, ratio, couple):
    partial = [[] for _ in rhs]
    for k in range(LEVELS):
        for values, done in zip(rhs, partial):
            current = values[k]
            if k > 0:
                current = current + couple[k - 1] * done[-1]
            done.append(current * inverse[k])
    found = [[done[-1]] for done in partial]
    for k in range(LEVELS - 2, -1, -1):
        for done, values in zip(partial, found):
            values.insert(0, done[k] + ratio[k] * values[0])
    return found


def column_factors(couples, depths):
    factors = [([], []) for _ in couples]
    for k in range(LEVELS):
        for couple, depth, (inverse, ratio) in zip(couples, depths, factors):
            pivot = 1.0 + couple[k]
            if k > 0:
                pivot = pivot + couple[k - 1] - couple[k - 1] * ratio[-1]
            inv = 1.0 / pivot
            if depth is not None:
                inv = jnp.where(depth > k, inv, 0.0)
            inverse.append(inv)
            ratio.append(couple[k] * inv)
    return factors


def beside(block, lane):
    b = lane % 32
    return jnp.where(b > 0, pltpu.roll(block, 1, 1), 0.0) + jnp.where(b < 31, pltpu.roll(block, LANES - 1, 1), 0.0)


def spread_matrix(mat_ref):
    shape = (LANES, LANES)
    source = lax.broadcasted_iota(jnp.int32, shape, 0)
    target = lax.broadcasted_iota(jnp.int32, shape, 1)
    line = (target < 32) | (target >= 96)
    kind, side = target // 8 % 2, target // 4 % 2
    row = jnp.where(target < 32, 4, jnp.where(target >= 96, -1, 4 * (target // 16) - 12 + target % 4))
    column = jnp.where(line, target % 32, jnp.where(side == 0, 32 - kind, kind - 1))
    for half, (to_row, to_column) in enumerate(((target // 32, target % 32), (row, column))):
        rows = jnp.abs(source // 32 - to_row)
        columns = jnp.abs(source % 32 - to_column)
        same = rows + columns == 0
        across = (rows == 1) & (columns == 1)
        weights = (
            jnp.where(same, 1.0, 0.0),
            jnp.where(same, -4.0, jnp.where(rows + columns == 1, 1.0, 0.0)),
            jnp.where(same, -4.0, jnp.where(across, 1.0, 0.0)),
        )
        for i, weight in enumerate(weights):
            mat_ref[i * LANES : (i + 1) * LANES, half * LANES : (half + 1) * LANES] = weight.astype(jnp.bfloat16)


def split(values):
    high = values.astype(jnp.bfloat16)
    return high, (values - high.astype(jnp.float32)).astype(jnp.bfloat16)


def spread_products(z_ref, lat_ref, dia_ref, mat_ref, left_ref, product_ref):
    rows = BLOCKS * LEVELS
    right = jnp.concatenate([mat_ref[...], mat_ref[...]], axis=0)
    for start in range(0, FIELDS, GROUP):
        for f in range(start, start + GROUP):
            z = z_ref[f]
            p = f // TRACERS
            for i, values in enumerate((z, lat_ref[p] * z, dia_ref[p] * z)):
                high, low = split(values)
                left_ref[f * rows : (f + 1) * rows, i * LANES : (i + 1) * LANES] = high
                left_ref[f * rows : (f + 1) * rows, (3 + i) * LANES : (4 + i) * LANES] = low
        part = slice(start * rows, (start + GROUP) * rows)
        product_ref[part, :] = jnp.dot(left_ref[part, :], right, preferred_element_type=jnp.float32)


def product_blocks(product_ref, f, i):
    rows = BLOCKS * LEVELS
    return [
        product_ref[f * rows + j * LEVELS : f * rows + (j + 1) * LEVELS, i * LANES : (i + 1) * LANES] for j in range(BLOCKS)
    ]


def from_neighbours(blocks, beyond, first_row, last_row):
    sums = []
    for j in range(BLOCKS):
        total = blocks[j]
        if j > 0:
            total = total + jnp.where(first_row, beyond[j - 1], 0.0)
        if j < BLOCKS - 1:
            total = total + jnp.where(last_row, beyond[j + 1], 0.0)
        sums.append(total)
    return sums


def pack_lines(columns, lane):
    residue = lane % 32
    mixed = pltpu.roll(columns[0], 1, 1)
    for j in range(1, BLOCKS):
        mixed = jnp.where(residue // 2 == j, pltpu.roll(columns[j], 2 * j + 1, 1), mixed)
    q, j = residue % 4, residue // 4
    index = jnp.where(lane < 64, 32 * ((q + 1) % 4) + 2 * j, 32 * q + 2 * j + 1)
    return jnp.where(lane < 32, columns[0], jnp.where(lane >= 96, columns[-1], take(mixed, index)))


def pack_products(inner, beyond, lane):
    slot = lane // 16
    mixed = jnp.zeros_like(beyond[0])
    for j in range(BLOCKS):
        moved = pltpu.roll(beyond[j], (16 * j - 48) % LANES, 1) if j != 3 else beyond[j]
        mixed = mixed + jnp.where((slot >= j - 1) & (slot <= j + 1), moved, 0.0)
    index = 16 * (lane % 32 // 4) + lane % 4 + jnp.where(lane >= 64, 4, 0)
    low, high = lane < 32, lane >= 96
    ghosts = take(jnp.where(lane < 64, beyond[-1], beyond[0]), lane ^ 96)
    strips = jnp.where(low | high, ghosts, take(mixed, index))
    lines = jnp.where(low, inner[0], jnp.where(high, inner[-1], take(mixed, index + 8)))
    return strips, lines


def unpack_lines(outer, inner, lane):
    residue = lane % 32
    j, part, q = residue // 4, residue % 4, lane // 32
    index = jnp.where(part < 2, 32 + 4 * j + (q + 3) % 4, 64 + 4 * j + q)
    mixed = jnp.where((part == 0) | (part == 3), take(inner, index), take(outer, index))
    near = (residue < 2) | (residue >= 30)
    adds = [jnp.where(near, pltpu.roll(mixed, (LANES - 4 * j - 2) % LANES, 1), 0.0) for j in range(BLOCKS)]
    segment = lane // 32
    low = jnp.where(segment == 0, outer, jnp.where(segment == 1, pltpu.roll(inner, 32, 1), 0.0))
    high = jnp.where(segment == 3, outer, jnp.where(segment == 2, pltpu.roll(inner, LANES - 32, 1), 0.0))
    adds[0] = adds[0] + low
    adds[-1] = adds[-1] + high
    return adds


def pack_corners(line, lane):
    c = lane % 4
    return take(line, jnp.where(c == 0, 0, jnp.where(c == 1, 31, jnp.where(c == 2, 127, 96))))


def first_kernel(
    *refs,
):
    sources, refs = refs[:8], refs[8:]
    pay_ref, y_ref, fac_ref, dep_ref, lat_ref, dia_ref, mat_ref, home_ref, edge_ref, corner_ref = refs[:10]
    ver_ref, x_ref, z_ref, left_ref, product_ref, sems = refs[10:]
    targets = (dep_ref, ver_ref, x_ref, lat_ref, dia_ref, home_ref, edge_ref, corner_ref)
    moves = [pltpu.make_async_copy(source, target, sems.at[i]) for i, (source, target) in enumerate(zip(sources, targets))]
    for move in moves:
        move.start()
    spread_matrix(mat_ref)
    lane = lane_iota()
    level = lax.broadcasted_iota(jnp.int32, (LEVELS, LANES), 0)
    group = lane // 32
    corners = jnp.zeros((LEVELS, LANES), jnp.float32)
    end_edge = lane % 8 // 2
    end_lane = 32 * (end_edge ^ (end_edge // 2)) + 31 * (lane % 2)
    moves[0].wait()
    moves[1].wait()
    depth = [dep_ref[pl.ds(p, BLOCKS, stride=PLACES), :] for p in range(PLACES)]
    couple = [
        [jnp.where(depth[p] > k + 1, ver_ref[p, level_rows(k), :], 0.0) for k in range(LEVELS - 1)]
        + [jnp.zeros((BLOCKS, LANES), jnp.float32)]
        for p in range(PLACES)
    ]
    factors = column_factors(couple, depth)
    for p in range(PLACES):
        for k in range(LEVELS):
            fac_ref[p, 0, k] = factors[p][0][k]
            fac_ref[p, 1, k] = factors[p][1][k]
            fac_ref[p, 2, k] = couple[p][k]
    moves[2].wait()
    for p in range(PLACES):
        fields = [p * TRACERS + t for t in range(TRACERS)]
        found = column_solve(
            [[x_ref[f, level_rows(k), :] for k in range(LEVELS)] for f in fields], *factors[p], couple[p]
        )
        for k in range(LEVELS):
            for f, values in zip(fields, found):
                z_ref[f, level_rows(k), :] = values[k]
    for move in moves[3:5]:
        move.wait()
    spread_products(z_ref, lat_ref, dia_ref, mat_ref, left_ref, product_ref)
    for p in range(PLACES):
        wet_lat, wet_dia, link = [], [], []
        for j in range(BLOCKS):
            row = dep_ref[j * PLACES + p : j * PLACES + p + 1, :]
            wet_lat.append(jnp.where(row > level, lat_ref[p, tile_rows(j), :], 0.0))
            wet_dia.append(jnp.where(row > level, dia_ref[p, tile_rows(j), :], 0.0))
            link.append(jnp.where((row > level + 1) & (level < LEVELS - 1), ver_ref[p, tile_rows(j), :], 0.0))
        coefs = [pack_lines(blocks, lane) for blocks in (link, wet_lat, wet_dia)]
        for i in range(3):
            pay_ref[12 + p * 3 + i] = coefs[i]
        link_corners = pack_corners(coefs[0], lane)
        dia_corners = pack_corners(coefs[2], lane)
        for t in range(TRACERS):
            f = p * TRACERS + t
            own, beyond = (product_blocks(product_ref, f, i) for i in range(2))
            inner = from_neighbours(own, beyond, lane < 32, lane >= 96)
            for j in range(BLOCKS):
                y_ref[f, tile_rows(j), :] = inner[j]
            strips, lines = pack_products(inner, beyond, lane)
            pay_ref[f] = strips
            pay_ref[FIELDS + f] = lines
            across = jnp.where(
                lane < 64,
                dia_ref[p, tile_rows(0), :] * z_ref[f, tile_rows(0), :],
                dia_ref[p, tile_rows(BLOCKS - 1), :] * z_ref[f, tile_rows(BLOCKS - 1), :],
            )
            cells = jnp.where(group == 0, pack_corners(across, lane), pack_corners(lines, lane))
            corners = jnp.where((lane < 64) & (lane % 32 // 4 == p * 4 + t), cells, corners)
            corners = jnp.where(lane // 8 == 10 + p * 3 + t, take(strips, end_lane), corners)
        corners = jnp.where(lane // 4 == 16 + p, link_corners, corners)
        corners = jnp.where(lane // 4 == 18 + p, dia_corners, corners)
    pay_ref[CORNER_BLOCK] = corners
    for move in moves[5:]:
        move.wait()


def pick(values, index, bits):
    packed = 0
    for i, value in enumerate(values):
        packed |= value << (bits * i)
    return lax.shift_right_logical(jnp.int32(packed), index * bits) & (2**bits - 1)


def window_kernel(
    home_ref, edge_ref, corner_ref, y_ref, fac_ref, lat_ref, dia_ref, dep_ref, mat_ref, pay_ref,
    out_ref, part_ref, own_ref, z_ref, link_ref, left_ref, product_ref,
):
    row = lax.axis_index("row")
    col = lax.axis_index("col")
    col_count = lax.axis_size("col")
    device = row * col_count + col

    def scan(t, found):
        here = home_ref[0, t]
        return tuple(jnp.where(here == device * PLACES + p, t, found[p]) for p in range(PLACES))

    tile_count = home_ref.shape[1]
    unroll = 8 if tile_count % 8 == 0 else 1

    def scan_some(i, found):
        for s in range(unroll):
            found = scan(i * unroll + s, found)
        return found

    tiles = lax.fori_loop(0, tile_count // unroll, scan_some, tuple(jnp.int32(-1) for _ in range(PLACES)))

    def block_of(tile):
        place = home_ref[0, tile]
        other = lax.shift_right_logical(place, 1)
        slot = (other ^ device) & (2 * col_count - 1)
        return slot * BLOCK_COUNT, place & 1

    def edge_of(tile, edge):
        code = edge_ref[edge, tile]
        return lax.shift_right_logical(code, 3), lax.shift_right_logical(code, 1) & 3, code & 1

    def strip_end(tile, edge_end):
        other, f, r = edge_of(tile, lax.shift_right_logical(edge_end, 1))
        base, place = block_of(other)
        return base + CORNER_BLOCK, 80 + place * 24 + f * 2 + ((edge_end & 1) ^ r)

    def point(tile, corner):
        code = corner_ref[corner, tile]
        safe = jnp.maximum(code, 0)
        other, g = lax.shift_right_logical(safe, 2), safe & 3
        base, place = block_of(other)
        return base + CORNER_BLOCK, jnp.where(code >= 0, place * 16 + g, -1), other, g

    for p in range(PLACES):
        at = p * TABLE
        tile = jnp.maximum(tiles[p], 0)
        out_ref[at + OCCUPIED_AT] = jnp.where(tiles[p] >= 0, 1, 0)
        for e in range(4):
            other, f, r = edge_of(tile, e)
            base, place = block_of(other)
            out_ref[at + LINE_AT + 3 * e] = base + place * 3
            out_ref[at + LINE_AT + 3 * e + 1] = 32 * (f ^ lax.shift_right_logical(f, 1)) + 31 * r
            out_ref[at + LINE_AT + 3 * e + 2] = 1 - 2 * r
            for end in range(2):
                index = f * 2 + (end ^ r)
                strip_row, strip_lane = strip_end(other, pick(OTHER_EDGE, index, 2) * 2 + pick(OTHER_END, index, 1))
                point_row, point_lane, _, _ = point(other, pick(CORNER_OF, index, 2))
                slot = at + END_AT + 4 * (2 * e + end)
                out_ref[slot] = strip_row
                out_ref[slot + 1] = strip_lane
                out_ref[slot + 2] = point_row
                out_ref[slot + 3] = point_lane
        for c in range(4):
            point_row, point_lane, other, g = point(tile, c)
            slot = at + POINT_AT + 6 * c
            out_ref[slot] = point_row
            out_ref[slot + 1] = point_lane
            row_a, lane_a = strip_end(other, pick(CORNER_A, g, 3))
            row_b, lane_b = strip_end(other, pick(CORNER_B, g, 3))
            out_ref[slot + 2] = row_a
            out_ref[slot + 3] = lane_a
            out_ref[slot + 4] = row_b
            out_ref[slot + 5] = lane_b

    lane = lane_iota()
    level = lax.broadcasted_iota(jnp.int32, (LEVELS, LANES), 0)
    for p in range(PLACES):
        fields = [p * TRACERS + t for t in range(TRACERS)]
        inverse = [fac_ref[p, 0, k] for k in range(LEVELS)]
        ratio = [fac_ref[p, 1, k] for k in range(LEVELS)]
        couple = [fac_ref[p, 2, k] for k in range(LEVELS)]
        found = column_solve(
            [[y_ref[f, level_rows(k), :] for k in range(LEVELS)] for f in fields], inverse, ratio, couple
        )
        for k in range(LEVELS):
            for f, values in zip(fields, found):
                z_ref[f, level_rows(k), :] = values[k]
    spread_products(z_ref, lat_ref, dia_ref, mat_ref, left_ref, product_ref)
    for f in range(FIELDS):
        own, beyond = (product_blocks(product_ref, f, i) for i in range(2))
        inner = from_neighbours(own, beyond, lane < 32, lane >= 96)
        for j in range(BLOCKS):
            part_ref[f, tile_rows(j), :] = jnp.where(tiles[f // TRACERS] >= 0, inner[j], 0.0)

    wet = []
    for p in range(PLACES):
        rows = [dep_ref[j * PLACES + p : j * PLACES + p + 1, :] for j in range(BLOCKS)]
        masks = [jnp.where(row > level, 1.0, 0.0) for row in rows]
        wet.append(pack_lines(masks, lane))
    for f in range(LEVELS):
        link_ref[0, tile_rows(f), :] = pay_ref[12 + f // TRACERS % PLACES * 3]
        link_ref[1, tile_rows(f), :] = wet[f // TRACERS % PLACES]
    couple = [link_ref[0, level_rows(k), :] for k in range(LEVELS)]
    ((inverse, ratio),) = column_factors([couple], [None])
    for k in range(LEVELS):
        mask = link_ref[1, level_rows(k), :]
        own_ref[0, k] = inverse[k] * mask
        own_ref[1, k] = ratio[k]
        own_ref[2, k] = couple[k]


def second_kernel(tab_ref, part_ref, own_ref, *refs):
    pay_refs = refs[:-5]
    out_ref, all_ref, own_line_ref, line_ref, link_ref = refs[-5:]
    lane = lane_iota()
    zero = jnp.zeros((LEVELS, LANES), jnp.float32)
    for slot, ref in enumerate(pay_refs):
        for i in range(BLOCK_COUNT):
            all_ref[slot * BLOCK_COUNT + i] = ref[i]
    segment, position = lane // 32, lane % 32
    edge = segment ^ (segment // 2)
    line_end = (position == 0) | (position == 31)

    strips, lines, line_lat, line_dia = [], [], [], []
    for p in range(PLACES):
        at = p * TABLE + LINE_AT
        rows = [tab_ref[at + 3 * e] for e in range(4)]
        places = [tab_ref[at + 3 * e + 1] for e in range(4)]
        signs = [tab_ref[at + 3 * e + 2] for e in range(4)]
        index = zero.astype(jnp.int32)
        for e in range(4):
            index = jnp.where(edge == e, places[e] + signs[e] * position, index)

        def fetch(block):
            found = take(all_ref[rows[0] + block], index)
            for e in range(1, 4):
                found = jnp.where(edge == e, take(all_ref[rows[e] + block], index), found)
            return found

        for t in range(TRACERS):
            strips.append(fetch(t))
            lines.append(fetch(FIELDS + t))
        link = fetch(12)
        for t in range(TRACERS):
            link_ref[tile_rows(p * TRACERS + t), :] = link
        line_lat.append(fetch(13))
        line_dia.append(fetch(14))

    ends = zero
    tracer = lane % 32 // 8
    for p in range(PLACES):
        for i in range(8):
            at = p * TABLE + END_AT + 4 * i
            here = (segment == p) & (lane % 8 == i)
            strip = take(all_ref[tab_ref[at]], jnp.minimum(tab_ref[at + 1] + tracer * 8, LANES - 1))
            point_lane = tab_ref[at + 3]
            point = take(all_ref[tab_ref[at + 2]], jnp.maximum(point_lane, 0) + tracer * 4)
            ends = jnp.where(here, strip + jnp.where(point_lane >= 0, point, 0.0), ends)

    cells = zero
    cell_adds = zero
    cell_tracer = lane % 16 // 4
    for p in range(PLACES):
        for c in range(4):
            at = p * TABLE + POINT_AT + 6 * c
            here = (position // 16 == p) & (lane % 4 == c)
            point_lane = tab_ref[at + 1]
            safe = jnp.maximum(point_lane, 0)
            cell_lane = jnp.where(
                segment < 2,
                safe + 32 * segment + 4 * cell_tracer,
                48 + 8 * segment + 4 * lax.shift_right_logical(safe, 4) + (safe & 3),
            )
            cell = take(all_ref[tab_ref[at]], cell_lane)
            cells = jnp.where(here & (point_lane >= 0), cell, cells)
            strip_a = take(all_ref[tab_ref[at + 2]], jnp.minimum(tab_ref[at + 3] + cell_tracer * 8, LANES - 1))
            strip_b = take(all_ref[tab_ref[at + 4]], jnp.minimum(tab_ref[at + 5] + cell_tracer * 8, LANES - 1))
            cell_adds = jnp.where(here, strip_a + strip_b, cell_adds)
    cell_adds = cell_adds + pltpu.roll(all_ref[CORNER_BLOCK], 32, 1)

    corner_of_lane = jnp.where(segment == 0, jnp.where(position == 31, 1, 0), jnp.where(position == 31, 2, 3))
    at_corner = line_end & ((segment == 0) | (segment == 3))
    for f in range(FIELDS):
        p, t = f // TRACERS, f % TRACERS
        spread = take(ends, p * 32 + t * 8 + edge * 2 + jnp.where(position == 31, 1, 0))
        line_ref[tile_rows(f), :] = lines[f] + all_ref[f] + jnp.where(line_end, spread, 0.0)
        points = take(cells, p * 16 + t * 4 + corner_of_lane)
        own_line_ref[tile_rows(f), :] = strips[f] + jnp.where(at_corner, points, 0.0)
    line_ref[tile_rows(FIELDS), :] = cells + cell_adds
    line_ref[tile_rows(FIELDS + 1), :] = zero
    own_line_ref[tile_rows(FIELDS), :] = zero
    own_line_ref[tile_rows(FIELDS + 1), :] = zero
    link_ref[tile_rows(FIELDS), :] = pltpu.roll(cells, LANES - 32, 1)
    link_ref[tile_rows(FIELDS + 1), :] = zero
    couple = [link_ref[level_rows(k), :] for k in range(LEVELS - 1)] + [zero]
    ((inverse, ratio),) = column_factors([couple], [None])
    (own_found,) = column_solve(
        [[own_line_ref[level_rows(k), :] for k in range(LEVELS)]],
        [own_ref[0, k] for k in range(LEVELS)],
        [own_ref[1, k] for k in range(LEVELS)],
        [own_ref[2, k] for k in range(LEVELS)],
    )
    (found,) = column_solve([[line_ref[level_rows(k), :] for k in range(LEVELS)]], inverse, ratio, couple)
    for k in range(LEVELS):
        own_line_ref[level_rows(k), :] = own_found[k]
        line_ref[level_rows(k), :] = found[k]
    points = line_ref[tile_rows(FIELDS), :] * pltpu.roll(cells, LANES - 64, 1)

    for p in range(PLACES):
        occupied = tab_ref[p * TABLE + OCCUPIED_AT] > 0
        own_lat, own_dia = all_ref[13 + 3 * p], all_ref[14 + 3 * p]
        for t in range(TRACERS):
            f = p * TRACERS + t
            line = line_ref[tile_rows(f), :]
            outer = line_lat[p] * line + beside(line_dia[p] * line, lane)
            outer = outer + jnp.where(at_corner, take(points, 32 + p * 16 + t * 4 + corner_of_lane), 0.0)
            line = own_line_ref[tile_rows(f), :]
            along, across = own_lat * line, own_dia * line
            outer = outer + line - 4.0 * (along + across) + beside(along, lane)
            inner = along + beside(across, lane)
            adds = unpack_lines(jnp.where(occupied, outer, 0.0), jnp.where(occupied, inner, 0.0), lane)
            for j in range(BLOCKS):
                out_ref[f, tile_rows(j), :] = part_ref[f, tile_rows(j), :] + adds[j]


def swap(value, axes, row_count, col_count, row_bit, col_bits):
    pairs = []
    for i in range(row_count):
        for j in range(col_count):
            pairs.append((i * col_count + j, (i ^ row_bit) * col_count + (j ^ col_bits)))
    return lax.ppermute(value, axes, pairs)


def tiled(array, lead):
    blocks = array.reshape(lead + (-1, BLOCKS, LANES))
    rows = blocks.shape[-3]
    order = tuple(range(len(lead))) + (len(lead) + 1, len(lead), len(lead) + 2)
    return blocks.transpose(order).reshape(lead + (BLOCKS * rows, LANES))


def on_device(adjoint_out, lateral, diagonal, vertical, depth, tile_home, edge_link, corner_link):
    row_count, col_count = lax.axis_size("row"), lax.axis_size("col")
    axes = ("row", "col")
    vmem = pl.BlockSpec(memory_space=pltpu.VMEM)
    smem = pl.BlockSpec(memory_space=pltpu.SMEM)
    params = pltpu.CompilerParams(vmem_limit_bytes=VMEM_LIMIT)
    rows = BLOCKS * LEVELS
    x = tiled(adjoint_out, (FIELDS,))
    lat = tiled(lateral, (PLACES,))
    dia = tiled(diagonal, (PLACES,))
    ver = tiled(vertical, (PLACES,))
    dep = tiled(depth, ())
    hbm = pl.BlockSpec(memory_space=pltpu.HBM)
    home, edges, corners = tile_home.reshape(1, -1), edge_link.T, corner_link.T
    sources = (dep, ver, x, lat, dia, home, edges, corners)
    payload, y, fac, dep, lat, dia, matrix, home, edges, corners = pl.pallas_call(
        first_kernel,
        out_shape=(
            f32((BLOCK_COUNT, LEVELS, LANES)),
            f32((FIELDS, rows, LANES)),
            f32((PLACES, 3, LEVELS, BLOCKS, LANES)),
        )
        + tuple(jax.ShapeDtypeStruct(value.shape, value.dtype) for value in (dep, lat, dia))
        + (jax.ShapeDtypeStruct((3 * LANES, 2 * LANES), jnp.bfloat16),)
        + tuple(pltpu.SMEM(value.shape, value.dtype) for value in (home, edges, corners)),
        in_specs=[hbm] * len(sources),
        out_specs=(vmem,) * 7 + (smem,) * 3,
        scratch_shapes=[
            pltpu.VMEM((PLACES, rows, LANES), jnp.float32),
            pltpu.VMEM((FIELDS, rows, LANES), jnp.float32),
            pltpu.VMEM((FIELDS, rows, LANES), jnp.float32),
            pltpu.VMEM((FIELDS * rows, 6 * LANES), jnp.bfloat16),
            pltpu.VMEM((FIELDS * rows, 2 * LANES), jnp.float32),
            pltpu.SemaphoreType.DMA((len(sources),)),
        ],
        compiler_params=params,
        name="first",
    )(*(pltpu.with_memory_space_constraint(value, pltpu.HBM) for value in sources))
    near = [swap(payload, axes, row_count, col_count, 0, m) for m in range(1, col_count)]
    table, part, own = pl.pallas_call(
        window_kernel,
        out_shape=(
            pltpu.SMEM((PLACES * TABLE,), jnp.int32),
            f32((FIELDS, rows, LANES)),
            f32((3, LEVELS, LEVELS, LANES)),
        ),
        in_specs=[smem] * 3 + [vmem] * 7,
        out_specs=(smem, vmem, vmem),
        scratch_shapes=[
            pltpu.VMEM((FIELDS, rows, LANES), jnp.float32),
            pltpu.VMEM((2, rows, LANES), jnp.float32),
            pltpu.VMEM((FIELDS * rows, 6 * LANES), jnp.bfloat16),
            pltpu.VMEM((FIELDS * rows, 2 * LANES), jnp.float32),
        ],
        compiler_params=params,
        name="window",
    )(home, edges, corners, y, fac, lat, dia, dep, matrix, payload)
    near = [lax.optimization_barrier((value, table))[0] for value in near]
    twin = swap(lax.optimization_barrier((payload, table))[0], axes, row_count, col_count, 1, 0)
    far = [swap(value, axes, row_count, col_count, 1, 0) for value in near]
    payloads = [payload] + near + [twin] + far
    out = pl.pallas_call(
        second_kernel,
        out_shape=f32((FIELDS, rows, LANES)),
        in_specs=[smem] + [vmem] * (2 + len(payloads)),
        out_specs=vmem,
        scratch_shapes=[
            pltpu.VMEM((len(payloads) * BLOCK_COUNT, LEVELS, LANES), jnp.float32),
            pltpu.VMEM((rows, LANES), jnp.float32),
            pltpu.VMEM((rows, LANES), jnp.float32),
            pltpu.VMEM((rows, LANES), jnp.float32),
        ],
        compiler_params=pltpu.CompilerParams(vmem_limit_bytes=VMEM_LIMIT + 2 * len(payloads) * BLOCK_COUNT * 4096),
        name="second",
    )(table, part, own, *payloads)
    out = out.reshape(FIELDS, BLOCKS, LEVELS, LANES).transpose(0, 2, 1, 3)
    return out.reshape(adjoint_out.shape)


def solution(mesh):
    return jax.shard_map(
        on_device,
        mesh=mesh,
        in_specs=(
            P("row", "col", None, None, None, None),
            P("row", "col", None, None, None),
            P("row", "col", None, None, None),
            P("row", "col", None, None, None),
            P("row", "col", None, None),
            P(),
            P(),
            P(),
        ),
        out_specs=P("row", "col", None, None, None, None),
        check_vma=False,
    )
```

```python
import jax
import jax.numpy as jnp
from jax import lax
from jax.experimental import pallas as pl
from jax.experimental.pallas import tpu as pltpu
from jax.sharding import PartitionSpec as P

LEVELS = 8
PLACES = 2
TRACERS = 3
FIELDS = PLACES * TRACERS
BLOCKS = 8
LANES = 128
BLOCK_COUNT = 19
CORNER_BLOCK = 18
VMEM_LIMIT = 8 * 2**20
GROUP = 3

CORNER_OF = (0, 1, 1, 2, 3, 2, 0, 3)
OTHER_EDGE = (3, 1, 0, 2, 3, 1, 0, 2)
OTHER_END = (0, 0, 1, 1, 1, 1, 0, 0)
CORNER_A = (0, 1, 3, 4)
CORNER_B = (6, 2, 5, 7)

LINE_AT = 0
END_AT = 12
POINT_AT = 44
OCCUPIED_AT = 68
TABLE = 72


def f32(shape):
    return jax.ShapeDtypeStruct(shape, jnp.float32)


def lane_iota():
    return lax.broadcasted_iota(jnp.int32, (LEVELS, LANES), 1)


def take(block, index):
    return jnp.take_along_axis(block, index, axis=1, mode="promise_in_bounds")


def level_rows(k):
    return pl.ds(k, BLOCKS, stride=LEVELS)


def tile_rows(j):
    return pl.ds(j * LEVELS, LEVELS)


def column_solve(rhs, inverse, ratio, couple):
    partial = [[] for _ in rhs]
    for k in range(LEVELS):
        for values, done in zip(rhs, partial):
            current = values[k]
            if k > 0:
                current = current + couple[k - 1] * done[-1]
            done.append(current * inverse[k])
    found = [[done[-1]] for done in partial]
    for k in range(LEVELS - 2, -1, -1):
        for done, values in zip(partial, found):
            values.insert(0, done[k] + ratio[k] * values[0])
    return found


def column_factors(couples, depths):
    factors = [([], []) for _ in couples]
    for k in range(LEVELS):
        for couple, depth, (inverse, ratio) in zip(couples, depths, factors):
            pivot = 1.0 + couple[k]
            if k > 0:
                pivot = pivot + couple[k - 1] - couple[k - 1] * ratio[-1]
            inv = 1.0 / pivot
            if depth is not None:
                inv = jnp.where(depth > k, inv, 0.0)
            inverse.append(inv)
            ratio.append(couple[k] * inv)
    return factors


def beside(block, lane):
    b = lane % 32
    return jnp.where(b > 0, pltpu.roll(block, 1, 1), 0.0) + jnp.where(b < 31, pltpu.roll(block, LANES - 1, 1), 0.0)


def spread_matrix(mat_ref):
    shape = (LANES, LANES)
    source = lax.broadcasted_iota(jnp.int32, shape, 0)
    target = lax.broadcasted_iota(jnp.int32, shape, 1)
    line = (target < 32) | (target >= 96)
    kind, side = target // 8 % 2, target // 4 % 2
    row = jnp.where(target < 32, 4, jnp.where(target >= 96, -1, 4 * (target // 16) - 12 + target % 4))
    column = jnp.where(line, target % 32, jnp.where(side == 0, 32 - kind, kind - 1))
    for half, (to_row, to_column) in enumerate(((target // 32, target % 32), (row, column))):
        rows = jnp.abs(source // 32 - to_row)
        columns = jnp.abs(source % 32 - to_column)
        same = rows + columns == 0
        across = (rows == 1) & (columns == 1)
        weights = (
            jnp.where(same, 1.0, 0.0),
            jnp.where(same, -4.0, jnp.where(rows + columns == 1, 1.0, 0.0)),
            jnp.where(same, -4.0, jnp.where(across, 1.0, 0.0)),
        )
        for i, weight in enumerate(weights):
            mat_ref[i * LANES : (i + 1) * LANES, half * LANES : (half + 1) * LANES] = weight.astype(jnp.bfloat16)


def split(values):
    high = values.astype(jnp.bfloat16)
    return high, (values - high.astype(jnp.float32)).astype(jnp.bfloat16)


def spread_products(z_ref, lat_ref, dia_ref, mat_ref, left_ref, product_ref):
    rows = BLOCKS * LEVELS
    right = jnp.concatenate([mat_ref[...], mat_ref[...]], axis=0)
    for start in range(0, FIELDS, GROUP):
        for f in range(start, start + GROUP):
            z = z_ref[f]
            p = f // TRACERS
            for i, values in enumerate((z, lat_ref[p] * z, dia_ref[p] * z)):
                high, low = split(values)
                left_ref[f * rows : (f + 1) * rows, i * LANES : (i + 1) * LANES] = high
                left_ref[f * rows : (f + 1) * rows, (3 + i) * LANES : (4 + i) * LANES] = low
        part = slice(start * rows, (start + GROUP) * rows)
        product_ref[part, :] = jnp.dot(left_ref[part, :], right, preferred_element_type=jnp.float32)


def product_blocks(product_ref, f, i):
    rows = BLOCKS * LEVELS
    return [
        product_ref[f * rows + j * LEVELS : f * rows + (j + 1) * LEVELS, i * LANES : (i + 1) * LANES] for j in range(BLOCKS)
    ]


def from_neighbours(blocks, beyond, first_row, last_row):
    sums = []
    for j in range(BLOCKS):
        total = blocks[j]
        if j > 0:
            total = total + jnp.where(first_row, beyond[j - 1], 0.0)
        if j < BLOCKS - 1:
            total = total + jnp.where(last_row, beyond[j + 1], 0.0)
        sums.append(total)
    return sums


def pack_lines(columns, lane):
    residue = lane % 32
    mixed = pltpu.roll(columns[0], 1, 1)
    for j in range(1, BLOCKS):
        mixed = jnp.where(residue // 2 == j, pltpu.roll(columns[j], 2 * j + 1, 1), mixed)
    q, j = residue % 4, residue // 4
    index = jnp.where(lane < 64, 32 * ((q + 1) % 4) + 2 * j, 32 * q + 2 * j + 1)
    return jnp.where(lane < 32, columns[0], jnp.where(lane >= 96, columns[-1], take(mixed, index)))


def pack_products(inner, beyond, lane):
    slot = lane // 16
    mixed = jnp.zeros_like(beyond[0])
    for j in range(BLOCKS):
        moved = pltpu.roll(beyond[j], (16 * j - 48) % LANES, 1) if j != 3 else beyond[j]
        mixed = mixed + jnp.where((slot >= j - 1) & (slot <= j + 1), moved, 0.0)
    index = 16 * (lane % 32 // 4) + lane % 4 + jnp.where(lane >= 64, 4, 0)
    low, high = lane < 32, lane >= 96
    ghosts = take(jnp.where(lane < 64, beyond[-1], beyond[0]), lane ^ 96)
    strips = jnp.where(low | high, ghosts, take(mixed, index))
    lines = jnp.where(low, inner[0], jnp.where(high, inner[-1], take(mixed, index + 8)))
    return strips, lines


def unpack_lines(outer, inner, lane):
    residue = lane % 32
    j, part, q = residue // 4, residue % 4, lane // 32
    index = jnp.where(part < 2, 32 + 4 * j + (q + 3) % 4, 64 + 4 * j + q)
    mixed = jnp.where((part == 0) | (part == 3), take(inner, index), take(outer, index))
    near = (residue < 2) | (residue >= 30)
    adds = [jnp.where(near, pltpu.roll(mixed, (LANES - 4 * j - 2) % LANES, 1), 0.0) for j in range(BLOCKS)]
    segment = lane // 32
    low = jnp.where(segment == 0, outer, jnp.where(segment == 1, pltpu.roll(inner, 32, 1), 0.0))
    high = jnp.where(segment == 3, outer, jnp.where(segment == 2, pltpu.roll(inner, LANES - 32, 1), 0.0))
    adds[0] = adds[0] + low
    adds[-1] = adds[-1] + high
    return adds


def pack_corners(line, lane):
    c = lane % 4
    return take(line, jnp.where(c == 0, 0, jnp.where(c == 1, 31, jnp.where(c == 2, 127, 96))))


def first_kernel(
    *refs,
):
    sources, refs = refs[:8], refs[8:]
    pay_ref, y_ref, fac_ref, dep_ref, lat_ref, dia_ref, mat_ref, home_ref, edge_ref, corner_ref = refs[:10]
    ver_ref, x_ref, z_ref, left_ref, product_ref, sems = refs[10:]
    targets = (dep_ref, ver_ref, x_ref, lat_ref, dia_ref, home_ref, edge_ref, corner_ref)
    moves = [pltpu.make_async_copy(source, target, sems.at[i]) for i, (source, target) in enumerate(zip(sources, targets))]
    for move in moves:
        move.start()
    spread_matrix(mat_ref)
    lane = lane_iota()
    level = lax.broadcasted_iota(jnp.int32, (LEVELS, LANES), 0)
    group = lane // 32
    corners = jnp.zeros((LEVELS, LANES), jnp.float32)
    end_edge = lane % 8 // 2
    end_lane = 32 * (end_edge ^ (end_edge // 2)) + 31 * (lane % 2)
    moves[0].wait()
    moves[1].wait()
    depth = [dep_ref[pl.ds(p, BLOCKS, stride=PLACES), :] for p in range(PLACES)]
    couple = [
        [jnp.where(depth[p] > k + 1, ver_ref[p, level_rows(k), :], 0.0) for k in range(LEVELS - 1)]
        + [jnp.zeros((BLOCKS, LANES), jnp.float32)]
        for p in range(PLACES)
    ]
    factors = column_factors(couple, depth)
    for p in range(PLACES):
        for k in range(LEVELS):
            fac_ref[p, 0, k] = factors[p][0][k]
            fac_ref[p, 1, k] = factors[p][1][k]
            fac_ref[p, 2, k] = couple[p][k]
    moves[2].wait()
    for p in range(PLACES):
        fields = [p * TRACERS + t for t in range(TRACERS)]
        found = column_solve(
            [[x_ref[f, level_rows(k), :] for k in range(LEVELS)] for f in fields], *factors[p], couple[p]
        )
        for k in range(LEVELS):
            for f, values in zip(fields, found):
                z_ref[f, level_rows(k), :] = values[k]
    for move in moves[3:5]:
        move.wait()
    spread_products(z_ref, lat_ref, dia_ref, mat_ref, left_ref, product_ref)
    for p in range(PLACES):
        wet_lat, wet_dia, link = [], [], []
        for j in range(BLOCKS):
            row = dep_ref[j * PLACES + p : j * PLACES + p + 1, :]
            wet_lat.append(jnp.where(row > level, lat_ref[p, tile_rows(j), :], 0.0))
            wet_dia.append(jnp.where(row > level, dia_ref[p, tile_rows(j), :], 0.0))
            link.append(jnp.where((row > level + 1) & (level < LEVELS - 1), ver_ref[p, tile_rows(j), :], 0.0))
        coefs = [pack_lines(blocks, lane) for blocks in (link, wet_lat, wet_dia)]
        for i in range(3):
            pay_ref[12 + p * 3 + i] = coefs[i]
        link_corners = pack_corners(coefs[0], lane)
        dia_corners = pack_corners(coefs[2], lane)
        for t in range(TRACERS):
            f = p * TRACERS + t
            own, beyond = (product_blocks(product_ref, f, i) for i in range(2))
            inner = from_neighbours(own, beyond, lane < 32, lane >= 96)
            for j in range(BLOCKS):
                y_ref[f, tile_rows(j), :] = inner[j]
            strips, lines = pack_products(inner, beyond, lane)
            pay_ref[f] = strips
            pay_ref[FIELDS + f] = lines
            across = jnp.where(
                lane < 64,
                dia_ref[p, tile_rows(0), :] * z_ref[f, tile_rows(0), :],
                dia_ref[p, tile_rows(BLOCKS - 1), :] * z_ref[f, tile_rows(BLOCKS - 1), :],
            )
            cells = jnp.where(group == 0, pack_corners(across, lane), pack_corners(lines, lane))
            corners = jnp.where((lane < 64) & (lane % 32 // 4 == p * 4 + t), cells, corners)
            corners = jnp.where(lane // 8 == 10 + p * 3 + t, take(strips, end_lane), corners)
        corners = jnp.where(lane // 4 == 16 + p, link_corners, corners)
        corners = jnp.where(lane // 4 == 18 + p, dia_corners, corners)
    pay_ref[CORNER_BLOCK] = corners
    for move in moves[5:]:
        move.wait()


def pick(values, index, bits):
    packed = 0
    for i, value in enumerate(values):
        packed |= value << (bits * i)
    return lax.shift_right_logical(jnp.int32(packed), index * bits) & (2**bits - 1)


def window_kernel(
    home_ref, edge_ref, corner_ref, y_ref, fac_ref, lat_ref, dia_ref, dep_ref, mat_ref, pay_ref,
    out_ref, part_ref, own_ref, z_ref, link_ref, left_ref, product_ref,
):
    row = lax.axis_index("row")
    col = lax.axis_index("col")
    col_count = lax.axis_size("col")
    device = row * col_count + col

    def scan(t, found):
        here = home_ref[0, t]
        return tuple(jnp.where(here == device * PLACES + p, t, found[p]) for p in range(PLACES))

    tile_count = home_ref.shape[1]
    unroll = 8 if tile_count % 8 == 0 else 1

    def scan_some(i, found):
        for s in range(unroll):
            found = scan(i * unroll + s, found)
        return found

    tiles = lax.fori_loop(0, tile_count // unroll, scan_some, tuple(jnp.int32(-1) for _ in range(PLACES)))

    def block_of(tile):
        place = home_ref[0, tile]
        other = lax.shift_right_logical(place, 1)
        slot = (other ^ device) & (2 * col_count - 1)
        return slot * BLOCK_COUNT, place & 1

    def edge_of(tile, edge):
        code = edge_ref[edge, tile]
        return lax.shift_right_logical(code, 3), lax.shift_right_logical(code, 1) & 3, code & 1

    def strip_end(tile, edge_end):
        other, f, r = edge_of(tile, lax.shift_right_logical(edge_end, 1))
        base, place = block_of(other)
        return base + CORNER_BLOCK, 80 + place * 24 + f * 2 + ((edge_end & 1) ^ r)

    def point(tile, corner):
        code = corner_ref[corner, tile]
        safe = jnp.maximum(code, 0)
        other, g = lax.shift_right_logical(safe, 2), safe & 3
        base, place = block_of(other)
        return base + CORNER_BLOCK, jnp.where(code >= 0, place * 16 + g, -1), other, g

    for p in range(PLACES):
        at = p * TABLE
        tile = jnp.maximum(tiles[p], 0)
        out_ref[at + OCCUPIED_AT] = jnp.where(tiles[p] >= 0, 1, 0)
        for e in range(4):
            other, f, r = edge_of(tile, e)
            base, place = block_of(other)
            out_ref[at + LINE_AT + 3 * e] = base + place * 3
            out_ref[at + LINE_AT + 3 * e + 1] = 32 * (f ^ lax.shift_right_logical(f, 1)) + 31 * r
            out_ref[at + LINE_AT + 3 * e + 2] = 1 - 2 * r
            for end in range(2):
                index = f * 2 + (end ^ r)
                strip_row, strip_lane = strip_end(other, pick(OTHER_EDGE, index, 2) * 2 + pick(OTHER_END, index, 1))
                point_row, point_lane, _, _ = point(other, pick(CORNER_OF, index, 2))
                slot = at + END_AT + 4 * (2 * e + end)
                out_ref[slot] = strip_row
                out_ref[slot + 1] = strip_lane
                out_ref[slot + 2] = point_row
                out_ref[slot + 3] = point_lane
        for c in range(4):
            point_row, point_lane, other, g = point(tile, c)
            slot = at + POINT_AT + 6 * c
            out_ref[slot] = point_row
            out_ref[slot + 1] = point_lane
            row_a, lane_a = strip_end(other, pick(CORNER_A, g, 3))
            row_b, lane_b = strip_end(other, pick(CORNER_B, g, 3))
            out_ref[slot + 2] = row_a
            out_ref[slot + 3] = lane_a
            out_ref[slot + 4] = row_b
            out_ref[slot + 5] = lane_b

    lane = lane_iota()
    level = lax.broadcasted_iota(jnp.int32, (LEVELS, LANES), 0)
    for p in range(PLACES):
        fields = [p * TRACERS + t for t in range(TRACERS)]
        inverse = [fac_ref[p, 0, k] for k in range(LEVELS)]
        ratio = [fac_ref[p, 1, k] for k in range(LEVELS)]
        couple = [fac_ref[p, 2, k] for k in range(LEVELS)]
        found = column_solve(
            [[y_ref[f, level_rows(k), :] for k in range(LEVELS)] for f in fields], inverse, ratio, couple
        )
        for k in range(LEVELS):
            for f, values in zip(fields, found):
                z_ref[f, level_rows(k), :] = values[k]
    spread_products(z_ref, lat_ref, dia_ref, mat_ref, left_ref, product_ref)
    for f in range(FIELDS):
        own, beyond = (product_blocks(product_ref, f, i) for i in range(2))
        inner = from_neighbours(own, beyond, lane < 32, lane >= 96)
        for j in range(BLOCKS):
            part_ref[f, tile_rows(j), :] = jnp.where(tiles[f // TRACERS] >= 0, inner[j], 0.0)

    wet = []
    for p in range(PLACES):
        rows = [dep_ref[j * PLACES + p : j * PLACES + p + 1, :] for j in range(BLOCKS)]
        masks = [jnp.where(row > level, 1.0, 0.0) for row in rows]
        wet.append(pack_lines(masks, lane))
    for f in range(LEVELS):
        link_ref[0, tile_rows(f), :] = pay_ref[12 + f // TRACERS % PLACES * 3]
        link_ref[1, tile_rows(f), :] = wet[f // TRACERS % PLACES]
    couple = [link_ref[0, level_rows(k), :] for k in range(LEVELS)]
    ((inverse, ratio),) = column_factors([couple], [None])
    for k in range(LEVELS):
        mask = link_ref[1, level_rows(k), :]
        own_ref[0, k] = inverse[k] * mask
        own_ref[1, k] = ratio[k]
        own_ref[2, k] = couple[k]


def second_kernel(tab_ref, part_ref, own_ref, *refs):
    pay_refs = refs[:-5]
    out_ref, all_ref, own_line_ref, line_ref, link_ref = refs[-5:]
    lane = lane_iota()
    zero = jnp.zeros((LEVELS, LANES), jnp.float32)
    for slot, ref in enumerate(pay_refs):
        for i in range(BLOCK_COUNT):
            all_ref[slot * BLOCK_COUNT + i] = ref[i]
    segment, position = lane // 32, lane % 32
    edge = segment ^ (segment // 2)
    line_end = (position == 0) | (position == 31)

    strips, lines, line_lat, line_dia = [], [], [], []
    for p in range(PLACES):
        at = p * TABLE + LINE_AT
        rows = [tab_ref[at + 3 * e] for e in range(4)]
        places = [tab_ref[at + 3 * e + 1] for e in range(4)]
        signs = [tab_ref[at + 3 * e + 2] for e in range(4)]
        index = zero.astype(jnp.int32)
        for e in range(4):
            index = jnp.where(edge == e, places[e] + signs[e] * position, index)

        def fetch(block):
            found = take(all_ref[rows[0] + block], index)
            for e in range(1, 4):
                found = jnp.where(edge == e, take(all_ref[rows[e] + block], index), found)
            return found

        for t in range(TRACERS):
            strips.append(fetch(t))
            lines.append(fetch(FIELDS + t))
        link = fetch(12)
        for t in range(TRACERS):
            link_ref[tile_rows(p * TRACERS + t), :] = link
        line_lat.append(fetch(13))
        line_dia.append(fetch(14))

    ends = zero
    tracer = lane % 32 // 8
    for p in range(PLACES):
        for i in range(8):
            at = p * TABLE + END_AT + 4 * i
            here = (segment == p) & (lane % 8 == i)
            strip = take(all_ref[tab_ref[at]], jnp.minimum(tab_ref[at + 1] + tracer * 8, LANES - 1))
            point_lane = tab_ref[at + 3]
            point = take(all_ref[tab_ref[at + 2]], jnp.maximum(point_lane, 0) + tracer * 4)
            ends = jnp.where(here, strip + jnp.where(point_lane >= 0, point, 0.0), ends)

    cells = zero
    cell_adds = zero
    cell_tracer = lane % 16 // 4
    for p in range(PLACES):
        for c in range(4):
            at = p * TABLE + POINT_AT + 6 * c
            here = (position // 16 == p) & (lane % 4 == c)
            point_lane = tab_ref[at + 1]
            safe = jnp.maximum(point_lane, 0)
            cell_lane = jnp.where(
                segment < 2,
                safe + 32 * segment + 4 * cell_tracer,
                48 + 8 * segment + 4 * lax.shift_right_logical(safe, 4) + (safe & 3),
            )
            cell = take(all_ref[tab_ref[at]], cell_lane)
            cells = jnp.where(here & (point_lane >= 0), cell, cells)
            strip_a = take(all_ref[tab_ref[at + 2]], jnp.minimum(tab_ref[at + 3] + cell_tracer * 8, LANES - 1))
            strip_b = take(all_ref[tab_ref[at + 4]], jnp.minimum(tab_ref[at + 5] + cell_tracer * 8, LANES - 1))
            cell_adds = jnp.where(here, strip_a + strip_b, cell_adds)
    cell_adds = cell_adds + pltpu.roll(all_ref[CORNER_BLOCK], 32, 1)

    corner_of_lane = jnp.where(segment == 0, jnp.where(position == 31, 1, 0), jnp.where(position == 31, 2, 3))
    at_corner = line_end & ((segment == 0) | (segment == 3))
    for f in range(FIELDS):
        p, t = f // TRACERS, f % TRACERS
        spread = take(ends, p * 32 + t * 8 + edge * 2 + jnp.where(position == 31, 1, 0))
        line_ref[tile_rows(f), :] = lines[f] + all_ref[f] + jnp.where(line_end, spread, 0.0)
        points = take(cells, p * 16 + t * 4 + corner_of_lane)
        own_line_ref[tile_rows(f), :] = strips[f] + jnp.where(at_corner, points, 0.0)
    line_ref[tile_rows(FIELDS), :] = cells + cell_adds
    line_ref[tile_rows(FIELDS + 1), :] = zero
    own_line_ref[tile_rows(FIELDS), :] = zero
    own_line_ref[tile_rows(FIELDS + 1), :] = zero
    link_ref[tile_rows(FIELDS), :] = pltpu.roll(cells, LANES - 32, 1)
    link_ref[tile_rows(FIELDS + 1), :] = zero
    couple = [link_ref[level_rows(k), :] for k in range(LEVELS - 1)] + [zero]
    ((inverse, ratio),) = column_factors([couple], [None])
    (own_found,) = column_solve(
        [[own_line_ref[level_rows(k), :] for k in range(LEVELS)]],
        [own_ref[0, k] for k in range(LEVELS)],
        [own_ref[1, k] for k in range(LEVELS)],
        [own_ref[2, k] for k in range(LEVELS)],
    )
    (found,) = column_solve([[line_ref[level_rows(k), :] for k in range(LEVELS)]], inverse, ratio, couple)
    for k in range(LEVELS):
        own_line_ref[level_rows(k), :] = own_found[k]
        line_ref[level_rows(k), :] = found[k]
    points = line_ref[tile_rows(FIELDS), :] * pltpu.roll(cells, LANES - 64, 1)

    for p in range(PLACES):
        occupied = tab_ref[p * TABLE + OCCUPIED_AT] > 0
        own_lat, own_dia = all_ref[13 + 3 * p], all_ref[14 + 3 * p]
        for t in range(TRACERS):
            f = p * TRACERS + t
            line = line_ref[tile_rows(f), :]
            outer = line_lat[p] * line + beside(line_dia[p] * line, lane)
            outer = outer + jnp.where(at_corner, take(points, 32 + p * 16 + t * 4 + corner_of_lane), 0.0)
            line = own_line_ref[tile_rows(f), :]
            along, across = own_lat * line, own_dia * line
            outer = outer + line - 4.0 * (along + across) + beside(along, lane)
            inner = along + beside(across, lane)
            adds = unpack_lines(jnp.where(occupied, outer, 0.0), jnp.where(occupied, inner, 0.0), lane)
            for j in range(BLOCKS):
                out_ref[f, tile_rows(j), :] = part_ref[f, tile_rows(j), :] + adds[j]


def swap(value, axes, row_count, col_count, row_bit, col_bits):
    pairs = []
    for i in range(row_count):
        for j in range(col_count):
            pairs.append((i * col_count + j, (i ^ row_bit) * col_count + (j ^ col_bits)))
    return lax.ppermute(value, axes, pairs)


def tiled(array, lead):
    blocks = array.reshape(lead + (-1, BLOCKS, LANES))
    rows = blocks.shape[-3]
    order = tuple(range(len(lead))) + (len(lead) + 1, len(lead), len(lead) + 2)
    return blocks.transpose(order).reshape(lead + (BLOCKS * rows, LANES))


def on_device(adjoint_out, lateral, diagonal, vertical, depth, tile_home, edge_link, corner_link):
    row_count, col_count = lax.axis_size("row"), lax.axis_size("col")
    axes = ("row", "col")
    vmem = pl.BlockSpec(memory_space=pltpu.VMEM)
    smem = pl.BlockSpec(memory_space=pltpu.SMEM)
    params = pltpu.CompilerParams(vmem_limit_bytes=VMEM_LIMIT)
    rows = BLOCKS * LEVELS
    x = tiled(adjoint_out, (FIELDS,))
    lat = tiled(lateral, (PLACES,))
    dia = tiled(diagonal, (PLACES,))
    ver = tiled(vertical, (PLACES,))
    dep = tiled(depth, ())
    hbm = pl.BlockSpec(memory_space=pltpu.HBM)
    home, edges, corners = tile_home.reshape(1, -1), edge_link.T, corner_link.T
    sources = (dep, ver, x, lat, dia, home, edges, corners)
    payload, y, fac, dep, lat, dia, matrix, home, edges, corners = pl.pallas_call(
        first_kernel,
        out_shape=(
            f32((BLOCK_COUNT, LEVELS, LANES)),
            f32((FIELDS, rows, LANES)),
            f32((PLACES, 3, LEVELS, BLOCKS, LANES)),
        )
        + tuple(jax.ShapeDtypeStruct(value.shape, value.dtype) for value in (dep, lat, dia))
        + (jax.ShapeDtypeStruct((3 * LANES, 2 * LANES), jnp.bfloat16),)
        + tuple(pltpu.SMEM(value.shape, value.dtype) for value in (home, edges, corners)),
        in_specs=[hbm] * len(sources),
        out_specs=(vmem,) * 7 + (smem,) * 3,
        scratch_shapes=[
            pltpu.VMEM((PLACES, rows, LANES), jnp.float32),
            pltpu.VMEM((FIELDS, rows, LANES), jnp.float32),
            pltpu.VMEM((FIELDS, rows, LANES), jnp.float32),
            pltpu.VMEM((FIELDS * rows, 6 * LANES), jnp.bfloat16),
            pltpu.VMEM((FIELDS * rows, 2 * LANES), jnp.float32),
            pltpu.SemaphoreType.DMA((len(sources),)),
        ],
        compiler_params=params,
        name="first",
    )(*(pltpu.with_memory_space_constraint(value, pltpu.HBM) for value in sources))
    near = [swap(payload, axes, row_count, col_count, 0, m) for m in range(1, col_count)]
    table, part, own = pl.pallas_call(
        window_kernel,
        out_shape=(
            pltpu.SMEM((PLACES * TABLE,), jnp.int32),
            f32((FIELDS, rows, LANES)),
            f32((3, LEVELS, LEVELS, LANES)),
        ),
        in_specs=[smem] * 3 + [vmem] * 7,
        out_specs=(smem, vmem, vmem),
        scratch_shapes=[
            pltpu.VMEM((FIELDS, rows, LANES), jnp.float32),
            pltpu.VMEM((2, rows, LANES), jnp.float32),
            pltpu.VMEM((FIELDS * rows, 6 * LANES), jnp.bfloat16),
            pltpu.VMEM((FIELDS * rows, 2 * LANES), jnp.float32),
        ],
        compiler_params=params,
        name="window",
    )(home, edges, corners, y, fac, lat, dia, dep, matrix, payload)
    near = [lax.optimization_barrier((value, table))[0] for value in near]
    twin = swap(payload, axes, row_count, col_count, 1, 0)
    far = [swap(value, axes, row_count, col_count, 1, 0) for value in near]
    payloads = [payload] + near + [twin] + far
    out = pl.pallas_call(
        second_kernel,
        out_shape=f32((FIELDS, rows, LANES)),
        in_specs=[smem] + [vmem] * (2 + len(payloads)),
        out_specs=vmem,
        scratch_shapes=[
            pltpu.VMEM((len(payloads) * BLOCK_COUNT, LEVELS, LANES), jnp.float32),
            pltpu.VMEM((rows, LANES), jnp.float32),
            pltpu.VMEM((rows, LANES), jnp.float32),
            pltpu.VMEM((rows, LANES), jnp.float32),
        ],
        compiler_params=pltpu.CompilerParams(vmem_limit_bytes=VMEM_LIMIT + 2 * len(payloads) * BLOCK_COUNT * 4096),
        name="second",
    )(table, part, own, *payloads)
    out = out.reshape(FIELDS, BLOCKS, LEVELS, LANES).transpose(0, 2, 1, 3)
    return out.reshape(adjoint_out.shape)


def solution(mesh):
    return jax.shard_map(
        on_device,
        mesh=mesh,
        in_specs=(
            P("row", "col", None, None, None, None),
            P("row", "col", None, None, None),
            P("row", "col", None, None, None),
            P("row", "col", None, None, None),
            P("row", "col", None, None),
            P(),
            P(),
            P(),
        ),
        out_specs=P("row", "col", None, None, None, None),
        check_vma=False,
    )
```
